512 devices in a mesh: dp: 16 (over y, x), expert: 32 (over z, core).
Axes of the slice: x: 4, y: 4, z: 16, core: 2. Of those that a mesh axis runs over, the one named last changes fastest.
Arguments:
- tokens: bfloat16 [2048, 5120], P(('dp', 'expert')), may hold values from -6 to 6
- chosen_expert_index: int32 [2048, 6], P(('dp', 'expert')), may hold values from 0 to 31, all different within a row; in each aligned block of 4 rows (0 to 3, 4 to 7, ...) at most 2 rows name the same one
- router_gate_weight: float32 [2048, 6], P(('dp', 'expert')), may hold values from 0.05 to 0.5
- partner: int32 [2048], P(('dp', 'expert')), may hold values from 0 to 3, as said below
- gate_up_weight: bfloat16 [32, 2, 1536, 5120], P('expert', None, 'dp'), may hold values from -0.078125 to 0.078125
- adapter_down_weight: bfloat16 [32, 8, 1536], P('expert', None, 'dp'), may hold values from -0.15625 to 0.15625
- adapter_up_weight: bfloat16 [32, 8, 5120], P('expert', None, 'dp'), may hold values from -2 to 2
Outputs:
- down_factor_gradient: float32 [32, 8, 1536], P('expert', None, 'dp')
- up_factor_gradient: float32 [32, 8, 5120], P('expert', None, 'dp')
The draws below stay inside these ranges and needn't reach their ends.
Inputs may be any that keep to these rules, and one draw needn't show every extreme that they name: `chosen_expert_index`: in each aligned block of 4 rows (the tokens of one device) a token names 6 different experts, no expert is named by more than 2 rows, a bound that some block reaches. Tokens are paired within each aligned block of 4 rows: partner holds the index of the other token of the pair within the block, never the token itself, and partner of partner is the token.
All inputs are finite; a program needn't handle non-finite values.
Results may differ from the reference program's by a relative error of at most 0.0039.
Values may be sent and summed in bfloat16 or wider, within the bound.
A program may use at most 64 MiB of HBM per device.

```python
import math
import jax
import jax.numpy as jnp
import numpy as np
from jax import lax

MODEL_WIDTH = 5120
EXPERT_UNITS = 1536
TOP = 6
ADAPTER_RANK = 8
TOK_DEV = 4
ROUTED_EXPERTS = 32
TOKENS = 2048
CAP = 2


def draw_partner(key, part):
    blocks = TOKENS // TOK_DEV
    block_keys = jax.random.split(key, blocks)

    def one_block(block_key):
        order = jax.random.permutation(block_key, TOK_DEV).astype(jnp.int32)
        first = order[0::2]
        second = order[1::2]
        mates = jnp.zeros((TOK_DEV,), jnp.int32)
        mates = mates.at[first].set(second)
        return mates.at[second].set(first)
    return jax.vmap(one_block)(block_keys).reshape(TOKENS)


def level_of(key, shape, pieces, low, top_value):
    factor_of = 1.0
    for axis_at, parts in pieces:
        draws = jax.random.uniform(jax.random.fold_in(jax.random.fold_in(key, 6), axis_at), (parts,), jnp.float32, low / len(pieces), top_value / len(pieces))
        factor_of = factor_of * jnp.repeat(jnp.exp(draws), shape[axis_at] // parts).reshape((-1,) + (1,) * (len(shape) - 1 - axis_at))
    return factor_of


def assign_block(rng, own, number, rows, amount, top, bound, skew):
    ranking = jax.random.permutation(rng, amount)
    packed, common = shares(amount, rows * top, bound, skew, True), shares(amount, rows * top, bound, skew, False)
    places = jnp.arange(amount)

    def named(lengths, turn):
        used = int((lengths > 0).sum())
        fixed = max(1, used // 4)
        shifted = fixed + (places - fixed + turn * (used - fixed)) % max(1, amount - fixed)
        return jnp.zeros((amount,), jnp.int32).at[ranking[jnp.where(places < fixed, places, shifted)]].set(jnp.asarray(lengths, jnp.int32))

    lengths = jnp.where(number % 4 == 0, named(packed, number // 4), named(common, number - number // 4 - 1))
    mixed = jax.random.permutation(jax.random.fold_in(own, 3), amount)
    donor, receiver = mixed[0:amount // 2 * 2:2], mixed[1:amount // 2 * 2:2]
    slack = jnp.minimum(lengths[donor] - 1, bound - lengths[receiver]) // 2
    slack = jnp.where((donor == ranking[0]) | (receiver == ranking[0]) | (lengths[receiver] == 0), 0, jnp.maximum(slack, 0))
    shifted = jax.random.randint(jax.random.fold_in(own, 4), (amount // 2,), 0, 1 << 20) % (slack + 1)
    lengths = lengths.at[donor].add(-shifted).at[receiver].add(shifted)
    items = jnp.searchsorted(jnp.cumsum(lengths), jnp.arange(rows * top), side="right").astype(jnp.int32)
    grid = items.reshape(top, rows).T
    grid = grid[jax.random.permutation(jax.random.fold_in(own, 1), rows)]
    turn = jax.random.randint(jax.random.fold_in(own, 2), (rows, 1), 0, top)
    return jnp.take_along_axis(grid, (jnp.arange(top)[None, :] + turn) % top, axis=1)


def shares(number_of, total, limit, lean, full):
    loads = [(1 << 20) // math.isqrt(rank ** lean) + 1 for rank in range(1, number_of + 1)]
    largest = limit if full else min(limit, max(-(-total // number_of), total * loads[0] // sum(loads)))
    least = 1 if total - largest >= number_of - 1 else 0
    counts, spare = [largest] + [least] * (number_of - 1), total - largest - least * (number_of - 1)
    while spare > 0:
        free = [i for i in range(1, number_of) if counts[i] < largest] or [i for i in range(1, number_of) if counts[i] < limit]
        whole, left = sum([loads[i] for i in free]), spare
        for i in free:
            addition = min(limit - counts[i], max(1, left * loads[i] // whole), spare)
            counts[i] = counts[i] + addition
            spare = spare - addition
    return np.array(counts)


def bell_draw(own_key, extent, spread, bound, pieces=(), kind=jnp.bfloat16):
    drawn = jax.random.normal(own_key, extent, jnp.float32) * spread
    if len(pieces) > 0:
        drawn = level_of(own_key, extent, pieces, -0.22, 0.18) * drawn
    return jnp.clip(drawn, min=-bound, max=bound).astype(kind)


def setup_inputs(seed: int = 0) -> dict:
    arg_keys = jax.random.split(jax.random.key(seed), 8)
    tokens = bell_draw(arg_keys[0], (TOKENS, MODEL_WIDTH), 1.0, 6.0, ((0, 512),))
    chosen_expert_index_keys = jax.random.split(jax.random.fold_in(arg_keys[1], 1), TOKENS // TOK_DEV)
    chosen_expert_index_turns = jax.random.permutation(jax.random.fold_in(arg_keys[1], 3), TOKENS // TOK_DEV)
    chosen_expert_index = jax.vmap(lambda own, number: assign_block(jax.random.fold_in(arg_keys[1], 2), own, number, TOK_DEV, ROUTED_EXPERTS, TOP, CAP, 2))(chosen_expert_index_keys, chosen_expert_index_turns).reshape((TOKENS, TOP))
    router_gate_weight = jnp.clip(0.05 + 0.45 * jax.random.uniform(arg_keys[2], (TOKENS, TOP), jnp.float32) ** level_of(arg_keys[2], (TOKENS, TOP), ((0, 512),), -0.2, 0.2), 0.05, 0.5)
    partner = draw_partner(jax.random.fold_in(arg_keys[7], 71), 0)
    gate_up_weight = bell_draw(arg_keys[4], (ROUTED_EXPERTS, 2, EXPERT_UNITS, MODEL_WIDTH), MODEL_WIDTH ** -0.5, 0.078125, ((0, 32), (2, 16)))
    adapter_down_weight = bell_draw(arg_keys[5], (ROUTED_EXPERTS, ADAPTER_RANK, EXPERT_UNITS), EXPERT_UNITS ** -0.5, 0.15625, ((0, 32), (2, 16)))
    adapter_up_weight = bell_draw(arg_keys[6], (ROUTED_EXPERTS, ADAPTER_RANK, MODEL_WIDTH), ADAPTER_RANK ** -0.5, 2.0, ((0, 32), (2, 16)))
    return {"tokens": tokens, "chosen_expert_index": chosen_expert_index, "router_gate_weight": router_gate_weight, "partner": partner, "gate_up_weight": gate_up_weight, "adapter_down_weight": adapter_down_weight, "adapter_up_weight": adapter_up_weight}


adapter_scale = 2.0
control = 0.5
highest_precision = lax.Precision.HIGHEST

def reference(tokens, chosen_expert_index, router_gate_weight, partner, gate_up_weight, adapter_down_weight, adapter_up_weight):
    blocks = TOKENS // TOK_DEV
    x_blocks = tokens.reshape(blocks, TOK_DEV, MODEL_WIDTH)
    x_wide = x_blocks.astype(jnp.float32)
    ids = chosen_expert_index.reshape(blocks, TOK_DEV, TOP)
    weights = router_gate_weight.reshape(blocks, TOK_DEV, TOP)
    picks = (ids[..., None] == jnp.arange(ROUTED_EXPERTS, dtype=jnp.int32)).astype(jnp.int32)
    flat = picks.reshape(blocks, TOK_DEV * TOP, ROUTED_EXPERTS)
    before = jnp.cumsum(flat, axis=1) - flat
    slots = lax.optimization_barrier(jnp.sum(before * flat, axis=2)).reshape(blocks, TOK_DEV, TOP)
    places = (slots[..., None] == jnp.arange(CAP, dtype=jnp.int32)).astype(jnp.float32)

    def tables(expert_number):
        chosen = (ids == expert_number).astype(jnp.float32)
        select = jnp.einsum('btk,btkc->bct', chosen, places, precision=highest_precision)
        weighted = jnp.einsum('btk,btkc,btk->bct', chosen, places, weights, precision=highest_precision)
        return (select, weighted)

    def forward(carry, expert_number):
        select, weighted = tables(expert_number)
        rows = jnp.einsum('bct,btd->bcd', select, x_wide, precision=highest_precision).astype(jnp.bfloat16)
        weight = lax.dynamic_index_in_dim(gate_up_weight, expert_number, 0, keepdims=False).astype(jnp.float32)
        both = jnp.einsum('bcd,gfd->bcgf', rows.astype(jnp.float32), weight, precision=highest_precision)
        hidden_state = (jax.nn.silu(both[:, :, 0]) * both[:, :, 1]).astype(jnp.bfloat16)
        down_factor = lax.dynamic_index_in_dim(adapter_down_weight, expert_number, 0, keepdims=False).astype(jnp.float32)
        up_factor = lax.dynamic_index_in_dim(adapter_up_weight, expert_number, 0, keepdims=False).astype(jnp.float32)
        narrow_product = jnp.einsum('bcf,rf->bcr', hidden_state.astype(jnp.float32), down_factor, precision=highest_precision)
        change_rows = (adapter_scale * jnp.einsum('gxl,lz->gxz', narrow_product, up_factor, precision=highest_precision)).astype(jnp.bfloat16)
        carry = carry + jnp.einsum('bct,bcd->btd', weighted, change_rows.astype(jnp.float32), precision=highest_precision)
        return (carry, (hidden_state, narrow_product))
    expert_range = jnp.arange(ROUTED_EXPERTS, dtype=jnp.int32)
    start = jnp.zeros((blocks, TOK_DEV, MODEL_WIDTH), jnp.float32)
    delta, (hiddens, lows) = lax.scan(forward, start, expert_range)
    mates = jnp.take_along_axis(x_blocks, partner.reshape(blocks, TOK_DEV)[..., None].astype(jnp.int32), axis=1)
    direction = x_wide - mates.astype(jnp.float32)
    cotangent = 2.0 / math.sqrt(TOKENS) * (delta - control * direction)

    def backward(pack):
        expert_number, hidden_state, narrow_product = pack
        select, weighted = tables(expert_number)
        cot_rows = jnp.einsum('bct,btd->bcd', weighted, cotangent, precision=highest_precision).astype(jnp.bfloat16)
        up_factor = lax.dynamic_index_in_dim(adapter_up_weight, expert_number, 0, keepdims=False).astype(jnp.float32)
        cotangent_broad = cot_rows.astype(jnp.float32)
        cotangent_narrow = jnp.einsum('bcd,rd->bcr', cotangent_broad, up_factor, precision=highest_precision)
        up_factor_gradient = adapter_scale * jnp.einsum('wsv,wsg->vg', narrow_product, cotangent_broad, precision=highest_precision)
        down_factor_gradient = adapter_scale * jnp.einsum('mpi,mpq->iq', cotangent_narrow, hidden_state.astype(jnp.float32), precision=highest_precision)
        return (down_factor_gradient, up_factor_gradient)
    down_factor_gradient, up_factor_gradient = lax.map(backward, (expert_range, hiddens, lows))
    return (down_factor_gradient, up_factor_gradient)
```

```python
import functools
import math

import jax
import jax.numpy as jnp
from jax import lax
from jax.experimental import pallas as pl
from jax.experimental.pallas import tpu as pltpu
from jax.sharding import PartitionSpec as P

SCALE = 2.0
CONTROL = 0.5
SIDE = 4
HIGH = lax.Precision.HIGHEST
MESH = pl.DeviceIdType.MESH
F32 = jnp.float32
BF16 = jnp.bfloat16


def dot_t(a, b, **kw):
    return lax.dot_general(a, b, (((1,), (1,)), ((), ())), preferred_element_type=F32, **kw)


def split(v):
    hi = v.astype(BF16)
    lo = (v - hi.astype(F32)).astype(BF16)
    return hi, lo


def gather_kernel(
    zs, x_ref, w_ref, b_ref, hid_ref, xs_ref, low_ref,
    xall, wbuf, accg, accu, lowp, lowr, lowz,
    ssem, rsem, lsem, wssem, wrsem, psend, precv, zsend, zrecv,
):
    d_half = x_ref.shape[1] // 2
    quarter = d_half // 2
    units = w_ref.shape[1]
    dp = lax.axis_index("dp")
    ex = lax.axis_index("expert")
    y, x = dp // SIDE, lax.rem(dp, SIDE)
    z, c = ex // 2, lax.rem(ex, 2)
    other = 2 * z + (1 - c)
    groups = SIDE * SIDE

    barrier = pltpu.get_barrier_semaphore()

    def greet_dp(k, carry):
        pl.semaphore_signal(barrier, inc=1, device_id={"dp": lax.rem(dp + k, groups)}, device_id_type=MESH)
        return carry

    def greet_z(k, carry):
        pl.semaphore_signal(
            barrier, inc=1, device_id={"expert": 2 * lax.rem(z + k, zs) + c}, device_id_type=MESH
        )
        return carry

    pl.semaphore_signal(barrier, inc=1, device_id={"expert": other}, device_id_type=MESH)
    lax.fori_loop(1, groups, greet_dp, 0)
    lax.fori_loop(1, zs, greet_z, 0)
    pl.semaphore_wait(barrier, groups + zs - 1)

    def far(h, first, step):
        along_x = (h == 0) == first
        yy = y if along_x else lax.rem(y + step + SIDE, SIDE)
        xx = lax.rem(x + step + SIDE, SIDE) if along_x else x
        return {"dp": yy * SIDE + xx}

    def place(h, da, db):
        dx, dy = (da, db) if h == 0 else (db, da)
        return lax.rem(y + dy + SIDE, SIDE), lax.rem(x + dx + SIDE, SIDE)

    def cols(h, part):
        lo = h * d_half
        if part is None:
            return pl.ds(lo, d_half)
        return pl.ds(lo + part * quarter, quarter)

    started = []

    def send(h, da, db, part, first, step, number):
        by, bx = place(h, da, db)
        block = xall.at[by, bx, :, cols(h, part)]
        source = x_ref.at[:, cols(h, part)] if da == 0 and db == 0 else block
        copy = pltpu.make_async_remote_copy(
            src_ref=source, dst_ref=block, send_sem=ssem.at[number], recv_sem=rsem.at[number],
            device_id=far(h, first, step), device_id_type=MESH,
        )
        copy.start()
        started.append(copy)

    def arrived(h, da, db, part, number):
        by, bx = place(h, da, db)
        block = xall.at[by, bx, :, cols(h, part)]
        pltpu.make_async_remote_copy(
            src_ref=block, dst_ref=block, send_sem=ssem.at[number], recv_sem=rsem.at[number],
            device_id=far(h, True, 1), device_id_type=MESH,
        ).wait_recv()

    offsets = (0, -1, 1, 2)

    def number(h, phase, j, kind):
        return h * 20 + (kind if phase == 0 else 4 + 4 * j + kind)

    own = pltpu.make_async_copy(x_ref, xall.at[y, x], lsem.at[0])
    own.start()
    for h in range(2):
        send(h, 0, 0, None, True, 1, number(h, 0, 0, 0))
        send(h, 0, 0, None, True, -1, number(h, 0, 0, 1))
    weights = []
    for g in range(2):
        mine = pltpu.make_async_copy(w_ref.at[g], wbuf.at[g, pl.ds(0, units)], lsem.at[1 + g])
        mine.start()
        theirs = pltpu.make_async_remote_copy(
            src_ref=w_ref.at[g], dst_ref=wbuf.at[g, pl.ds(units, units)],
            send_sem=wssem.at[g], recv_sem=wrsem.at[g],
            device_id={"expert": other}, device_id_type=MESH,
        )
        theirs.start()
        weights += [mine, theirs]
    for h in range(2):
        send(h, 0, 0, None, False, 1, number(h, 1, 0, 0))
        send(h, 0, 0, None, False, -1, number(h, 1, 0, 1))
    accg[...] = jnp.zeros_like(accg)
    accu[...] = jnp.zeros_like(accu)
    for h in range(2):
        arrived(h, -1, 0, None, number(h, 0, 0, 0))
        send(h, -1, 0, 0, True, 1, number(h, 0, 0, 2))
        arrived(h, 1, 0, None, number(h, 0, 0, 1))
        send(h, 1, 0, 1, True, -1, number(h, 0, 0, 3))
        for j in (1, 2):
            send(h, offsets[j], 0, None, False, 1, number(h, 1, j, 0))
            send(h, offsets[j], 0, None, False, -1, number(h, 1, j, 1))
    for h in range(2):
        arrived(h, 2, 0, 0, number(h, 0, 0, 2))
        arrived(h, 2, 0, 1, number(h, 0, 0, 3))
        send(h, 2, 0, None, False, 1, number(h, 1, 3, 0))
        send(h, 2, 0, None, False, -1, number(h, 1, 3, 1))

    own.wait()
    for copy in weights:
        copy.wait()
    chunk = 512 if d_half % 512 == 0 else d_half
    rows = SIDE * x_ref.shape[0]

    def multiply(h, db):
        by, bx = place(h, 0, db)

        def step(i, carry):
            at = pl.ds(pl.multiple_of(h * d_half + i * chunk, 128), chunk)
            if h == 0:
                block = xall[by, :, :, at]
            else:
                block = xall[:, bx, :, at]
            block = block.reshape(rows, chunk)
            for g, acc in ((0, accg), (1, accu)):
                part = dot_t(block, wbuf[g, :, at]).reshape(SIDE, rows // SIDE, 2 * units)
                if h == 0:
                    acc[by] = acc[by] + part
                else:
                    acc[:, bx] = acc[:, bx] + part
            return carry

        lax.fori_loop(0, d_half // chunk, step, 0)

    for j in range(4):
        for h in range(2):
            arrived(h, offsets[j], -1, None, number(h, 1, j, 0))
            send(h, offsets[j], -1, 0, False, 1, number(h, 1, j, 2))
            arrived(h, offsets[j], 1, None, number(h, 1, j, 1))
            send(h, offsets[j], 1, 1, False, -1, number(h, 1, j, 3))
        if j == 1:
            for h in range(2):
                multiply(h, 0)
    for h in range(2):
        multiply(h, -1)
        multiply(h, 1)
    for h in range(2):
        for j in range(4):
            arrived(h, offsets[j], 2, 0, number(h, 1, j, 2))
            arrived(h, offsets[j], 2, 1, number(h, 1, j, 3))
        multiply(h, 2)

    pair = xs_ref.shape[-1]
    piece = pltpu.make_async_copy(
        xall.at[:, :, :, pl.ds(pl.multiple_of(pair * (dp // 2), 128), pair)], xs_ref, lsem.at[3]
    )
    piece.start()
    tokens = accg.shape[2]
    both = accg.shape[3]
    gate = accg[...].reshape(groups * tokens, both)
    hidden = (gate * (1.0 / (1.0 + jnp.exp(-gate))) * accu[...].reshape(groups * tokens, both)).astype(BF16)
    hid_ref[...] = hidden
    low = dot_t(b_ref[...], hidden)
    for k in range(groups):
        lowp[k, :, 0:tokens] = low[:, k * tokens : (k + 1) * tokens]

    def low_copy(k):
        peer = lax.rem(dp + k, groups)
        return pltpu.make_async_remote_copy(
            src_ref=lowp.at[peer], dst_ref=lowr.at[k], send_sem=psend.at[k], recv_sem=precv.at[k],
            device_id={"dp": peer}, device_id_type=MESH,
        )

    def start_low(k, carry):
        low_copy(k).start()
        return carry

    def wait_low(k, total):
        low_copy(k).wait()
        return total + lowr[k]

    lax.fori_loop(1, groups, start_low, 0)
    total = lax.fori_loop(1, groups, wait_low, lowp[dp])
    lowz[z] = total

    def z_copy(k):
        return pltpu.make_async_remote_copy(
            src_ref=lowz.at[z], dst_ref=lowz.at[z], send_sem=zsend.at[k], recv_sem=zrecv.at[k],
            device_id={"expert": 2 * lax.rem(z + k, zs) + c}, device_id_type=MESH,
        )

    def z_arrival(k):
        source = lax.rem(z - k + zs, zs)
        return pltpu.make_async_remote_copy(
            src_ref=lowz.at[source], dst_ref=lowz.at[source], send_sem=zsend.at[k], recv_sem=zrecv.at[k],
            device_id={"expert": 2 * source + c}, device_id_type=MESH,
        )

    def start_z(k, carry):
        z_copy(k).start()
        return carry

    def wait_z(k, carry):
        z_arrival(k).wait_recv()
        return carry

    def done_z(k, carry):
        z_copy(k).wait_send()
        return carry

    lax.fori_loop(1, zs, start_z, 0)
    lax.fori_loop(1, zs, wait_z, 0)
    low_ref[...] = lowz[...].reshape(low_ref.shape)
    lax.fori_loop(1, zs, done_z, 0)
    for copy in started:
        copy.wait_send()
    piece.wait()


def finish_kernel(
    zs, total, low_ref, w8_ref, q_ref, g_ref, zt_ref, hid_ref, xs_ref, asl_ref, down_ref, up_ref,
    ct, msgs, arrived, cot, chat, half, taken, psend, precv, csend, crecv,
):
    dp = lax.axis_index("dp")
    ex = lax.axis_index("expert")
    z, c = ex // 2, lax.rem(ex, 2)
    other = 2 * z + (1 - c)
    groups = SIDE * SIDE
    tokens = q_ref.shape[0]
    units = down_ref.shape[1]
    width = up_ref.shape[1]
    wide = zs * 16
    factor = 2.0 / math.sqrt(total)

    barrier = pltpu.get_barrier_semaphore()

    def greet(k, carry):
        pl.semaphore_signal(barrier, inc=1, device_id={"dp": lax.rem(dp + k, groups)}, device_id_type=MESH)
        return carry

    pl.semaphore_signal(barrier, inc=1, device_id={"expert": other}, device_id_type=MESH)
    lax.fori_loop(1, groups, greet, 0)

    values = low_ref[:, 0:tokens] * w8_ref[...]
    ct[...] = values
    here = pl.ds(pl.multiple_of(16 * z, 16), 16)
    mine = ct[here, :]
    weight = w8_ref[here, :]
    inner = jnp.dot(g_ref[...], values, precision=HIGH, preferred_element_type=F32)
    msgs[:, 0:tokens] = weight * (factor * (SCALE * inner - CONTROL * zt_ref[...]))
    msgs[:, tokens : 2 * tokens] = jnp.dot(mine, q_ref[...], precision=HIGH, preferred_element_type=F32)
    msgs[:, 2 * tokens : 2 * tokens + wide] = dot_t(mine, values, precision=HIGH)
    arrived[0] = msgs[...]

    pl.semaphore_wait(barrier, groups)

    def copy_of(k):
        return pltpu.make_async_remote_copy(
            src_ref=msgs, dst_ref=arrived.at[k], send_sem=psend.at[k], recv_sem=precv.at[k],
            device_id={"dp": lax.rem(dp + k, groups)}, device_id_type=MESH,
        )

    def start(k, carry):
        copy_of(k).start()
        return carry

    def wait(k, carry):
        copy_of(k).wait()
        return carry

    lax.fori_loop(1, groups, start, 0)
    lax.fori_loop(1, groups, wait, 0)

    gram = arrived[0, :, 2 * tokens : 2 * tokens + wide]
    for k in range(1, groups):
        gram = gram + arrived[k, :, 2 * tokens : 2 * tokens + wide]
    for k in range(groups):
        source = lax.rem(dp - k + groups, groups)
        block = arrived[lax.rem(dp - k + groups, groups)]
        cot[:, k * tokens : (k + 1) * tokens] = block[:, 0:tokens]
        chat[:, k * tokens : (k + 1) * tokens] = block[:, tokens : 2 * tokens]
        del source

    hi, lo = split(cot[...])
    down = jnp.dot(hi, hid_ref[...], preferred_element_type=F32) + jnp.dot(
        lo, hid_ref[...], preferred_element_type=F32
    )
    hi, lo = split(chat[...])
    along = jnp.dot(hi, xs_ref[...], preferred_element_type=F32) + jnp.dot(
        lo, xs_ref[...], preferred_element_type=F32
    )
    along = jnp.where(lax.rem(dp, 2) == 0, along[:, 0:width], along[:, width : 2 * width])
    hi, lo = split(gram)
    through = jnp.dot(hi, asl_ref[...], preferred_element_type=F32) + jnp.dot(
        lo, asl_ref[...], preferred_element_type=F32
    )
    up = (SCALE * factor) * (SCALE * through - CONTROL * along)
    down = SCALE * down
    half[:, 0:units] = down[8:16, units : 2 * units]
    half[:, 128 : 128 + width] = up[8:16, :]
    swap = pltpu.make_async_remote_copy(
        src_ref=half, dst_ref=taken, send_sem=csend, recv_sem=crecv,
        device_id={"expert": other}, device_id_type=MESH,
    )
    swap.start()
    swap.wait()
    down_ref[...] = down[0:8, 0:units] + taken[:, 0:units]
    up_ref[...] = up[0:8, :] + taken[:, 128 : 128 + width]


def whole(space=pltpu.VMEM):
    return pl.BlockSpec(memory_space=space)


def body(tokens, chosen, router, partner, gate_up, a_down, a_up):
    count, d_model = tokens.shape
    groups = lax.axis_size("dp")
    experts = lax.axis_size("expert")
    zs = experts // 2
    units = gate_up.shape[2]
    width = a_up.shape[2]
    ex = lax.axis_index("expert")
    z, c = ex // 2, ex % 2
    rank = a_up.shape[1]
    gtok = zs * count

    relative = jnp.bitwise_xor(chosen, c)
    wtab = jnp.sum(
        jnp.where(relative[:, :, None] == jnp.arange(experts, dtype=jnp.int32), router[:, :, None], 0.0), axis=1
    )
    hi = wtab.astype(BF16)
    mid = (wtab - hi.astype(F32)).astype(BF16)
    low = (wtab - hi.astype(F32) - mid.astype(F32)).astype(BF16)
    mates = (partner[:, None] == jnp.arange(count, dtype=jnp.int32)).astype(BF16)
    pad = 128 - (3 * experts + count) % 128
    sent = jnp.concatenate([tokens, hi, mid, low, mates, jnp.zeros((count, pad), BF16)], axis=1)
    same = [[2 * i + k for i in range(zs)] for k in range(2)]
    held = lax.all_gather(sent, "expert", axis=0, axis_index_groups=same, tiled=True)
    x_group = held[:, :d_model]
    table = held[:, d_model:].astype(F32)
    wgroup = (
        table[:, :experts] + table[:, experts : 2 * experts] + table[:, 2 * experts : 3 * experts]
    )
    w8 = jnp.repeat(wgroup.T, rank, axis=0)
    onehot = table[:, 3 * experts : 3 * experts + count]
    tid = jnp.arange(gtok, dtype=jnp.int32)
    mate_of = jnp.where(
        tid[:, None] // count == tid[None, :] // count, jnp.tile(onehot, (1, zs)), 0.0
    )
    q = jnp.eye(gtok, dtype=F32) - mate_of.T

    packed = jnp.concatenate([a_up[0], a_down[0]], axis=1)
    pairs = lax.all_gather(packed, "expert", axis=0, tiled=False).reshape(zs, 2, rank, width + units)
    pairs = jnp.where(c == 0, pairs, pairs[:, ::-1])
    a_slice = pairs[..., :width].reshape(experts * rank, width)
    here = lax.dynamic_index_in_dim(pairs, z, 0, keepdims=False)
    a_pair = here[..., :width].reshape(2 * rank, width)
    blank = jnp.zeros((rank, units), BF16)
    b_pair = jnp.concatenate(
        [
            jnp.concatenate([a_down[0], blank], axis=1),
            jnp.concatenate([blank, here[1, :, width:]], axis=1),
        ],
        axis=0,
    )
    part = dot_t(a_pair, a_slice)
    summed = lax.all_gather(jnp.concatenate([a_pair.astype(F32), part], axis=1), "dp", axis=0, tiled=False)
    g16 = jnp.sum(summed[:, :, width:], axis=0)
    a_full = summed[:, :, :width].astype(BF16).transpose(1, 0, 2).reshape(2 * rank, groups * width)

    hidden, xs, lows = pl.pallas_call(
        functools.partial(gather_kernel, zs),
        out_shape=(
            jax.ShapeDtypeStruct((groups * gtok, 2 * units), BF16),
            jax.ShapeDtypeStruct((SIDE, SIDE, gtok, 2 * width), BF16),
            jax.ShapeDtypeStruct((zs * 16, 128), F32),
        ),
        in_specs=[whole(), whole(pl.ANY), whole()],
        out_specs=(whole(), whole(pl.ANY), whole()),
        scratch_shapes=[
            pltpu.VMEM((SIDE, SIDE, gtok, d_model), BF16),
            pltpu.VMEM((2, 2 * units, d_model), BF16),
            pltpu.VMEM((SIDE, SIDE, gtok, 2 * units), F32),
            pltpu.VMEM((SIDE, SIDE, gtok, 2 * units), F32),
            pltpu.VMEM((groups, 16, 128), F32),
            pltpu.VMEM((groups, 16, 128), F32),
            pltpu.VMEM((zs, 16, 128), F32),
            pltpu.SemaphoreType.DMA((40,)),
            pltpu.SemaphoreType.DMA((40,)),
            pltpu.SemaphoreType.DMA((4,)),
            pltpu.SemaphoreType.DMA((2,)),
            pltpu.SemaphoreType.DMA((2,)),
            pltpu.SemaphoreType.DMA((groups,)),
            pltpu.SemaphoreType.DMA((groups,)),
            pltpu.SemaphoreType.DMA((zs,)),
            pltpu.SemaphoreType.DMA((zs,)),
        ],
        compiler_params=pltpu.CompilerParams(
            collective_id=0, has_side_effects=True, vmem_limit_bytes=48 << 20
        ),
        name="gather_low",
    )(x_group, gate_up[0], b_pair)

    tall = dot_t(a_full, x_group)
    zt = jnp.dot(tall, q, precision=HIGH)

    mw = 2 * gtok + max(128, zs * 16)
    total = count * groups * experts
    down, up = pl.pallas_call(
        functools.partial(finish_kernel, zs, total),
        out_shape=(
            jax.ShapeDtypeStruct((rank, units), F32),
            jax.ShapeDtypeStruct((rank, width), F32),
        ),
        in_specs=[whole()] * 8,
        out_specs=(whole(), whole()),
        scratch_shapes=[
            pltpu.VMEM((zs * 16, gtok), F32),
            pltpu.VMEM((16, mw), F32),
            pltpu.VMEM((groups, 16, mw), F32),
            pltpu.VMEM((16, groups * gtok), F32),
            pltpu.VMEM((16, groups * gtok), F32),
            pltpu.VMEM((8, 128 + width), F32),
            pltpu.VMEM((8, 128 + width), F32),
            pltpu.SemaphoreType.DMA((groups,)),
            pltpu.SemaphoreType.DMA((groups,)),
            pltpu.SemaphoreType.DMA,
            pltpu.SemaphoreType.DMA,
        ],
        compiler_params=pltpu.CompilerParams(
            collective_id=1, has_side_effects=True, vmem_limit_bytes=32 << 20
        ),
        name="finish",
    )(lows, w8, q, g16, zt, hidden, xs.reshape(groups * gtok, 2 * width), a_slice)
    return (down[None], up[None])


def solution(mesh):
    placed = (
        P(("dp", "expert"), None),
        P(("dp", "expert"), None),
        P(("dp", "expert"), None),
        P(("dp", "expert")),
        P("expert", None, "dp", None),
        P("expert", None, "dp"),
        P("expert", None, "dp"),
    )
    return jax.shard_map(
        body,
        mesh=mesh,
        in_specs=placed,
        out_specs=(P("expert", None, "dp"), P("expert", None, "dp")),
        check_vma=False,
    )
```

```python
import functools
import math

import jax
import jax.numpy as jnp
from jax import lax
from jax.experimental import pallas as pl
from jax.experimental.pallas import tpu as pltpu
from jax.sharding import PartitionSpec as P

SCALE = 2.0
CONTROL = 0.5
SIDE = 4
HIGH = lax.Precision.HIGHEST
MESH = pl.DeviceIdType.MESH
F32 = jnp.float32
BF16 = jnp.bfloat16


def dot_t(a, b, **kw):
    return lax.dot_general(a, b, (((1,), (1,)), ((), ())), preferred_element_type=F32, **kw)


def split(v):
    hi = v.astype(BF16)
    lo = (v - hi.astype(F32)).astype(BF16)
    return hi, lo


def step_kernel(
    zs, total, tok_ref, ids_ref, route_ref, mate_ref, w_ref, adn_ref, aup_ref, down_ref, up_ref,
    zg, xf, xg, tab, pk, pks, apair, apad, aall, bd, gsend, grecv,
    xall, wbuf, accg, accu, hid, lowp, lowr, lowz, ct, msgs, met, cot, chat, half, taken,
    ssem, rsem, lsem, wssem, wrsem, asend, arecv, rsend, rrecv, lsend, lrecv,
    azsend, azrecv, gssem, grsem, psend, precv, zsend, zrecv, msend, mrecv, csend, crecv,
):
    count, d_model = tok_ref.shape
    d_half = d_model // 2
    quarter = d_half // 2
    units = w_ref.shape[1]
    width = aup_ref.shape[1]
    aw = apair.shape[1]
    tokens = zs * count
    experts = 2 * zs
    wide = zs * 16
    factor = 2.0 / math.sqrt(total)
    dp = lax.axis_index("dp")
    ex = lax.axis_index("expert")
    y, x = dp // SIDE, lax.rem(dp, SIDE)
    z, c = ex // 2, lax.rem(ex, 2)
    other = 2 * z + (1 - c)
    groups = SIDE * SIDE

    barrier = pltpu.get_barrier_semaphore()

    def greet_dp(k, carry):
        pl.semaphore_signal(barrier, inc=1, device_id={"dp": lax.rem(dp + k, groups)}, device_id_type=MESH)
        return carry

    def greet_z(k, carry):
        pl.semaphore_signal(
            barrier, inc=1, device_id={"expert": 2 * lax.rem(z + k, zs) + c}, device_id_type=MESH
        )
        return carry

    lax.fori_loop(1, zs, greet_z, 0)
    pl.semaphore_signal(barrier, inc=1, device_id={"expert": other}, device_id_type=MESH)
    lax.fori_loop(1, groups, greet_dp, 0)

    col = lax.broadcasted_iota(jnp.int32, (count, 128), 1)
    named = lax.rem(col, experts)
    wtab = jnp.zeros((count, 128), F32)
    for k in range(ids_ref.shape[1]):
        place_of = jnp.bitwise_xor(ids_ref[:, k : k + 1], c)
        wtab = wtab + jnp.where(named == place_of, route_ref[:, k : k + 1], 0.0)
    top = wtab.astype(BF16).astype(F32)
    mid = (wtab - top).astype(BF16).astype(F32)
    rest = wtab - top - mid
    pick = (col - 3 * experts == mate_ref[...]).astype(F32)
    packed = jnp.where(
        col < experts, top, jnp.where(col < 2 * experts, mid, jnp.where(col < 3 * experts, rest, pick))
    )
    zg[z, :, 0:d_model] = tok_ref[...]
    zg[z, :, d_model : d_model + 128] = packed.astype(BF16)
    pk[...] = jnp.zeros_like(pk)
    pk[:, 0:width] = aup_ref[...]
    pk[:, aw : aw + units] = adn_ref[...]

    pl.semaphore_wait(barrier, groups + zs - 1)

    def line(rightward, s):
        step = 1 if rightward else -1
        block = lax.rem(z - step * s + zs, zs)
        return pltpu.make_async_remote_copy(
            src_ref=zg.at[block], dst_ref=zg.at[block],
            send_sem=(rsend if rightward else lsend).at[s], recv_sem=(rrecv if rightward else lrecv).at[s],
            device_id={"expert": 2 * lax.rem(z + step + zs, zs) + c}, device_id_type=MESH,
        )

    def landed(rightward, s):
        step = 1 if rightward else -1
        block = lax.rem(z - step * (s + 1) + zs, zs)
        pltpu.make_async_remote_copy(
            src_ref=zg.at[block], dst_ref=zg.at[block],
            send_sem=(rsend if rightward else lsend).at[s], recv_sem=(rrecv if rightward else lrecv).at[s],
            device_id={"expert": 2 * lax.rem(z + step + zs, zs) + c}, device_id_type=MESH,
        ).wait_recv()

    reach_r, reach_l = zs // 2, zs - 1 - zs // 2
    line(True, 0).start()
    if reach_l > 0:
        line(False, 0).start()
    swap_a = pltpu.make_async_remote_copy(
        src_ref=pk, dst_ref=pks, send_sem=asend, recv_sem=arecv,
        device_id={"expert": other}, device_id_type=MESH,
    )
    swap_a.start()
    weights = []
    for g in range(2):
        mine = pltpu.make_async_copy(w_ref.at[g], wbuf.at[g, pl.ds(0, units)], lsem.at[1 + g])
        mine.start()
        theirs = pltpu.make_async_remote_copy(
            src_ref=w_ref.at[g], dst_ref=wbuf.at[g, pl.ds(units, units)],
            send_sem=wssem.at[g], recv_sem=wrsem.at[g],
            device_id={"expert": other}, device_id_type=MESH,
        )
        theirs.start()
        weights += [mine, theirs]
    accg[...] = jnp.zeros_like(accg)
    accu[...] = jnp.zeros_like(accu)

    def hop(s, carry):
        landed(True, s - 1)
        line(True, s).start()
        landed(False, s - 1)
        line(False, s).start()
        return carry

    lax.fori_loop(1, min(reach_r, reach_l), hop, 0)
    if reach_l > 0:
        landed(False, reach_l - 1)
    if reach_r > reach_l and reach_r > 1:
        landed(True, reach_r - 2)
        line(True, reach_r - 1).start()
    landed(True, reach_r - 1)

    for k in range(zs):
        xf[count * k : count * (k + 1), :] = zg[k].astype(F32)
    xg[...] = xf[:, 0:d_model].astype(BF16)
    tab[...] = xf[:, d_model : d_model + 128].astype(BF16)

    def far(h, first, step):
        along_x = (h == 0) == first
        yy = y if along_x else lax.rem(y + step + SIDE, SIDE)
        xx = lax.rem(x + step + SIDE, SIDE) if along_x else x
        return {"dp": yy * SIDE + xx}

    def place(h, da, db):
        dx, dy = (da, db) if h == 0 else (db, da)
        return lax.rem(y + dy + SIDE, SIDE), lax.rem(x + dx + SIDE, SIDE)

    def cols(h, part):
        lo = h * d_half
        if part is None:
            return pl.ds(lo, d_half)
        return pl.ds(lo + part * quarter, quarter)

    started = []

    def send(h, da, db, part, first, step, number):
        by, bx = place(h, da, db)
        block = xall.at[by, bx, :, cols(h, part)]
        source = xg.at[:, cols(h, part)] if da == 0 and db == 0 else block
        copy = pltpu.make_async_remote_copy(
            src_ref=source, dst_ref=block, send_sem=ssem.at[number], recv_sem=rsem.at[number],
            device_id=far(h, first, step), device_id_type=MESH,
        )
        copy.start()
        started.append(copy)

    def arrived(h, da, db, part, number):
        by, bx = place(h, da, db)
        block = xall.at[by, bx, :, cols(h, part)]
        pltpu.make_async_remote_copy(
            src_ref=block, dst_ref=block, send_sem=ssem.at[number], recv_sem=rsem.at[number],
            device_id=far(h, True, 1), device_id_type=MESH,
        ).wait_recv()

    offsets = (0, -1, 1, 2)

    def number(h, phase, j, kind):
        return h * 20 + (kind if phase == 0 else 4 + 4 * j + kind)

    for h in range(2):
        send(h, 0, 0, None, True, 1, number(h, 0, 0, 0))
        send(h, 0, 0, None, True, -1, number(h, 0, 0, 1))
    for h in range(2):
        send(h, 0, 0, None, False, 1, number(h, 1, 0, 0))
        send(h, 0, 0, None, False, -1, number(h, 1, 0, 1))
    own = pltpu.make_async_copy(xg, xall.at[y, x], lsem.at[0])
    own.start()

    swap_a.wait()
    lead, follow = pk[...].astype(F32), pks[...].astype(F32)
    stacked = jnp.concatenate([lead, follow], axis=0)
    apair[...] = stacked[:, 0:aw].astype(BF16)
    aall[z] = stacked[:, 0:aw].astype(BF16)
    spread = jnp.concatenate([stacked[:, 0:width], jnp.zeros((16, width), F32)], axis=1)
    odd = jnp.concatenate([jnp.zeros((16, width), F32), stacked[:, 0:width]], axis=1)
    apad[...] = jnp.where(lax.rem(dp, 2) == 0, spread, odd).astype(BF16)
    blank = jnp.zeros((8, units), F32)
    bd[...] = jnp.concatenate(
        [
            jnp.concatenate([lead[:, aw : aw + units], blank], axis=1),
            jnp.concatenate([blank, follow[:, aw : aw + units]], axis=1),
        ],
        axis=0,
    ).astype(BF16)

    def a_copy(k):
        return pltpu.make_async_remote_copy(
            src_ref=apair, dst_ref=aall.at[z], send_sem=azsend.at[k], recv_sem=azrecv.at[k],
            device_id={"expert": 2 * lax.rem(z + k, zs) + c}, device_id_type=MESH,
        )

    def a_arrival(k):
        source = lax.rem(z - k + zs, zs)
        return pltpu.make_async_remote_copy(
            src_ref=apair, dst_ref=aall.at[source], send_sem=azsend.at[k], recv_sem=azrecv.at[k],
            device_id={"expert": 2 * source + c}, device_id_type=MESH,
        )

    def start_a(k, carry):
        a_copy(k).start()
        return carry

    def wait_a(k, carry):
        a_arrival(k).wait_recv()
        a_copy(k).wait_send()
        return carry

    lax.fori_loop(1, zs, start_a, 0)

    for h in range(2):
        arrived(h, -1, 0, None, number(h, 0, 0, 0))
        send(h, -1, 0, 0, True, 1, number(h, 0, 0, 2))
        arrived(h, 1, 0, None, number(h, 0, 0, 1))
        send(h, 1, 0, 1, True, -1, number(h, 0, 0, 3))
        for j in (1, 2):
            send(h, offsets[j], 0, None, False, 1, number(h, 1, j, 0))
            send(h, offsets[j], 0, None, False, -1, number(h, 1, j, 1))
    for h in range(2):
        arrived(h, 2, 0, 0, number(h, 0, 0, 2))
        arrived(h, 2, 0, 1, number(h, 0, 0, 3))
        send(h, 2, 0, None, False, 1, number(h, 1, 3, 0))
        send(h, 2, 0, None, False, -1, number(h, 1, 3, 1))

    own.wait()
    for copy in weights:
        copy.wait()
    chunk = 512 if d_half % 512 == 0 else d_half
    rows = SIDE * tokens

    def multiply(h, db):
        by, bx = place(h, 0, db)

        def step(i, carry):
            at = pl.ds(pl.multiple_of(h * d_half + i * chunk, 128), chunk)
            if h == 0:
                block = xall[by, :, :, at]
            else:
                block = xall[:, bx, :, at]
            block = block.reshape(rows, chunk)
            for g, acc in ((0, accg), (1, accu)):
                part = dot_t(block, wbuf[g, :, at]).reshape(SIDE, rows // SIDE, 2 * units)
                if h == 0:
                    acc[by] = acc[by] + part
                else:
                    acc[:, bx] = acc[:, bx] + part
            return carry

        lax.fori_loop(0, d_half // chunk, step, 0)

    def g_copy(k):
        return pltpu.make_async_remote_copy(
            src_ref=gsend, dst_ref=grecv.at[k], send_sem=gssem.at[k], recv_sem=grsem.at[k],
            device_id={"dp": lax.rem(dp + k, groups)}, device_id_type=MESH,
        )

    def start_g(k, carry):
        g_copy(k).start()
        return carry

    def wait_g(k, carry):
        g_copy(k).wait()
        return carry + grecv[k]

    for j in range(4):
        for h in range(2):
            arrived(h, offsets[j], -1, None, number(h, 1, j, 0))
            send(h, offsets[j], -1, 0, False, 1, number(h, 1, j, 2))
            arrived(h, offsets[j], 1, None, number(h, 1, j, 1))
            send(h, offsets[j], 1, 1, False, -1, number(h, 1, j, 3))
        if j == 0:
            lax.fori_loop(1, zs, wait_a, 0)
            gsend[...] = dot_t(apair[...], aall[...].reshape(wide, aw))
            lax.fori_loop(1, groups, start_g, 0)
        if j == 1:
            for h in range(2):
                multiply(h, 0)
    for h in range(2):
        multiply(h, -1)
        multiply(h, 1)
    gmat = lax.fori_loop(1, groups, wait_g, gsend[...])
    for h in range(2):
        for j in range(4):
            arrived(h, offsets[j], 2, 0, number(h, 1, j, 2))
            arrived(h, offsets[j], 2, 1, number(h, 1, j, 3))
        multiply(h, 2)

    both = accg.shape[3]
    gate = accg[...].reshape(groups * tokens, both)
    hid[...] = (gate * (1.0 / (1.0 + jnp.exp(-gate))) * accu[...].reshape(groups * tokens, both)).astype(BF16)
    strip = pl.ds(pl.multiple_of(2 * width * (dp // 2), 128), 2 * width)
    low = dot_t(bd[...], hid[...])
    tall = dot_t(apad[...], xall[:, :, :, strip].reshape(groups * tokens, 2 * width))
    for k in range(groups):
        lowp[k, :, 0:tokens] = low[:, k * tokens : (k + 1) * tokens]
        lowp[k, :, 64 : 64 + tokens] = tall[:, k * tokens : (k + 1) * tokens]

    def low_copy(k):
        peer = lax.rem(dp + k, groups)
        return pltpu.make_async_remote_copy(
            src_ref=lowp.at[peer], dst_ref=lowr.at[k], send_sem=psend.at[k], recv_sem=precv.at[k],
            device_id={"dp": peer}, device_id_type=MESH,
        )

    def start_low(k, carry):
        low_copy(k).start()
        return carry

    def wait_low(k, carry):
        low_copy(k).wait()
        return carry + lowr[k]

    lax.fori_loop(1, groups, start_low, 0)
    row = lax.broadcasted_iota(jnp.int32, (wide, 128), 0)
    lane = lax.broadcasted_iota(jnp.int32, (wide, 128), 1)
    chooser = jnp.where((row // 8 == lax.rem(lane, experts)) & (lane < 3 * experts), 1.0, 0.0).astype(BF16)
    w8 = dot_t(chooser, tab[...])
    trow = lax.broadcasted_iota(jnp.int32, (tokens, 128), 0)
    tlane = lax.broadcasted_iota(jnp.int32, (tokens, 128), 1)
    finder = jnp.where(tlane - 3 * experts == lax.rem(trow, count), 1.0, 0.0).astype(BF16)
    t0 = lax.broadcasted_iota(jnp.int32, (tokens, tokens), 0)
    t1 = lax.broadcasted_iota(jnp.int32, (tokens, tokens), 1)
    mate = jnp.where(t0 // count == t1 // count, dot_t(finder, tab[...]), 0.0)
    q = jnp.where(t0 == t1, 1.0, 0.0) - mate
    summed = lax.fori_loop(1, groups, wait_low, lowp[dp])
    lowz[z] = summed

    def z_copy(k):
        return pltpu.make_async_remote_copy(
            src_ref=lowz.at[z], dst_ref=lowz.at[z], send_sem=zsend.at[k], recv_sem=zrecv.at[k],
            device_id={"expert": 2 * lax.rem(z + k, zs) + c}, device_id_type=MESH,
        )

    def z_arrival(k):
        source = lax.rem(z - k + zs, zs)
        return pltpu.make_async_remote_copy(
            src_ref=lowz.at[source], dst_ref=lowz.at[source], send_sem=zsend.at[k], recv_sem=zrecv.at[k],
            device_id={"expert": 2 * source + c}, device_id_type=MESH,
        )

    def start_z(k, carry):
        z_copy(k).start()
        return carry

    def wait_z(k, carry):
        z_arrival(k).wait_recv()
        return carry

    def done_z(k, carry):
        z_copy(k).wait_send()
        return carry

    lax.fori_loop(1, zs, start_z, 0)
    zt = jnp.dot(summed[:, 64 : 64 + tokens], q, precision=HIGH, preferred_element_type=F32)
    lax.fori_loop(1, zs, wait_z, 0)

    values = lowz[...].reshape(wide, 128)[:, 0:tokens] * w8
    ct[:, 0:tokens] = values
    ct[:, 64 : 64 + tokens] = w8
    here = pl.ds(pl.multiple_of(16 * z, 16), 16)
    mine = ct[here, 0:tokens]
    weight = ct[here, 64 : 64 + tokens]
    inner = jnp.dot(gmat, values, precision=HIGH, preferred_element_type=F32)
    msgs[:, 0:tokens] = weight * (factor * (SCALE * inner - CONTROL * zt))
    msgs[:, tokens : 2 * tokens] = jnp.dot(mine, q, precision=HIGH, preferred_element_type=F32)
    msgs[:, 2 * tokens : 2 * tokens + wide] = dot_t(mine, values, precision=HIGH)

    def m_copy(k):
        return pltpu.make_async_remote_copy(
            src_ref=msgs, dst_ref=met.at[k], send_sem=msend.at[k], recv_sem=mrecv.at[k],
            device_id={"dp": lax.rem(dp + k, groups)}, device_id_type=MESH,
        )

    def start_m(k, carry):
        m_copy(k).start()
        return carry

    def wait_m(k, carry):
        m_copy(k).wait()
        return carry + met[k, :, 2 * tokens : 2 * tokens + wide]

    lax.fori_loop(1, groups, start_m, 0)
    met[0] = msgs[...]
    lax.fori_loop(1, zs, done_z, 0)

    def done_line(s, carry):
        line(True, s).wait_send()
        return carry

    def done_left(s, carry):
        line(False, s).wait_send()
        return carry

    lax.fori_loop(0, reach_r, done_line, 0)
    lax.fori_loop(0, reach_l, done_left, 0)
    for copy in started:
        copy.wait_send()
    gram = lax.fori_loop(1, groups, wait_m, msgs[:, 2 * tokens : 2 * tokens + wide])
    for k in range(groups):
        block = met[lax.rem(dp - k + groups, groups)]
        cot[:, k * tokens : (k + 1) * tokens] = block[:, 0:tokens]
        chat[:, k * tokens : (k + 1) * tokens] = block[:, tokens : 2 * tokens]

    def both_parts(v, right):
        hi, lo = split(v)
        return jnp.dot(hi, right, preferred_element_type=F32) + jnp.dot(lo, right, preferred_element_type=F32)

    down = SCALE * both_parts(cot[...], hid[...])
    along = both_parts(chat[...], xall[:, :, :, strip].reshape(groups * tokens, 2 * width))
    along = jnp.where(lax.rem(dp, 2) == 0, along[:, 0:width], along[:, width : 2 * width])
    through = both_parts(gram, aall[...].reshape(wide, aw))[:, 0:width]
    up = (SCALE * factor) * (SCALE * through - CONTROL * along)
    half[:, 0:units] = down[8:16, units : 2 * units]
    half[:, 128 : 128 + width] = up[8:16, :]
    swap = pltpu.make_async_remote_copy(
        src_ref=half, dst_ref=taken, send_sem=csend, recv_sem=crecv,
        device_id={"expert": other}, device_id_type=MESH,
    )
    swap.start()
    swap.wait()
    down_ref[...] = down[0:8, 0:units] + taken[:, 0:units]
    up_ref[...] = up[0:8, :] + taken[:, 128 : 128 + width]


def whole(space=pltpu.VMEM):
    return pl.BlockSpec(memory_space=space)


def body(tokens, chosen, router, partner, gate_up, a_down, a_up):
    count, d_model = tokens.shape
    groups = lax.axis_size("dp")
    experts = lax.axis_size("expert")
    zs = experts // 2
    units = gate_up.shape[2]
    width = a_up.shape[2]
    rank = a_up.shape[1]
    gtok = zs * count
    wide = zs * 16
    aw = -(-width // 128) * 128
    mw = 2 * gtok + max(128, wide)
    total = count * groups * experts
    dma = pltpu.SemaphoreType.DMA
    down, up = pl.pallas_call(
        functools.partial(step_kernel, zs, total),
        out_shape=(
            jax.ShapeDtypeStruct((rank, units), F32),
            jax.ShapeDtypeStruct((rank, width), F32),
        ),
        in_specs=[whole()] * 4 + [whole(pl.ANY)] + [whole()] * 2,
        out_specs=(whole(), whole()),
        scratch_shapes=[
            pltpu.VMEM((zs, count, d_model + 128), BF16),
            pltpu.VMEM((gtok, d_model + 128), F32),
            pltpu.VMEM((gtok, d_model), BF16),
            pltpu.VMEM((gtok, 128), BF16),
            pltpu.VMEM((rank, aw + 128), BF16),
            pltpu.VMEM((rank, aw + 128), BF16),
            pltpu.VMEM((16, aw), BF16),
            pltpu.VMEM((16, 2 * width), BF16),
            pltpu.VMEM((zs, 16, aw), BF16),
            pltpu.VMEM((16, 2 * units), BF16),
            pltpu.VMEM((16, wide), F32),
            pltpu.VMEM((groups, 16, wide), F32),
            pltpu.VMEM((SIDE, SIDE, gtok, d_model), BF16),
            pltpu.VMEM((2, 2 * units, d_model), BF16),
            pltpu.VMEM((SIDE, SIDE, gtok, 2 * units), F32),
            pltpu.VMEM((SIDE, SIDE, gtok, 2 * units), F32),
            pltpu.VMEM((groups * gtok, 2 * units), BF16),
            pltpu.VMEM((groups, 16, 128), F32),
            pltpu.VMEM((groups, 16, 128), F32),
            pltpu.VMEM((zs, 16, 128), F32),
            pltpu.VMEM((wide, 128), F32),
            pltpu.VMEM((16, mw), F32),
            pltpu.VMEM((groups, 16, mw), F32),
            pltpu.VMEM((16, groups * gtok), F32),
            pltpu.VMEM((16, groups * gtok), F32),
            pltpu.VMEM((8, 128 + aw), F32),
            pltpu.VMEM((8, 128 + aw), F32),
            dma((40,)), dma((40,)), dma((4,)), dma((2,)), dma((2,)), dma, dma,
            dma((zs,)), dma((zs,)), dma((zs,)), dma((zs,)),
            dma((zs,)), dma((zs,)), dma((groups,)), dma((groups,)), dma((groups,)), dma((groups,)),
            dma((zs,)), dma((zs,)), dma((groups,)), dma((groups,)), dma, dma,
        ],
        compiler_params=pltpu.CompilerParams(
            collective_id=0, has_side_effects=True, vmem_limit_bytes=56 << 20
        ),
        name="lorra_step",
    )(tokens, chosen, router, partner.reshape(count, 1), gate_up[0], a_down[0], a_up[0])
    return (down[None], up[None])


def solution(mesh):
    placed = (
        P(("dp", "expert"), None),
        P(("dp", "expert"), None),
        P(("dp", "expert"), None),
        P(("dp", "expert")),
        P("expert", None, "dp", None),
        P("expert", None, "dp"),
        P("expert", None, "dp"),
    )
    return jax.shard_map(
        body,
        mesh=mesh,
        in_specs=placed,
        out_specs=(P("expert", None, "dp"), P("expert", None, "dp")),
        check_vma=False,
    )
```

```python
import functools
import math

import jax
import jax.numpy as jnp
from jax import lax
from jax.experimental import pallas as pl
from jax.experimental.pallas import tpu as pltpu
from jax.sharding import PartitionSpec as P

SCALE = 2.0
CONTROL = 0.5
SIDE = 4
SHARE = 1536
HIGH = lax.Precision.HIGHEST
MESH = pl.DeviceIdType.MESH
F32 = jnp.float32
BF16 = jnp.bfloat16


def dot_t(a, b, **kw):
    return lax.dot_general(a, b, (((1,), (1,)), ((), ())), preferred_element_type=F32, **kw)


def split(v):
    hi = v.astype(BF16)
    lo = (v - hi.astype(F32)).astype(BF16)
    return hi, lo


def step_kernel(
    zs, total, share, tok_ref, ids_ref, route_ref, mate_ref, w_ref, adn_ref, aup_ref, out_ref,
    zg, zq, xf, xt, xg, tab, pk, pks, apair, apad, aall, bd, gsend, grecv,
    xall, wbuf, accg, accu, hid, lowp, lowr, lown, lowz, val, ct, msgs, met, cot, chat, half, taken,
    ssem, rsem, lsem, wssem, wrsem, asend, arecv, rsend, rrecv, lsend, lrecv, qsend, qrecv,
    pssend, psrecv, prsend, prrecv,
    azsend, azrecv, gssem, grsem, psend, precv, zsend, zrecv, msend, mrecv, csend, crecv,
):
    count, d_model = tok_ref.shape
    part = d_model - share
    d_half = part // 2
    quarter = d_half // 2
    units = w_ref.shape[1]
    width = aup_ref.shape[1]
    aw = apair.shape[1]
    tokens = zs * count
    experts = 2 * zs
    wide = zs * 16
    factor = 2.0 / math.sqrt(total)
    qz = zq.shape[0]
    nq = zs // qz
    qrows = qz * count
    slice_w = share // qz
    dp = lax.axis_index("dp")
    ex = lax.axis_index("expert")
    y, x = dp // SIDE, lax.rem(dp, SIDE)
    z, c = ex // 2, lax.rem(ex, 2)
    a, b = z // qz, lax.rem(z, qz)
    other = 2 * z + (1 - c)
    groups = SIDE * SIDE

    barrier = pltpu.get_barrier_semaphore()

    def greet_dp(k, carry):
        pl.semaphore_signal(barrier, inc=1, device_id={"dp": lax.rem(dp + k, groups)}, device_id_type=MESH)
        return carry

    def greet_z(k, carry):
        pl.semaphore_signal(
            barrier, inc=1, device_id={"expert": 2 * lax.rem(z + k, zs) + c}, device_id_type=MESH
        )
        return carry

    lax.fori_loop(1, zs, greet_z, 0)
    pl.semaphore_signal(barrier, inc=1, device_id={"expert": other}, device_id_type=MESH)
    lax.fori_loop(1, groups, greet_dp, 0)

    weights = []
    for g in range(2):
        mine = pltpu.make_async_copy(w_ref.at[g], wbuf.at[g, pl.ds(0, units)], lsem.at[g])
        mine.start()
        weights.append(mine)
    col = lax.broadcasted_iota(jnp.int32, (count, 128), 1)
    row4 = lax.broadcasted_iota(jnp.int32, (count, 128), 0)
    named = lax.rem(col, experts)
    wtab = jnp.zeros((count, 128), F32)
    for k in range(ids_ref.shape[1]):
        place_of = jnp.bitwise_xor(ids_ref[:, k : k + 1], c)
        wtab = wtab + jnp.where(named == place_of, route_ref[:, k : k + 1], 0.0)
    top = wtab.astype(BF16).astype(F32)
    mid = (wtab - top).astype(BF16).astype(F32)
    rest = wtab - top - mid
    pick = jnp.zeros((count, 128), F32)
    for k in range(count):
        pick = jnp.where((row4 == k) & (col - 3 * experts == mate_ref[k]), 1.0, pick)
    packed = jnp.where(
        col < experts, top, jnp.where(col < 2 * experts, mid, jnp.where(col < 3 * experts, rest, pick))
    )
    zq[b] = tok_ref[...]
    zg[z, :, 0:part] = tok_ref[:, 0:part]
    zg[z, :, part : part + 128] = packed.astype(BF16)
    pk[...] = jnp.zeros_like(pk)
    pk[:, 0:width] = aup_ref[...]
    pk[:, aw : aw + units] = adn_ref[...]
    accg[...] = jnp.zeros_like(accg)
    accu[...] = jnp.zeros_like(accu)

    pl.semaphore_wait(barrier, groups + zs - 1)

    def zdev(step):
        return {"expert": 2 * lax.rem(z + step + zs, zs) + c}

    def quad_copy(k):
        return pltpu.make_async_remote_copy(
            src_ref=zq.at[b], dst_ref=zq.at[b], send_sem=qsend.at[k], recv_sem=qrecv.at[k],
            device_id={"expert": 2 * (a * qz + lax.rem(b + k, qz)) + c}, device_id_type=MESH,
        )

    def quad_arrived(k):
        slot = lax.rem(b - k + qz, qz)
        pltpu.make_async_remote_copy(
            src_ref=zq.at[slot], dst_ref=zq.at[slot], send_sem=qsend.at[k], recv_sem=qrecv.at[k],
            device_id={"expert": 2 * (a * qz + slot) + c}, device_id_type=MESH,
        ).wait_recv()

    def line(step, s):
        block = lax.rem(z - step * s + zs, zs)
        return pltpu.make_async_remote_copy(
            src_ref=zg.at[block], dst_ref=zg.at[block],
            send_sem=(rsend if step > 0 else lsend).at[s], recv_sem=(rrecv if step > 0 else lrecv).at[s],
            device_id=zdev(step), device_id_type=MESH,
        )

    def landed(step, s):
        block = lax.rem(z - step * (s + 1) + zs, zs)
        pltpu.make_async_remote_copy(
            src_ref=zg.at[block], dst_ref=zg.at[block],
            send_sem=(rsend if step > 0 else lsend).at[s], recv_sem=(rrecv if step > 0 else lrecv).at[s],
            device_id=zdev(step), device_id_type=MESH,
        ).wait_recv()

    reach = {1: zs // 2, -1: zs - 1 - zs // 2}

    def hop(s):
        for step in (1, -1):
            if 1 <= s <= reach[step]:
                landed(step, s - 1)
            if s < reach[step]:
                line(step, s).start()

    hop(0)
    for k in range(1, qz):
        quad_copy(k).start()
    swap_a = pltpu.make_async_remote_copy(
        src_ref=pk, dst_ref=pks, send_sem=asend, recv_sem=arecv,
        device_id={"expert": other}, device_id_type=MESH,
    )
    swap_a.start()
    for g in range(2):
        theirs = pltpu.make_async_remote_copy(
            src_ref=w_ref.at[g], dst_ref=wbuf.at[g, pl.ds(units, units)],
            send_sem=wssem.at[g], recv_sem=wrsem.at[g],
            device_id={"expert": other}, device_id_type=MESH,
        )
        theirs.start()
        weights.append(theirs)

    def far(h, first, step):
        along_x = (h == 0) == first
        yy = y if along_x else lax.rem(y + step + SIDE, SIDE)
        xx = lax.rem(x + step + SIDE, SIDE) if along_x else x
        return {"dp": yy * SIDE + xx}

    def place(h, da, db):
        dx, dy = (da, db) if h == 0 else (db, da)
        return lax.rem(y + dy + SIDE, SIDE), lax.rem(x + dx + SIDE, SIDE)

    def cols(h, piece):
        lo = h * d_half
        if piece is None:
            return pl.ds(lo, d_half)
        return pl.ds(lo + piece * quarter, quarter)

    started = []
    span = (pl.ds(0, qrows), pl.ds(qrows, tokens - qrows))
    offsets = (0, -1, 1, 2)

    def number(stage, h, phase, j, kind):
        return stage * 40 + h * 20 + (kind if phase == 0 else 4 + 4 * j + kind)

    def send(stage, h, da, db, piece, first, step, at):
        by, bx = place(h, da, db)
        block = xall.at[by, bx, span[stage], cols(h, piece)]
        source = xg.at[span[stage], cols(h, piece)] if da == 0 and db == 0 else block
        copy = pltpu.make_async_remote_copy(
            src_ref=source, dst_ref=block, send_sem=ssem.at[at], recv_sem=rsem.at[at],
            device_id=far(h, first, step), device_id_type=MESH,
        )
        copy.start()
        started.append(copy)

    def arrived(stage, h, da, db, piece, at):
        by, bx = place(h, da, db)
        block = xall.at[by, bx, span[stage], cols(h, piece)]
        pltpu.make_async_remote_copy(
            src_ref=block, dst_ref=block, send_sem=ssem.at[at], recv_sem=rsem.at[at],
            device_id=far(h, True, 1), device_id_type=MESH,
        ).wait_recv()

    def xy_own(stage):
        for phase in (0, 1):
            for h in range(2):
                for kind, step in ((0, 1), (1, -1)):
                    send(stage, h, 0, 0, None, phase == 0, step, number(stage, h, phase, 0, kind))
        copy = pltpu.make_async_copy(
            xg.at[span[stage], pl.ds(0, part)], xall.at[y, x, span[stage], pl.ds(0, part)], lsem.at[2 + stage]
        )
        copy.start()
        return copy

    def xy_near(stage):
        for h in range(2):
            arrived(stage, h, -1, 0, None, number(stage, h, 0, 0, 0))
            send(stage, h, -1, 0, 0, True, 1, number(stage, h, 0, 0, 2))
            arrived(stage, h, 1, 0, None, number(stage, h, 0, 0, 1))
            send(stage, h, 1, 0, 1, True, -1, number(stage, h, 0, 0, 3))
            for j in (1, 2):
                send(stage, h, offsets[j], 0, None, False, 1, number(stage, h, 1, j, 0))
                send(stage, h, offsets[j], 0, None, False, -1, number(stage, h, 1, j, 1))

    def xy_far(stage):
        for h in range(2):
            arrived(stage, h, 2, 0, 0, number(stage, h, 0, 0, 2))
            arrived(stage, h, 2, 0, 1, number(stage, h, 0, 0, 3))
            send(stage, h, 2, 0, None, False, 1, number(stage, h, 1, 3, 0))
            send(stage, h, 2, 0, None, False, -1, number(stage, h, 1, 3, 1))

    def xy_pass(stage, j):
        for h in range(2):
            arrived(stage, h, offsets[j], -1, None, number(stage, h, 1, j, 0))
            send(stage, h, offsets[j], -1, 0, False, 1, number(stage, h, 1, j, 2))
            arrived(stage, h, offsets[j], 1, None, number(stage, h, 1, j, 1))
            send(stage, h, offsets[j], 1, 1, False, -1, number(stage, h, 1, j, 3))

    def xy_last(stage, h):
        for j in range(4):
            arrived(stage, h, offsets[j], 2, 0, number(stage, h, 1, j, 2))
            arrived(stage, h, offsets[j], 2, 1, number(stage, h, 1, j, 3))

    strip_cols = pl.ds(pl.multiple_of(part + b * slice_w, 128), slice_w)

    def spread_copy(k):
        return pltpu.make_async_remote_copy(
            src_ref=xg.at[pl.ds(0, qrows), strip_cols],
            dst_ref=xall.at[y, x, pl.ds(0, qrows), strip_cols],
            send_sem=pssend.at[k], recv_sem=psrecv.at[k],
            device_id={"dp": lax.rem(dp + k, groups)}, device_id_type=MESH,
        )

    def spread_arrived(k):
        source = lax.rem(dp - k + groups, groups)
        block = xall.at[source // SIDE, lax.rem(source, SIDE), pl.ds(0, qrows), strip_cols]
        pltpu.make_async_remote_copy(
            src_ref=block, dst_ref=block, send_sem=pssend.at[k], recv_sem=psrecv.at[k],
            device_id={"dp": source}, device_id_type=MESH,
        ).wait_recv()

    def piece_at(source, holder, sub):
        theirs = lax.rem(source // qz - holder // qz + nq, nq)
        return xall.at[
            pl.ds(2 * sub, 2), :, pl.ds(pl.multiple_of(qrows * theirs, qrows), qrows),
            pl.ds(pl.multiple_of(part + lax.rem(source, qz) * slice_w, 128), slice_w),
        ]

    def ring_slot(step, s, sub):
        return (0 if step > 0 else 2 * (zs // 2)) + 2 * s + sub

    def ring_copy(step, s, sub):
        source = lax.rem(z - step * s + zs, zs)
        peer = lax.rem(z + step + zs, zs)
        at = ring_slot(step, s, sub)
        return pltpu.make_async_remote_copy(
            src_ref=piece_at(source, z, sub), dst_ref=piece_at(source, peer, sub),
            send_sem=prsend.at[at], recv_sem=prrecv.at[at], device_id=zdev(step), device_id_type=MESH,
        )

    def ring_landed(step, s, sub):
        source = lax.rem(z - step * (s + 1) + zs, zs)
        at = ring_slot(step, s, sub)
        block = piece_at(source, z, sub)
        pltpu.make_async_remote_copy(
            src_ref=block, dst_ref=block,
            send_sem=prsend.at[at], recv_sem=prrecv.at[at], device_id=zdev(step), device_id_type=MESH,
        ).wait_recv()

    def ring(s):
        for sub in range(2):
            for step in (1, -1):
                if 1 <= s <= reach[step]:
                    ring_landed(step, s - 1, sub)
                if s < reach[step]:
                    ring_copy(step, s, sub).start()

    hop(1)
    for k in range(1, qz):
        quad_arrived(k)
    for k in range(qz):
        xf[count * k : count * (k + 1), :] = zq[k].astype(F32)
    xg[0:qrows, :] = xf[0:qrows, :].astype(BF16)

    def start_spread(k, carry):
        spread_copy(k).start()
        return carry

    def wait_spread(k, carry):
        spread_arrived(k)
        return carry

    lax.fori_loop(1, groups, start_spread, 0)
    mine_q = pltpu.make_async_copy(
        xg.at[pl.ds(0, qrows), strip_cols], xall.at[y, x, pl.ds(0, qrows), strip_cols], lsem.at[4]
    )
    mine_q.start()
    own0 = xy_own(0)
    hop(2)

    swap_a.wait()
    lead, follow = pk[...].astype(F32), pks[...].astype(F32)
    stacked = jnp.concatenate([lead, follow], axis=0)
    apair[...] = stacked[:, 0:aw].astype(BF16)
    aall[z] = stacked[:, 0:aw].astype(BF16)
    spread = jnp.concatenate([stacked[:, 0:width], jnp.zeros((16, width), F32)], axis=1)
    odd = jnp.concatenate([jnp.zeros((16, width), F32), stacked[:, 0:width]], axis=1)
    apad[...] = jnp.where(lax.rem(dp, 2) == 0, spread, odd).astype(BF16)
    blank = jnp.zeros((8, units), F32)
    bd[...] = jnp.concatenate(
        [
            jnp.concatenate([lead[:, aw : aw + units], blank], axis=1),
            jnp.concatenate([blank, follow[:, aw : aw + units]], axis=1),
        ],
        axis=0,
    ).astype(BF16)

    def a_copy(k):
        return pltpu.make_async_remote_copy(
            src_ref=apair, dst_ref=aall.at[z], send_sem=azsend.at[k], recv_sem=azrecv.at[k],
            device_id=zdev(k), device_id_type=MESH,
        )

    def a_arrival(k):
        source = lax.rem(z - k + zs, zs)
        return pltpu.make_async_remote_copy(
            src_ref=apair, dst_ref=aall.at[source], send_sem=azsend.at[k], recv_sem=azrecv.at[k],
            device_id={"expert": 2 * source + c}, device_id_type=MESH,
        )

    def start_a(k, carry):
        a_copy(k).start()
        return carry

    def wait_a(k, carry):
        a_arrival(k).wait_recv()
        a_copy(k).wait_send()
        return carry

    def g_copy(k):
        return pltpu.make_async_remote_copy(
            src_ref=gsend, dst_ref=grecv.at[k], send_sem=gssem.at[k], recv_sem=grsem.at[k],
            device_id={"dp": lax.rem(dp + k, groups)}, device_id_type=MESH,
        )

    def start_g(k, carry):
        g_copy(k).start()
        return carry

    def wait_g(k, carry):
        g_copy(k).wait()
        return carry + grecv[k].astype(F32)

    steps = zs // 2
    early = {
        3: lambda: xy_near(0),
        5: lambda: xy_far(0),
        6: lambda: xy_pass(0, 0),
        7: lambda: xy_pass(0, 1),
    }
    for s in range(3, steps + 1):
        hop(s)
        if s == 4:
            mine_q.wait()
            lax.fori_loop(1, groups, wait_spread, 0)
            ring(0)
        if s == 6:
            ring(1)
        if s in early:
            early[s]()
    late = [s for s in sorted(early) if s > steps]

    order = [lax.rem(a + rho, nq) * qz + k for rho in range(nq) for k in range(qz)]
    for at, source in enumerate(order):
        xt[count * at : count * (at + 1), :] = zg[source, :, part : part + 128].astype(F32)
        if at >= qz:
            xf[count * at : count * (at + 1), 0:part] = zg[source, :, 0:part].astype(F32)
    xg[qrows:tokens, 0:part] = xf[qrows:tokens, 0:part].astype(BF16)
    tab[...] = xt[...].astype(BF16)
    own1 = xy_own(1)
    if steps < 4:
        mine_q.wait()
        lax.fori_loop(1, groups, wait_spread, 0)
        ring(0)
    if steps < 6:
        ring(1)
    for s in late:
        early[s]()
    lax.fori_loop(1, zs, start_a, 0)
    ring(2)
    xy_pass(0, 2)
    xy_near(1)
    xy_pass(0, 3)
    ring(3)
    xy_far(1)
    own0.wait()
    own1.wait()
    for copy in weights:
        copy.wait()
    for h in range(2):
        xy_last(0, h)

    def panel(block, at):
        return [dot_t(block, wbuf[g, :, at]) for g in range(2)]

    chunk = 512 if d_half % 512 == 0 else 256 if d_half % 256 == 0 else 128
    while chunk * 2 <= 1024 and d_half % (chunk * 2) == 0:
        chunk *= 2
    rows = SIDE * tokens

    def multiply(h, db):
        by, bx = place(h, 0, db)

        def step(i, carry):
            at = pl.ds(pl.multiple_of(h * d_half + i * chunk, 128), chunk)
            if h == 0:
                block = xall[by, :, :, at]
            else:
                block = xall[:, bx, :, at]
            for acc, value in zip((accg, accu), panel(block.reshape(rows, chunk), at)):
                value = value.reshape(SIDE, tokens, 2 * units)
                if h == 0:
                    acc[by] = acc[by] + value
                else:
                    acc[:, bx] = acc[:, bx] + value
            return carry

        lax.fori_loop(0, d_half // chunk, step, 0)

    def multiply_q(lo, hi):
        size = (hi - lo) * qrows

        def step(i, carry):
            at = pl.ds(pl.multiple_of(part + i * slice_w, 128), slice_w)
            block = xall[:, :, lo * qrows : hi * qrows, at].reshape(groups * size, slice_w)
            for acc, value in zip((accg, accu), panel(block, at)):
                where = (slice(None), slice(None), slice(lo * qrows, hi * qrows))
                acc[where] = acc[where] + value.reshape(SIDE, SIDE, size, 2 * units)
            return carry

        lax.fori_loop(0, qz, step, 0)

    xy_pass(1, 0)
    ring(4)
    lax.fori_loop(1, zs, wait_a, 0)
    gsend[...] = dot_t(apair[...], aall[...].reshape(wide, aw)).astype(BF16)
    lax.fori_loop(1, groups, start_g, 0)
    multiply(0, 0)
    xy_pass(1, 1)
    ring(5)
    multiply(1, 0)
    xy_pass(1, 2)
    ring(6)
    xy_pass(1, 3)
    ring(7)
    multiply(0, -1)
    multiply(0, 1)
    multiply(1, -1)
    multiply(1, 1)
    ring(8)
    multiply_q(0, nq)
    gmat = lax.fori_loop(1, groups, wait_g, gsend[...].astype(F32))
    for h in range(2):
        xy_last(1, h)
        multiply(h, 2)

    both = accg.shape[3]
    gate = accg[...].reshape(groups * tokens, both)
    hid[...] = (gate * (1.0 / (1.0 + jnp.exp(-gate))) * accu[...].reshape(groups * tokens, both)).astype(BF16)
    strip = pl.ds(pl.multiple_of(2 * width * (dp // 2), 128), 2 * width)
    low = dot_t(bd[...], hid[...])
    tall = dot_t(apad[...], xall[:, :, :, strip].reshape(groups * tokens, 2 * width))
    for k in range(groups):
        lowp[k, :, 0:tokens] = low[:, k * tokens : (k + 1) * tokens]
        lowp[k, :, 64 : 64 + tokens] = tall[:, k * tokens : (k + 1) * tokens]

    def low_copy(k):
        peer = lax.rem(dp + k, groups)
        return pltpu.make_async_remote_copy(
            src_ref=lowp.at[peer], dst_ref=lowr.at[k], send_sem=psend.at[k], recv_sem=precv.at[k],
            device_id={"dp": peer}, device_id_type=MESH,
        )

    def start_low(k, carry):
        low_copy(k).start()
        return carry

    def wait_low(k, carry):
        low_copy(k).wait()
        return carry + lowr[k]

    lax.fori_loop(1, groups, start_low, 0)
    row = lax.broadcasted_iota(jnp.int32, (wide, 128), 0)
    lane = lax.broadcasted_iota(jnp.int32, (wide, 128), 1)
    chooser = jnp.where((row // 8 == lax.rem(lane, experts)) & (lane < 3 * experts), 1.0, 0.0).astype(BF16)
    w8 = dot_t(chooser, tab[...])
    trow = lax.broadcasted_iota(jnp.int32, (tokens, 128), 0)
    tlane = lax.broadcasted_iota(jnp.int32, (tokens, 128), 1)
    finder = jnp.where(tlane - 3 * experts == lax.rem(trow, count), 1.0, 0.0).astype(BF16)
    t0 = lax.broadcasted_iota(jnp.int32, (tokens, tokens), 0)
    t1 = lax.broadcasted_iota(jnp.int32, (tokens, tokens), 1)
    mate = jnp.where(t0 // count == t1 // count, dot_t(finder, tab[...]), 0.0)
    q = jnp.where(t0 == t1, 1.0, 0.0) - mate
    summed = lax.fori_loop(1, groups, wait_low, lowp[dp])
    lown[:, 0:tokens] = summed[0:8, 0:tokens]
    lown[:, 64 : 64 + tokens] = summed[8:16, 0:tokens]

    def z_copy(k):
        return pltpu.make_async_remote_copy(
            src_ref=lown, dst_ref=lowz.at[z], send_sem=zsend.at[k], recv_sem=zrecv.at[k],
            device_id=zdev(k), device_id_type=MESH,
        )

    def z_arrival(k):
        source = lax.rem(z - k + zs, zs)
        return pltpu.make_async_remote_copy(
            src_ref=lown, dst_ref=lowz.at[source], send_sem=zsend.at[k], recv_sem=zrecv.at[k],
            device_id={"expert": 2 * source + c}, device_id_type=MESH,
        )

    def start_z(k, carry):
        z_copy(k).start()
        return carry

    def wait_z(k, carry):
        z_arrival(k).wait_recv()
        return carry

    def done_z(k, carry):
        z_copy(k).wait_send()
        return carry

    lax.fori_loop(1, zs, start_z, 0)
    lowz[z] = lown[...]
    zt = jnp.dot(summed[:, 64 : 64 + tokens], q, precision=HIGH, preferred_element_type=F32)
    lax.fori_loop(1, zs, wait_z, 0)

    for rho in range(nq):
        there = pl.ds(qz * lax.rem(a + rho, nq), qz)
        found = lowz[there]
        turn = qrows * rho
        for o in range(2):
            lanes = found[:, :, 64 * o : 64 * o + tokens]
            if turn:
                lanes = jnp.concatenate([lanes[:, :, tokens - turn :], lanes[:, :, : tokens - turn]], axis=2)
            val[there, 8 * o : 8 * o + 8, 0:tokens] = lanes
    values = val[...].reshape(wide, 128)[:, 0:tokens] * w8
    ct[:, 0:tokens] = values
    ct[:, 64 : 64 + tokens] = w8
    here = pl.ds(pl.multiple_of(16 * z, 16), 16)
    mine = ct[here, 0:tokens]
    weight = ct[here, 64 : 64 + tokens]
    inner = jnp.dot(gmat, values, precision=HIGH, preferred_element_type=F32)
    first = weight * (factor * (SCALE * inner - CONTROL * zt))
    second = jnp.dot(mine, q, precision=HIGH, preferred_element_type=F32)
    msgs[:, 0 : 2 * tokens] = jnp.concatenate([first, second], axis=1).astype(BF16)
    msgs[:, 2 * tokens : 2 * tokens + wide] = dot_t(mine, values, precision=HIGH).astype(BF16)

    def m_copy(k):
        return pltpu.make_async_remote_copy(
            src_ref=msgs, dst_ref=met.at[k], send_sem=msend.at[k], recv_sem=mrecv.at[k],
            device_id={"dp": lax.rem(dp + k, groups)}, device_id_type=MESH,
        )

    def start_m(k, carry):
        m_copy(k).start()
        return carry

    def wait_m(k, carry):
        m_copy(k).wait()
        return carry + met[k, :, 2 * tokens : 2 * tokens + wide].astype(F32)

    lax.fori_loop(1, groups, start_m, 0)
    met[0] = msgs[...]
    lax.fori_loop(1, zs, done_z, 0)
    for step in (1, -1):
        for s in range(reach[step]):
            line(step, s).wait_send()
            for sub in range(2):
                ring_copy(step, s, sub).wait_send()
    for k in range(1, qz):
        quad_copy(k).wait_send()

    def done_spread(k, carry):
        spread_copy(k).wait_send()
        return carry

    lax.fori_loop(1, groups, done_spread, 0)
    for copy in started:
        copy.wait_send()
    gram = lax.fori_loop(1, groups, wait_m, msgs[:, 2 * tokens : 2 * tokens + wide].astype(F32))
    for k in range(groups):
        block = met[lax.rem(dp - k + groups, groups), :, 0 : 2 * tokens].astype(F32)
        cot[:, k * tokens : (k + 1) * tokens] = block[:, 0:tokens]
        chat[:, k * tokens : (k + 1) * tokens] = block[:, tokens : 2 * tokens]

    down = SCALE * jnp.dot(cot[...].astype(BF16), hid[...], preferred_element_type=F32)
    along = jnp.dot(
        chat[...].astype(BF16), xall[:, :, :, strip].reshape(groups * tokens, 2 * width),
        preferred_element_type=F32,
    )
    along = jnp.where(lax.rem(dp, 2) == 0, along[:, 0:width], along[:, width : 2 * width])
    slices = aall[...].reshape(wide, aw)
    hi, lo = split(gram)
    through = jnp.dot(hi, slices, preferred_element_type=F32) + jnp.dot(lo, slices, preferred_element_type=F32)
    up = (SCALE * factor) * (SCALE * through[:, 0:width] - CONTROL * along)
    half[:, 0:units] = down[8:16, units : 2 * units]
    half[:, 128 : 128 + width] = up[8:16, :]
    swap = pltpu.make_async_remote_copy(
        src_ref=half, dst_ref=taken, send_sem=csend, recv_sem=crecv,
        device_id={"expert": other}, device_id_type=MESH,
    )
    swap.start()
    swap.wait()
    out_ref[...] = jnp.zeros_like(out_ref)
    out_ref[:, 0:units] = down[0:8, 0:units] + taken[:, 0:units]
    out_ref[:, 128 : 128 + width] = up[0:8, :] + taken[:, 128 : 128 + width]


def part_kernel(both_ref, down_ref, up_ref):
    down_ref[...] = both_ref[:, 0 : down_ref.shape[1]]
    up_ref[...] = both_ref[:, 128 : 128 + up_ref.shape[1]]


def whole(space=pltpu.VMEM):
    return pl.BlockSpec(memory_space=space)


def body(tokens, chosen, router, partner, gate_up, a_down, a_up):
    count, d_model = tokens.shape
    groups = lax.axis_size("dp")
    experts = lax.axis_size("expert")
    zs = experts // 2
    units = gate_up.shape[2]
    width = a_up.shape[2]
    rank = a_up.shape[1]
    gtok = zs * count
    wide = zs * 16
    qz = 4 if zs >= 8 else 2
    share = SHARE if d_model == 5120 else d_model // 2
    aw = -(-width // 128) * 128
    mw = 2 * gtok + max(128, wide)
    total = count * groups * experts
    dma = pltpu.SemaphoreType.DMA
    out = pl.pallas_call(
        functools.partial(step_kernel, zs, total, share),
        out_shape=jax.ShapeDtypeStruct((rank, 128 + aw), F32),
        in_specs=[whole()] * 3 + [whole(pltpu.SMEM), whole(pl.ANY)] + [whole()] * 2,
        out_specs=whole(),
        scratch_shapes=[
            pltpu.VMEM((zs, count, d_model - share + 128), BF16),
            pltpu.VMEM((qz, count, d_model), BF16),
            pltpu.VMEM((gtok, d_model), F32),
            pltpu.VMEM((gtok, 128), F32),
            pltpu.VMEM((gtok, d_model), BF16),
            pltpu.VMEM((gtok, 128), BF16),
            pltpu.VMEM((rank, aw + 128), BF16),
            pltpu.VMEM((rank, aw + 128), BF16),
            pltpu.VMEM((16, aw), BF16),
            pltpu.VMEM((16, 2 * width), BF16),
            pltpu.VMEM((zs, 16, aw), BF16),
            pltpu.VMEM((16, 2 * units), BF16),
            pltpu.VMEM((16, wide), BF16),
            pltpu.VMEM((groups, 16, wide), BF16),
            pltpu.VMEM((SIDE, SIDE, gtok, d_model), BF16),
            pltpu.VMEM((2, 2 * units, d_model), BF16),
            pltpu.VMEM((SIDE, SIDE, gtok, 2 * units), F32),
            pltpu.VMEM((SIDE, SIDE, gtok, 2 * units), F32),
            pltpu.VMEM((groups * gtok, 2 * units), BF16),
            pltpu.VMEM((groups, 16, 128), F32),
            pltpu.VMEM((groups, 16, 128), F32),
            pltpu.VMEM((8, 128), F32),
            pltpu.VMEM((zs, 8, 128), F32),
            pltpu.VMEM((zs, 16, 128), F32),
            pltpu.VMEM((wide, 128), F32),
            pltpu.VMEM((16, mw), BF16),
            pltpu.VMEM((groups, 16, mw), BF16),
            pltpu.VMEM((16, groups * gtok), F32),
            pltpu.VMEM((16, groups * gtok), F32),
            pltpu.VMEM((8, 128 + aw), F32),
            pltpu.VMEM((8, 128 + aw), F32),
            dma((80,)), dma((80,)), dma((5,)), dma((2,)), dma((2,)), dma, dma,
            dma((zs,)), dma((zs,)), dma((zs,)), dma((zs,)), dma((qz,)), dma((qz,)),
            dma((groups,)), dma((groups,)), dma((2 * zs,)), dma((2 * zs,)),
            dma((zs,)), dma((zs,)), dma((groups,)), dma((groups,)), dma((groups,)), dma((groups,)),
            dma((zs,)), dma((zs,)), dma((groups,)), dma((groups,)), dma, dma,
        ],
        compiler_params=pltpu.CompilerParams(
            collective_id=0, has_side_effects=True, vmem_limit_bytes=56 << 20
        ),
        name="lorra_step",
    )(tokens, chosen, router, partner, gate_up[0], a_down[0], a_up[0])
    down, up = pl.pallas_call(
        part_kernel,
        out_shape=(
            jax.ShapeDtypeStruct((rank, units), F32),
            jax.ShapeDtypeStruct((rank, width), F32),
        ),
        in_specs=[whole()],
        out_specs=(whole(), whole()),
        name="part",
    )(out)
    return (down[None], up[None])


def solution(mesh):
    placed = (
        P(("dp", "expert"), None),
        P(("dp", "expert"), None),
        P(("dp", "expert"), None),
        P(("dp", "expert")),
        P("expert", None, "dp", None),
        P("expert", None, "dp"),
        P("expert", None, "dp"),
    )
    return jax.shard_map(
        body,
        mesh=mesh,
        in_specs=placed,
        out_specs=(P("expert", None, "dp"), P("expert", None, "dp")),
        check_vma=False,
    )
```

```python
import functools
import math

import jax
import jax.numpy as jnp
from jax import lax
from jax.experimental import pallas as pl
from jax.experimental.pallas import tpu as pltpu
from jax.sharding import PartitionSpec as P

SCALE = 2.0
CONTROL = 0.5
SIDE = 4
SHARE = 1536
HIGH = lax.Precision.HIGHEST
MESH = pl.DeviceIdType.MESH
F32 = jnp.float32
BF16 = jnp.bfloat16


def dot_t(a, b, **kw):
    return lax.dot_general(a, b, (((1,), (1,)), ((), ())), preferred_element_type=F32, **kw)


def split(v):
    hi = v.astype(BF16)
    lo = (v - hi.astype(F32)).astype(BF16)
    return hi, lo


def step_kernel(
    zs, total, share, tok_ref, ids_ref, route_ref, mate_ref, w_ref, adn_ref, aup_ref, out_ref,
    zg, zq, xf, xt, xg, tab, pk, pks, apair, apad, aall, bd, gsend, grecv,
    xall, wbuf, accg, accu, hid, lowp, lowr, lown, lowz, val, ct, msgs, met, cot, chat, half, taken,
    ssem, rsem, lsem, wssem, wrsem, asend, arecv, rsend, rrecv, lsend, lrecv, qsend, qrecv,
    pssend, psrecv, prsend, prrecv,
    azsend, azrecv, gssem, grsem, psend, precv, zsend, zrecv, msend, mrecv, csend, crecv,
):
    count, d_model = tok_ref.shape
    part = d_model - share
    d_half = part // 2
    quarter = d_half // 2
    units = w_ref.shape[1]
    width = aup_ref.shape[1]
    aw = apair.shape[1]
    tokens = zs * count
    experts = 2 * zs
    wide = zs * 16
    factor = 2.0 / math.sqrt(total)
    qz = zq.shape[0]
    nq = zs // qz
    qrows = qz * count
    slice_w = share // qz
    dp = lax.axis_index("dp")
    ex = lax.axis_index("expert")
    y, x = dp // SIDE, lax.rem(dp, SIDE)
    z, c = ex // 2, lax.rem(ex, 2)
    a, b = z // qz, lax.rem(z, qz)
    up_side = (2 * b) // qz
    quads = (a, lax.rem(a + 2 * up_side + 3, nq), lax.rem(a + 5 - 2 * up_side, nq), lax.rem(a + 2, nq))
    other = 2 * z + (1 - c)
    groups = SIDE * SIDE

    barrier = pltpu.get_barrier_semaphore()

    def greet_dp(k, carry):
        pl.semaphore_signal(barrier, inc=1, device_id={"dp": lax.rem(dp + k, groups)}, device_id_type=MESH)
        return carry

    def greet_z(k, carry):
        pl.semaphore_signal(
            barrier, inc=1, device_id={"expert": 2 * lax.rem(z + k, zs) + c}, device_id_type=MESH
        )
        return carry

    lax.fori_loop(1, zs, greet_z, 0)
    pl.semaphore_signal(barrier, inc=1, device_id={"expert": other}, device_id_type=MESH)
    lax.fori_loop(1, groups, greet_dp, 0)

    weights = []
    for g in range(2):
        mine = pltpu.make_async_copy(w_ref.at[g], wbuf.at[g, pl.ds(0, units)], lsem.at[g])
        mine.start()
        weights.append(mine)
    col = lax.broadcasted_iota(jnp.int32, (count, 128), 1)
    row4 = lax.broadcasted_iota(jnp.int32, (count, 128), 0)
    named = lax.rem(col, experts)
    wtab = jnp.zeros((count, 128), F32)
    for k in range(ids_ref.shape[1]):
        place_of = jnp.bitwise_xor(ids_ref[:, k : k + 1], c)
        wtab = wtab + jnp.where(named == place_of, route_ref[:, k : k + 1], 0.0)
    top = wtab.astype(BF16).astype(F32)
    mid = (wtab - top).astype(BF16).astype(F32)
    rest = wtab - top - mid
    pick = jnp.zeros((count, 128), F32)
    for k in range(count):
        pick = jnp.where((row4 == k) & (col - 3 * experts == mate_ref[k]), 1.0, pick)
    packed = jnp.where(
        col < experts, top, jnp.where(col < 2 * experts, mid, jnp.where(col < 3 * experts, rest, pick))
    )
    zq[b] = tok_ref[...]
    zg[z, :, 0:part] = tok_ref[:, 0:part]
    zg[z, :, part : part + 128] = packed.astype(BF16)
    pk[...] = jnp.zeros_like(pk)
    pk[:, 0:width] = aup_ref[...]
    pk[:, aw : aw + units] = adn_ref[...]
    accg[...] = jnp.zeros_like(accg)
    accu[...] = jnp.zeros_like(accu)

    pl.semaphore_wait(barrier, groups + zs - 1)

    def zdev(step):
        return {"expert": 2 * lax.rem(z + step + zs, zs) + c}

    def quad_copy(k):
        return pltpu.make_async_remote_copy(
            src_ref=zq.at[b], dst_ref=zq.at[b], send_sem=qsend.at[k], recv_sem=qrecv.at[k],
            device_id={"expert": 2 * (a * qz + lax.rem(b + k, qz)) + c}, device_id_type=MESH,
        )

    def quad_arrived(k):
        slot = lax.rem(b - k + qz, qz)
        pltpu.make_async_remote_copy(
            src_ref=zq.at[slot], dst_ref=zq.at[slot], send_sem=qsend.at[k], recv_sem=qrecv.at[k],
            device_id={"expert": 2 * (a * qz + slot) + c}, device_id_type=MESH,
        ).wait_recv()

    def line(step, s):
        block = lax.rem(z - step * s + zs, zs)
        return pltpu.make_async_remote_copy(
            src_ref=zg.at[block], dst_ref=zg.at[block],
            send_sem=(rsend if step > 0 else lsend).at[s], recv_sem=(rrecv if step > 0 else lrecv).at[s],
            device_id=zdev(step), device_id_type=MESH,
        )

    def landed(step, s):
        block = lax.rem(z - step * (s + 1) + zs, zs)
        pltpu.make_async_remote_copy(
            src_ref=zg.at[block], dst_ref=zg.at[block],
            send_sem=(rsend if step > 0 else lsend).at[s], recv_sem=(rrecv if step > 0 else lrecv).at[s],
            device_id=zdev(step), device_id_type=MESH,
        ).wait_recv()

    reach = {1: zs // 2, -1: zs - 1 - zs // 2}

    def hop(s):
        for step in (1, -1):
            if 1 <= s <= reach[step]:
                landed(step, s - 1)
            if s < reach[step]:
                line(step, s).start()

    hop(0)
    for k in range(1, qz):
        quad_copy(k).start()
    swap_a = pltpu.make_async_remote_copy(
        src_ref=pk, dst_ref=pks, send_sem=asend, recv_sem=arecv,
        device_id={"expert": other}, device_id_type=MESH,
    )
    swap_a.start()
    for g in range(2):
        theirs = pltpu.make_async_remote_copy(
            src_ref=w_ref.at[g], dst_ref=wbuf.at[g, pl.ds(units, units)],
            send_sem=wssem.at[g], recv_sem=wrsem.at[g],
            device_id={"expert": other}, device_id_type=MESH,
        )
        theirs.start()
        weights.append(theirs)

    def a_line(step, s):
        block = lax.rem(z - step * s + zs, zs)
        return pltpu.make_async_remote_copy(
            src_ref=aall.at[block], dst_ref=aall.at[block],
            send_sem=azsend.at[(0 if step > 0 else zs // 2) + s], recv_sem=azrecv.at[(0 if step > 0 else zs // 2) + s],
            device_id=zdev(step), device_id_type=MESH,
        )

    def a_landed(step, s):
        block = lax.rem(z - step * (s + 1) + zs, zs)
        pltpu.make_async_remote_copy(
            src_ref=aall.at[block], dst_ref=aall.at[block],
            send_sem=azsend.at[(0 if step > 0 else zs // 2) + s], recv_sem=azrecv.at[(0 if step > 0 else zs // 2) + s],
            device_id=zdev(step), device_id_type=MESH,
        ).wait_recv()

    def a_hop(s):
        for step in (1, -1):
            if 1 <= s <= reach[step]:
                a_landed(step, s - 1)
            if s < reach[step]:
                a_line(step, s).start()

    def far(h, first, step):
        along_x = (h == 0) == first
        yy = y if along_x else lax.rem(y + step + SIDE, SIDE)
        xx = lax.rem(x + step + SIDE, SIDE) if along_x else x
        return {"dp": yy * SIDE + xx}

    def place(h, da, db):
        dx, dy = (da, db) if h == 0 else (db, da)
        return lax.rem(y + dy + SIDE, SIDE), lax.rem(x + dx + SIDE, SIDE)

    def cols(h, piece):
        lo = h * d_half
        if piece is None:
            return pl.ds(lo, d_half)
        return pl.ds(lo + piece * quarter, quarter)

    started = []
    span = (pl.ds(0, qrows), pl.ds(qrows, qrows), pl.ds(2 * qrows, 2 * qrows))
    offsets = (0, -1, 1, 2)

    def number(stage, h, phase, j, kind):
        return stage * 40 + h * 20 + (kind if phase == 0 else 4 + 4 * j + kind)

    def send(stage, h, da, db, piece, first, step, at):
        by, bx = place(h, da, db)
        block = xall.at[by, bx, span[stage], cols(h, piece)]
        source = xg.at[span[stage], cols(h, piece)] if da == 0 and db == 0 else block
        copy = pltpu.make_async_remote_copy(
            src_ref=source, dst_ref=block, send_sem=ssem.at[at], recv_sem=rsem.at[at],
            device_id=far(h, first, step), device_id_type=MESH,
        )
        copy.start()
        started.append(copy)

    def arrived(stage, h, da, db, piece, at):
        by, bx = place(h, da, db)
        block = xall.at[by, bx, span[stage], cols(h, piece)]
        pltpu.make_async_remote_copy(
            src_ref=block, dst_ref=block, send_sem=ssem.at[at], recv_sem=rsem.at[at],
            device_id=far(h, True, 1), device_id_type=MESH,
        ).wait_recv()

    def xy_own(stage):
        for phase in (0, 1):
            for h in range(2):
                for kind, step in ((0, 1), (1, -1)):
                    send(stage, h, 0, 0, None, phase == 0, step, number(stage, h, phase, 0, kind))
        copy = pltpu.make_async_copy(
            xg.at[span[stage], pl.ds(0, part)], xall.at[y, x, span[stage], pl.ds(0, part)], lsem.at[2 + stage]
        )
        copy.start()
        return copy

    def xy_near(stage):
        for h in range(2):
            arrived(stage, h, -1, 0, None, number(stage, h, 0, 0, 0))
            send(stage, h, -1, 0, 0, True, 1, number(stage, h, 0, 0, 2))
            arrived(stage, h, 1, 0, None, number(stage, h, 0, 0, 1))
            send(stage, h, 1, 0, 1, True, -1, number(stage, h, 0, 0, 3))
            for j in (1, 2):
                send(stage, h, offsets[j], 0, None, False, 1, number(stage, h, 1, j, 0))
                send(stage, h, offsets[j], 0, None, False, -1, number(stage, h, 1, j, 1))

    def xy_far(stage):
        for h in range(2):
            arrived(stage, h, 2, 0, 0, number(stage, h, 0, 0, 2))
            arrived(stage, h, 2, 0, 1, number(stage, h, 0, 0, 3))
            send(stage, h, 2, 0, None, False, 1, number(stage, h, 1, 3, 0))
            send(stage, h, 2, 0, None, False, -1, number(stage, h, 1, 3, 1))

    def xy_pass(stage, j):
        for h in range(2):
            arrived(stage, h, offsets[j], -1, None, number(stage, h, 1, j, 0))
            send(stage, h, offsets[j], -1, 0, False, 1, number(stage, h, 1, j, 2))
            arrived(stage, h, offsets[j], 1, None, number(stage, h, 1, j, 1))
            send(stage, h, offsets[j], 1, 1, False, -1, number(stage, h, 1, j, 3))

    def xy_last(stage, h):
        for j in range(4):
            arrived(stage, h, offsets[j], 2, 0, number(stage, h, 1, j, 2))
            arrived(stage, h, offsets[j], 2, 1, number(stage, h, 1, j, 3))

    strip_cols = pl.ds(pl.multiple_of(part + b * slice_w, 128), slice_w)

    def spread_copy(k):
        return pltpu.make_async_remote_copy(
            src_ref=xg.at[pl.ds(0, qrows), strip_cols],
            dst_ref=xall.at[y, x, pl.ds(0, qrows), strip_cols],
            send_sem=pssend.at[k], recv_sem=psrecv.at[k],
            device_id={"dp": lax.rem(dp + k, groups)}, device_id_type=MESH,
        )

    def spread_arrived(k):
        source = lax.rem(dp - k + groups, groups)
        block = xall.at[source // SIDE, lax.rem(source, SIDE), pl.ds(0, qrows), strip_cols]
        pltpu.make_async_remote_copy(
            src_ref=block, dst_ref=block, send_sem=pssend.at[k], recv_sem=psrecv.at[k],
            device_id={"dp": source}, device_id_type=MESH,
        ).wait_recv()

    def piece_at(source, holder, sub):
        gap = lax.rem(source // qz - holder // qz + nq, nq)
        side = (2 * lax.rem(holder, qz)) // qz
        odd_gap = lax.rem(gap, 2)
        theirs = (1 - odd_gap) * (gap // 2) * 3 + odd_gap * (2 - side + (gap // 2) * (2 * side - 1))
        return xall.at[
            pl.ds(2 * sub, 2), :, pl.ds(pl.multiple_of(qrows * theirs, qrows), qrows),
            pl.ds(pl.multiple_of(part + lax.rem(source, qz) * slice_w, 128), slice_w),
        ]

    def ring_slot(step, s, sub):
        return (0 if step > 0 else 2 * (zs // 2)) + 2 * s + sub

    def ring_copy(step, s, sub):
        source = lax.rem(z - step * s + zs, zs)
        peer = lax.rem(z + step + zs, zs)
        at = ring_slot(step, s, sub)
        return pltpu.make_async_remote_copy(
            src_ref=piece_at(source, z, sub), dst_ref=piece_at(source, peer, sub),
            send_sem=prsend.at[at], recv_sem=prrecv.at[at], device_id=zdev(step), device_id_type=MESH,
        )

    def ring_landed(step, s, sub):
        source = lax.rem(z - step * (s + 1) + zs, zs)
        at = ring_slot(step, s, sub)
        block = piece_at(source, z, sub)
        pltpu.make_async_remote_copy(
            src_ref=block, dst_ref=block,
            send_sem=prsend.at[at], recv_sem=prrecv.at[at], device_id=zdev(step), device_id_type=MESH,
        ).wait_recv()

    def ring(s):
        for sub in range(2):
            for step in (1, -1):
                if 1 <= s <= reach[step]:
                    ring_landed(step, s - 1, sub)
                if s < reach[step]:
                    ring_copy(step, s, sub).start()

    hop(1)
    for k in range(1, qz):
        quad_arrived(k)
    for k in range(qz):
        xf[count * k : count * (k + 1), :] = zq[k].astype(F32)
    xg[0:qrows, :] = xf[0:qrows, :].astype(BF16)

    def start_spread(k, carry):
        spread_copy(k).start()
        return carry

    def wait_spread(k, carry):
        spread_arrived(k)
        return carry

    lax.fori_loop(1, groups, start_spread, 0)
    mine_q = pltpu.make_async_copy(
        xg.at[pl.ds(0, qrows), strip_cols], xall.at[y, x, pl.ds(0, qrows), strip_cols], lsem.at[5]
    )
    mine_q.start()
    own0 = xy_own(0)
    hop(2)

    swap_a.wait()
    lead, follow = pk[...].astype(F32), pks[...].astype(F32)
    stacked = jnp.concatenate([lead, follow], axis=0)
    apair[...] = stacked[:, 0:aw].astype(BF16)
    aall[z] = stacked[:, 0:aw].astype(BF16)
    spread = jnp.concatenate([stacked[:, 0:width], jnp.zeros((16, width), F32)], axis=1)
    odd = jnp.concatenate([jnp.zeros((16, width), F32), stacked[:, 0:width]], axis=1)
    apad[...] = jnp.where(lax.rem(dp, 2) == 0, spread, odd).astype(BF16)
    blank = jnp.zeros((8, units), F32)
    bd[...] = jnp.concatenate(
        [
            jnp.concatenate([lead[:, aw : aw + units], blank], axis=1),
            jnp.concatenate([blank, follow[:, aw : aw + units]], axis=1),
        ],
        axis=0,
    ).astype(BF16)

    def g_copy(k):
        return pltpu.make_async_remote_copy(
            src_ref=gsend, dst_ref=grecv.at[k], send_sem=gssem.at[k], recv_sem=grsem.at[k],
            device_id={"dp": lax.rem(dp + k, groups)}, device_id_type=MESH,
        )

    def start_g(k, carry):
        g_copy(k).start()
        return carry

    def wait_g(k, carry):
        g_copy(k).wait()
        return carry + grecv[k].astype(F32)

    def bring(r):
        for k in range(qz):
            at = (r * qz + k) * count
            xf[at : at + count, 0:part] = zg[quads[r] * qz + k, :, 0:part].astype(F32)
        rows_r = slice(r * qrows, (r + 1) * qrows)
        xg[rows_r, 0:part] = xf[rows_r, 0:part].astype(BF16)

    a_hop(0)
    xy_near(0)
    hop(3)
    mine_q.wait()
    lax.fori_loop(1, groups, wait_spread, 0)
    ring(0)
    a_hop(1)
    xy_far(0)
    hop(4)
    xy_pass(0, 0)
    a_hop(2)
    hop(5)
    bring(1)
    own1 = xy_own(1)
    ring(1)
    xy_pass(0, 1)
    a_hop(3)
    hop(6)
    xy_near(1)
    ring(2)
    xy_pass(0, 2)
    a_hop(4)
    hop(7)
    xy_far(1)
    ring(3)
    xy_pass(0, 3)
    a_hop(5)
    hop(8)
    bring(2)
    bring(3)
    own2 = xy_own(2)
    for r in range(nq):
        for k in range(qz):
            at = (r * qz + k) * count
            xt[at : at + count, :] = zg[quads[r] * qz + k, :, part : part + 128].astype(F32)
    tab[...] = xt[...].astype(BF16)
    xy_pass(1, 0)
    a_hop(6)
    ring(4)
    xy_near(2)
    xy_pass(1, 1)
    a_hop(7)
    for h in range(2):
        xy_last(0, h)
    xy_far(2)
    a_hop(8)
    ring(5)
    own0.wait()
    own1.wait()
    own2.wait()
    for copy in weights:
        copy.wait()
    xy_pass(1, 2)
    xy_pass(1, 3)

    def panel(block, at):
        return [dot_t(block, wbuf[g, :, at]) for g in range(2)]

    chunk = d_half
    rows = SIDE * tokens

    def multiply(h, db):
        by, bx = place(h, 0, db)

        def step(i, carry):
            at = pl.ds(pl.multiple_of(h * d_half + i * chunk, 128), chunk)
            if h == 0:
                block = xall[by, :, :, at]
            else:
                block = xall[:, bx, :, at]
            for acc, value in zip((accg, accu), panel(block.reshape(rows, chunk), at)):
                value = value.reshape(SIDE, tokens, 2 * units)
                if h == 0:
                    acc[by] = acc[by] + value
                else:
                    acc[:, bx] = acc[:, bx] + value
            return carry

        lax.fori_loop(0, d_half // chunk, step, 0)

    def multiply_q():
        at = pl.ds(part, share)

        def step(i, carry):
            block = xall[i, :, :, at].reshape(rows, share)
            for acc, value in zip((accg, accu), panel(block, at)):
                acc[i] = acc[i] + value.reshape(SIDE, tokens, 2 * units)
            return carry

        lax.fori_loop(0, SIDE, step, 0)

    xy_pass(2, 0)
    ring(6)
    gsend[...] = dot_t(apair[...], aall[...].reshape(wide, aw)).astype(BF16)
    lax.fori_loop(1, groups, start_g, 0)
    multiply(0, 0)
    xy_pass(2, 1)
    ring(7)
    multiply(1, 0)
    xy_pass(2, 2)
    for h in range(2):
        xy_last(1, h)
    xy_pass(2, 3)
    ring(8)
    for h in range(2):
        multiply(h, -1)
        multiply(h, 1)
    multiply_q()
    gmat = lax.fori_loop(1, groups, wait_g, gsend[...].astype(F32))
    for h in range(2):
        xy_last(2, h)
        multiply(h, 2)

    both = accg.shape[3]
    gate = accg[...].reshape(groups * tokens, both)
    hid[...] = (gate * (1.0 / (1.0 + jnp.exp(-gate))) * accu[...].reshape(groups * tokens, both)).astype(BF16)
    strip = pl.ds(pl.multiple_of(2 * width * (dp // 2), 128), 2 * width)
    low = dot_t(bd[...], hid[...])
    tall = dot_t(apad[...], xall[:, :, :, strip].reshape(groups * tokens, 2 * width))
    for k in range(groups):
        lowp[k, :, 0:tokens] = low[:, k * tokens : (k + 1) * tokens]
        lowp[k, :, 64 : 64 + tokens] = tall[:, k * tokens : (k + 1) * tokens]

    def low_copy(k):
        peer = lax.rem(dp + k, groups)
        return pltpu.make_async_remote_copy(
            src_ref=lowp.at[peer], dst_ref=lowr.at[k], send_sem=psend.at[k], recv_sem=precv.at[k],
            device_id={"dp": peer}, device_id_type=MESH,
        )

    def start_low(k, carry):
        low_copy(k).start()
        return carry

    def wait_low(k, carry):
        low_copy(k).wait()
        return carry + lowr[k]

    lax.fori_loop(1, groups, start_low, 0)
    row = lax.broadcasted_iota(jnp.int32, (wide, 128), 0)
    lane = lax.broadcasted_iota(jnp.int32, (wide, 128), 1)
    chooser = jnp.where((row // 8 == lax.rem(lane, experts)) & (lane < 3 * experts), 1.0, 0.0).astype(BF16)
    w8 = dot_t(chooser, tab[...])
    trow = lax.broadcasted_iota(jnp.int32, (tokens, 128), 0)
    tlane = lax.broadcasted_iota(jnp.int32, (tokens, 128), 1)
    finder = jnp.where(tlane - 3 * experts == lax.rem(trow, count), 1.0, 0.0).astype(BF16)
    t0 = lax.broadcasted_iota(jnp.int32, (tokens, tokens), 0)
    t1 = lax.broadcasted_iota(jnp.int32, (tokens, tokens), 1)
    mate = jnp.where(t0 // count == t1 // count, dot_t(finder, tab[...]), 0.0)
    q = jnp.where(t0 == t1, 1.0, 0.0) - mate
    summed = lax.fori_loop(1, groups, wait_low, lowp[dp])

    def shuffle(v, high, low_side):
        pieces = [v[:, qrows * i : qrows * (i + 1)] for i in range(nq)]
        return jnp.where(
            up_side == 1,
            jnp.concatenate([pieces[i] for i in high], axis=1),
            jnp.concatenate([pieces[i] for i in low_side], axis=1),
        )

    steady = shuffle(summed[:, 0:tokens], (0, 1, 3, 2), (0, 2, 3, 1))
    lown[:, 0:tokens] = steady[0:8]
    lown[:, 64 : 64 + tokens] = steady[8:16]

    def z_copy(k):
        return pltpu.make_async_remote_copy(
            src_ref=lown, dst_ref=lowz.at[z], send_sem=zsend.at[k], recv_sem=zrecv.at[k],
            device_id=zdev(k), device_id_type=MESH,
        )

    def z_arrival(k):
        source = lax.rem(z - k + zs, zs)
        return pltpu.make_async_remote_copy(
            src_ref=lown, dst_ref=lowz.at[source], send_sem=zsend.at[k], recv_sem=zrecv.at[k],
            device_id={"expert": 2 * source + c}, device_id_type=MESH,
        )

    def start_z(k, carry):
        z_copy(k).start()
        return carry

    def wait_z(k, carry):
        z_arrival(k).wait_recv()
        return carry

    def done_z(k, carry):
        z_copy(k).wait_send()
        return carry

    lax.fori_loop(1, zs, start_z, 0)
    lowz[z] = lown[...]
    zt = jnp.dot(summed[:, 64 : 64 + tokens], q, precision=HIGH, preferred_element_type=F32)
    lax.fori_loop(1, zs, wait_z, 0)

    for rho in range(nq):
        there = pl.ds(qz * lax.rem(a + rho, nq), qz)
        found = lowz[there]
        turn = qrows * rho
        for o in range(2):
            lanes = found[:, :, 64 * o : 64 * o + tokens]
            if turn:
                lanes = jnp.concatenate([lanes[:, :, tokens - turn :], lanes[:, :, : tokens - turn]], axis=2)
            val[there, 8 * o : 8 * o + 8, 0:tokens] = lanes
    values = shuffle(val[...].reshape(wide, 128)[:, 0:tokens], (0, 1, 3, 2), (0, 3, 1, 2)) * w8
    ct[:, 0:tokens] = values
    ct[:, 64 : 64 + tokens] = w8
    here = pl.ds(pl.multiple_of(16 * z, 16), 16)
    mine = ct[here, 0:tokens]
    weight = ct[here, 64 : 64 + tokens]
    inner = jnp.dot(gmat, values, precision=HIGH, preferred_element_type=F32)
    first = weight * (factor * (SCALE * inner - CONTROL * zt))
    second = jnp.dot(mine, q, precision=HIGH, preferred_element_type=F32)
    msgs[:, 0 : 2 * tokens] = jnp.concatenate([first, second], axis=1).astype(BF16)
    msgs[:, 2 * tokens : 2 * tokens + wide] = dot_t(mine, values, precision=HIGH).astype(BF16)

    def m_copy(k):
        return pltpu.make_async_remote_copy(
            src_ref=msgs, dst_ref=met.at[k], send_sem=msend.at[k], recv_sem=mrecv.at[k],
            device_id={"dp": lax.rem(dp + k, groups)}, device_id_type=MESH,
        )

    def start_m(k, carry):
        m_copy(k).start()
        return carry

    def wait_m(k, carry):
        m_copy(k).wait()
        return carry + met[k, :, 2 * tokens : 2 * tokens + wide].astype(F32)

    lax.fori_loop(1, groups, start_m, 0)
    met[0] = msgs[...]
    lax.fori_loop(1, zs, done_z, 0)
    for step in (1, -1):
        for s in range(reach[step]):
            line(step, s).wait_send()
            a_line(step, s).wait_send()
            for sub in range(2):
                ring_copy(step, s, sub).wait_send()
    for k in range(1, qz):
        quad_copy(k).wait_send()

    def done_spread(k, carry):
        spread_copy(k).wait_send()
        return carry

    lax.fori_loop(1, groups, done_spread, 0)
    for copy in started:
        copy.wait_send()
    gram = lax.fori_loop(1, groups, wait_m, msgs[:, 2 * tokens : 2 * tokens + wide].astype(F32))
    for k in range(groups):
        block = met[lax.rem(dp - k + groups, groups), :, 0 : 2 * tokens].astype(F32)
        cot[:, k * tokens : (k + 1) * tokens] = block[:, 0:tokens]
        chat[:, k * tokens : (k + 1) * tokens] = block[:, tokens : 2 * tokens]

    down = SCALE * jnp.dot(cot[...].astype(BF16), hid[...], preferred_element_type=F32)
    along = jnp.dot(
        chat[...].astype(BF16), xall[:, :, :, strip].reshape(groups * tokens, 2 * width),
        preferred_element_type=F32,
    )
    along = jnp.where(lax.rem(dp, 2) == 0, along[:, 0:width], along[:, width : 2 * width])
    slices = aall[...].reshape(wide, aw)
    hi, lo = split(gram)
    through = jnp.dot(hi, slices, preferred_element_type=F32) + jnp.dot(lo, slices, preferred_element_type=F32)
    up = (SCALE * factor) * (SCALE * through[:, 0:width] - CONTROL * along)
    half[:, 0:units] = down[8:16, units : 2 * units]
    half[:, 128 : 128 + width] = up[8:16, :]
    swap = pltpu.make_async_remote_copy(
        src_ref=half, dst_ref=taken, send_sem=csend, recv_sem=crecv,
        device_id={"expert": other}, device_id_type=MESH,
    )
    swap.start()
    swap.wait()
    out_ref[...] = jnp.zeros_like(out_ref)
    out_ref[:, 0:units] = down[0:8, 0:units] + taken[:, 0:units]
    out_ref[:, 128 : 128 + width] = up[0:8, :] + taken[:, 128 : 128 + width]


def part_kernel(both_ref, down_ref, up_ref):
    down_ref[...] = both_ref[:, 0 : down_ref.shape[1]]
    up_ref[...] = both_ref[:, 128 : 128 + up_ref.shape[1]]


def whole(space=pltpu.VMEM):
    return pl.BlockSpec(memory_space=space)


def body(tokens, chosen, router, partner, gate_up, a_down, a_up):
    count, d_model = tokens.shape
    groups = lax.axis_size("dp")
    experts = lax.axis_size("expert")
    zs = experts // 2
    units = gate_up.shape[2]
    width = a_up.shape[2]
    rank = a_up.shape[1]
    gtok = zs * count
    wide = zs * 16
    qz = zs // SIDE
    share = SHARE if d_model == 5120 else d_model // 2
    aw = -(-width // 128) * 128
    mw = 2 * gtok + max(128, wide)
    total = count * groups * experts
    dma = pltpu.SemaphoreType.DMA
    out = pl.pallas_call(
        functools.partial(step_kernel, zs, total, share),
        out_shape=jax.ShapeDtypeStruct((rank, 128 + aw), F32),
        in_specs=[whole()] * 3 + [whole(pltpu.SMEM), whole(pl.ANY)] + [whole()] * 2,
        out_specs=whole(),
        scratch_shapes=[
            pltpu.VMEM((zs, count, d_model - share + 128), BF16),
            pltpu.VMEM((qz, count, d_model), BF16),
            pltpu.VMEM((gtok, d_model), F32),
            pltpu.VMEM((gtok, 128), F32),
            pltpu.VMEM((gtok, d_model), BF16),
            pltpu.VMEM((gtok, 128), BF16),
            pltpu.VMEM((rank, aw + 128), BF16),
            pltpu.VMEM((rank, aw + 128), BF16),
            pltpu.VMEM((16, aw), BF16),
            pltpu.VMEM((16, 2 * width), BF16),
            pltpu.VMEM((zs, 16, aw), BF16),
            pltpu.VMEM((16, 2 * units), BF16),
            pltpu.VMEM((16, wide), BF16),
            pltpu.VMEM((groups, 16, wide), BF16),
            pltpu.VMEM((SIDE, SIDE, gtok, d_model), BF16),
            pltpu.VMEM((2, 2 * units, d_model), BF16),
            pltpu.VMEM((SIDE, SIDE, gtok, 2 * units), F32),
            pltpu.VMEM((SIDE, SIDE, gtok, 2 * units), F32),
            pltpu.VMEM((groups * gtok, 2 * units), BF16),
            pltpu.VMEM((groups, 16, 128), F32),
            pltpu.VMEM((groups, 16, 128), F32),
            pltpu.VMEM((8, 128), F32),
            pltpu.VMEM((zs, 8, 128), F32),
            pltpu.VMEM((zs, 16, 128), F32),
            pltpu.VMEM((wide, 128), F32),
            pltpu.VMEM((16, mw), BF16),
            pltpu.VMEM((groups, 16, mw), BF16),
            pltpu.VMEM((16, groups * gtok), F32),
            pltpu.VMEM((16, groups * gtok), F32),
            pltpu.VMEM((8, 128 + aw), F32),
            pltpu.VMEM((8, 128 + aw), F32),
            dma((120,)), dma((120,)), dma((6,)), dma((2,)), dma((2,)), dma, dma,
            dma((zs,)), dma((zs,)), dma((zs,)), dma((zs,)), dma((qz,)), dma((qz,)),
            dma((groups,)), dma((groups,)), dma((2 * zs,)), dma((2 * zs,)),
            dma((zs,)), dma((zs,)), dma((groups,)), dma((groups,)), dma((groups,)), dma((groups,)),
            dma((zs,)), dma((zs,)), dma((groups,)), dma((groups,)), dma, dma,
        ],
        compiler_params=pltpu.CompilerParams(
            collective_id=0, has_side_effects=True, vmem_limit_bytes=56 << 20
        ),
        name="lorra_step",
    )(tokens, chosen, router, partner, gate_up[0], a_down[0], a_up[0])
    down, up = pl.pallas_call(
        part_kernel,
        out_shape=(
            jax.ShapeDtypeStruct((rank, units), F32),
            jax.ShapeDtypeStruct((rank, width), F32),
        ),
        in_specs=[whole()],
        out_specs=(whole(), whole()),
        name="part",
    )(out)
    return (down[None], up[None])


def solution(mesh):
    placed = (
        P(("dp", "expert"), None),
        P(("dp", "expert"), None),
        P(("dp", "expert"), None),
        P(("dp", "expert")),
        P("expert", None, "dp", None),
        P("expert", None, "dp"),
        P("expert", None, "dp"),
    )
    return jax.shard_map(
        body,
        mesh=mesh,
        in_specs=placed,
        out_specs=(P("expert", None, "dp"), P("expert", None, "dp")),
        check_vma=False,
    )
```

```python
import functools
import math

import jax
import jax.numpy as jnp
from jax import lax
from jax.experimental import pallas as pl
from jax.experimental.pallas import tpu as pltpu
from jax.sharding import PartitionSpec as P

SCALE = 2.0
CONTROL = 0.5
SIDE = 4
SHARE = 1024
HIGH = lax.Precision.HIGHEST
MESH = pl.DeviceIdType.MESH
F32 = jnp.float32
BF16 = jnp.bfloat16


def dot_t(a, b, **kw):
    return lax.dot_general(a, b, (((1,), (1,)), ((), ())), preferred_element_type=F32, **kw)


def split(v):
    hi = v.astype(BF16)
    lo = (v - hi.astype(F32)).astype(BF16)
    return hi, lo


def step_kernel(
    zs, total, share, tok_ref, ids_ref, route_ref, mate_ref, w_ref, adn_ref, aup_ref, out_ref,
    zg, zq, xf, xt, xg, tab, pk, pks, apair, apad, aall, bd, gsend, grecv,
    xall, wbuf, accg, accu, hid, lowp, lowr, lown, lowz, val, ct, msgs, met, cot, chat, half, taken,
    ssem, rsem, lsem, wssem, wrsem, asend, arecv, rsend, rrecv, lsend, lrecv, qsend, qrecv,
    pssend, psrecv, prsend, prrecv,
    azsend, azrecv, gssem, grsem, psend, precv, zsend, zrecv, msend, mrecv, csend, crecv,
):
    count, d_model = tok_ref.shape
    part = d_model - share
    d_half = part // 2
    quarter = d_half // 2
    units = w_ref.shape[1]
    width = aup_ref.shape[1]
    aw = apair.shape[1]
    tokens = zs * count
    experts = 2 * zs
    wide = zs * 16
    factor = 2.0 / math.sqrt(total)
    qz = zq.shape[0]
    nq = zs // qz
    qrows = qz * count
    slice_w = share // qz
    dp = lax.axis_index("dp")
    ex = lax.axis_index("expert")
    y, x = dp // SIDE, lax.rem(dp, SIDE)
    z, c = ex // 2, lax.rem(ex, 2)
    a, b = z // qz, lax.rem(z, qz)
    up_side = (2 * b) // qz
    quads = (a, lax.rem(a + 2 * up_side + 3, nq), lax.rem(a + 5 - 2 * up_side, nq), lax.rem(a + 2, nq))
    other = 2 * z + (1 - c)
    groups = SIDE * SIDE

    barrier = pltpu.get_barrier_semaphore()

    def greet_dp(k, carry):
        pl.semaphore_signal(barrier, inc=1, device_id={"dp": lax.rem(dp + k, groups)}, device_id_type=MESH)
        return carry

    def greet_z(k, carry):
        pl.semaphore_signal(
            barrier, inc=1, device_id={"expert": 2 * lax.rem(z + k, zs) + c}, device_id_type=MESH
        )
        return carry

    lax.fori_loop(1, zs, greet_z, 0)
    pl.semaphore_signal(barrier, inc=1, device_id={"expert": other}, device_id_type=MESH)
    lax.fori_loop(1, groups, greet_dp, 0)

    weights = []
    for g in range(2):
        mine = pltpu.make_async_copy(w_ref.at[g], wbuf.at[g, pl.ds(0, units)], lsem.at[g])
        mine.start()
        weights.append(mine)
    col = lax.broadcasted_iota(jnp.int32, (count, 128), 1)
    row4 = lax.broadcasted_iota(jnp.int32, (count, 128), 0)
    named = lax.rem(col, experts)
    wtab = jnp.zeros((count, 128), F32)
    for k in range(ids_ref.shape[1]):
        place_of = jnp.bitwise_xor(ids_ref[:, k : k + 1], c)
        wtab = wtab + jnp.where(named == place_of, route_ref[:, k : k + 1], 0.0)
    top = wtab.astype(BF16).astype(F32)
    mid = (wtab - top).astype(BF16).astype(F32)
    rest = wtab - top - mid
    pick = jnp.zeros((count, 128), F32)
    for k in range(count):
        pick = jnp.where((row4 == k) & (col - 3 * experts == mate_ref[k]), 1.0, pick)
    packed = jnp.where(
        col < experts, top, jnp.where(col < 2 * experts, mid, jnp.where(col < 3 * experts, rest, pick))
    )
    zq[b] = tok_ref[...]
    zg[z, :, 0:part] = tok_ref[:, 0:part]
    zg[z, :, part : part + 128] = packed.astype(BF16)
    pk[...] = jnp.zeros_like(pk)
    pk[:, 0:width] = aup_ref[...]
    pk[:, aw : aw + units] = adn_ref[...]
    accg[...] = jnp.zeros_like(accg)
    accu[...] = jnp.zeros_like(accu)

    pl.semaphore_wait(barrier, groups + zs - 1)

    def zdev(step):
        return {"expert": 2 * lax.rem(z + step + zs, zs) + c}

    def quad_copy(k):
        return pltpu.make_async_remote_copy(
            src_ref=zq.at[b], dst_ref=zq.at[b], send_sem=qsend.at[k], recv_sem=qrecv.at[k],
            device_id={"expert": 2 * (a * qz + lax.rem(b + k, qz)) + c}, device_id_type=MESH,
        )

    def quad_arrived(k):
        slot = lax.rem(b - k + qz, qz)
        pltpu.make_async_remote_copy(
            src_ref=zq.at[slot], dst_ref=zq.at[slot], send_sem=qsend.at[k], recv_sem=qrecv.at[k],
            device_id={"expert": 2 * (a * qz + slot) + c}, device_id_type=MESH,
        ).wait_recv()

    def line(step, s):
        block = lax.rem(z - step * s + zs, zs)
        return pltpu.make_async_remote_copy(
            src_ref=zg.at[block], dst_ref=zg.at[block],
            send_sem=(rsend if step > 0 else lsend).at[s], recv_sem=(rrecv if step > 0 else lrecv).at[s],
            device_id=zdev(step), device_id_type=MESH,
        )

    def landed(step, s):
        block = lax.rem(z - step * (s + 1) + zs, zs)
        pltpu.make_async_remote_copy(
            src_ref=zg.at[block], dst_ref=zg.at[block],
            send_sem=(rsend if step > 0 else lsend).at[s], recv_sem=(rrecv if step > 0 else lrecv).at[s],
            device_id=zdev(step), device_id_type=MESH,
        ).wait_recv()

    reach = {1: zs // 2, -1: zs - 1 - zs // 2}

    def hop(s):
        for step in (1, -1):
            if 1 <= s <= reach[step]:
                landed(step, s - 1)
            if s < reach[step]:
                line(step, s).start()

    hop(0)
    for k in range(1, qz):
        quad_copy(k).start()
    swap_a = pltpu.make_async_remote_copy(
        src_ref=pk, dst_ref=pks, send_sem=asend, recv_sem=arecv,
        device_id={"expert": other}, device_id_type=MESH,
    )
    swap_a.start()
    for g in range(2):
        theirs = pltpu.make_async_remote_copy(
            src_ref=w_ref.at[g], dst_ref=wbuf.at[g, pl.ds(units, units)],
            send_sem=wssem.at[g], recv_sem=wrsem.at[g],
            device_id={"expert": other}, device_id_type=MESH,
        )
        theirs.start()
        weights.append(theirs)

    def a_line(step, s):
        block = lax.rem(z - step * s + zs, zs)
        return pltpu.make_async_remote_copy(
            src_ref=aall.at[block], dst_ref=aall.at[block],
            send_sem=azsend.at[(0 if step > 0 else zs // 2) + s], recv_sem=azrecv.at[(0 if step > 0 else zs // 2) + s],
            device_id=zdev(step), device_id_type=MESH,
        )

    def a_landed(step, s):
        block = lax.rem(z - step * (s + 1) + zs, zs)
        pltpu.make_async_remote_copy(
            src_ref=aall.at[block], dst_ref=aall.at[block],
            send_sem=azsend.at[(0 if step > 0 else zs // 2) + s], recv_sem=azrecv.at[(0 if step > 0 else zs // 2) + s],
            device_id=zdev(step), device_id_type=MESH,
        ).wait_recv()

    def a_hop(s):
        for step in (1, -1):
            if 1 <= s <= reach[step]:
                a_landed(step, s - 1)
            if s < reach[step]:
                a_line(step, s).start()

    def far(h, first, step):
        along_x = (h == 0) == first
        yy = y if along_x else lax.rem(y + step + SIDE, SIDE)
        xx = lax.rem(x + step + SIDE, SIDE) if along_x else x
        return {"dp": yy * SIDE + xx}

    def place(h, da, db):
        dx, dy = (da, db) if h == 0 else (db, da)
        return lax.rem(y + dy + SIDE, SIDE), lax.rem(x + dx + SIDE, SIDE)

    def cols(h, piece):
        lo = h * d_half
        if piece is None:
            return pl.ds(lo, d_half)
        return pl.ds(lo + piece * quarter, quarter)

    started = []
    span = (pl.ds(0, qrows), pl.ds(qrows, qrows), pl.ds(2 * qrows, 2 * qrows))
    offsets = (0, -1, 1, 2)

    def number(stage, h, phase, j, kind):
        return stage * 40 + h * 20 + (kind if phase == 0 else 4 + 4 * j + kind)

    def send(stage, h, da, db, piece, first, step, at):
        by, bx = place(h, da, db)
        block = xall.at[by, bx, span[stage], cols(h, piece)]
        source = xg.at[span[stage], cols(h, piece)] if da == 0 and db == 0 else block
        copy = pltpu.make_async_remote_copy(
            src_ref=source, dst_ref=block, send_sem=ssem.at[at], recv_sem=rsem.at[at],
            device_id=far(h, first, step), device_id_type=MESH,
        )
        copy.start()
        started.append(copy)

    def arrived(stage, h, da, db, piece, at):
        by, bx = place(h, da, db)
        block = xall.at[by, bx, span[stage], cols(h, piece)]
        pltpu.make_async_remote_copy(
            src_ref=block, dst_ref=block, send_sem=ssem.at[at], recv_sem=rsem.at[at],
            device_id=far(h, True, 1), device_id_type=MESH,
        ).wait_recv()

    def xy_own(stage):
        for phase in (0, 1):
            for h in range(2):
                for kind, step in ((0, 1), (1, -1)):
                    send(stage, h, 0, 0, None, phase == 0, step, number(stage, h, phase, 0, kind))
        copy = pltpu.make_async_copy(
            xg.at[span[stage], pl.ds(0, part)], xall.at[y, x, span[stage], pl.ds(0, part)], lsem.at[2 + stage]
        )
        copy.start()
        return copy

    def xy_near(stage):
        for h in range(2):
            arrived(stage, h, -1, 0, None, number(stage, h, 0, 0, 0))
            send(stage, h, -1, 0, 0, True, 1, number(stage, h, 0, 0, 2))
            arrived(stage, h, 1, 0, None, number(stage, h, 0, 0, 1))
            send(stage, h, 1, 0, 1, True, -1, number(stage, h, 0, 0, 3))
            for j in (1, 2):
                send(stage, h, offsets[j], 0, None, False, 1, number(stage, h, 1, j, 0))
                send(stage, h, offsets[j], 0, None, False, -1, number(stage, h, 1, j, 1))

    def xy_far(stage):
        for h in range(2):
            arrived(stage, h, 2, 0, 0, number(stage, h, 0, 0, 2))
            arrived(stage, h, 2, 0, 1, number(stage, h, 0, 0, 3))
            send(stage, h, 2, 0, None, False, 1, number(stage, h, 1, 3, 0))
            send(stage, h, 2, 0, None, False, -1, number(stage, h, 1, 3, 1))

    def xy_pass(stage, j):
        for h in range(2):
            arrived(stage, h, offsets[j], -1, None, number(stage, h, 1, j, 0))
            send(stage, h, offsets[j], -1, 0, False, 1, number(stage, h, 1, j, 2))
            arrived(stage, h, offsets[j], 1, None, number(stage, h, 1, j, 1))
            send(stage, h, offsets[j], 1, 1, False, -1, number(stage, h, 1, j, 3))

    def xy_last(stage, h):
        for j in range(4):
            arrived(stage, h, offsets[j], 2, 0, number(stage, h, 1, j, 2))
            arrived(stage, h, offsets[j], 2, 1, number(stage, h, 1, j, 3))

    strip_cols = pl.ds(pl.multiple_of(part + b * slice_w, 128), slice_w)

    def spread_copy(k):
        return pltpu.make_async_remote_copy(
            src_ref=xg.at[pl.ds(0, qrows), strip_cols],
            dst_ref=xall.at[y, x, pl.ds(0, qrows), strip_cols],
            send_sem=pssend.at[k], recv_sem=psrecv.at[k],
            device_id={"dp": lax.rem(dp + k, groups)}, device_id_type=MESH,
        )

    def spread_arrived(k):
        source = lax.rem(dp - k + groups, groups)
        block = xall.at[source // SIDE, lax.rem(source, SIDE), pl.ds(0, qrows), strip_cols]
        pltpu.make_async_remote_copy(
            src_ref=block, dst_ref=block, send_sem=pssend.at[k], recv_sem=psrecv.at[k],
            device_id={"dp": source}, device_id_type=MESH,
        ).wait_recv()

    def piece_at(source, holder, sub):
        gap = lax.rem(source // qz - holder // qz + nq, nq)
        side = (2 * lax.rem(holder, qz)) // qz
        odd_gap = lax.rem(gap, 2)
        theirs = (1 - odd_gap) * (gap // 2) * 3 + odd_gap * (2 - side + (gap // 2) * (2 * side - 1))
        return xall.at[
            pl.ds(2 * sub, 2), :, pl.ds(pl.multiple_of(qrows * theirs, qrows), qrows),
            pl.ds(pl.multiple_of(part + lax.rem(source, qz) * slice_w, 128), slice_w),
        ]

    def ring_slot(step, s, sub):
        return (0 if step > 0 else 2 * (zs // 2)) + 2 * s + sub

    def ring_copy(step, s, sub):
        source = lax.rem(z - step * s + zs, zs)
        peer = lax.rem(z + step + zs, zs)
        at = ring_slot(step, s, sub)
        return pltpu.make_async_remote_copy(
            src_ref=piece_at(source, z, sub), dst_ref=piece_at(source, peer, sub),
            send_sem=prsend.at[at], recv_sem=prrecv.at[at], device_id=zdev(step), device_id_type=MESH,
        )

    def ring_landed(step, s, sub):
        source = lax.rem(z - step * (s + 1) + zs, zs)
        at = ring_slot(step, s, sub)
        block = piece_at(source, z, sub)
        pltpu.make_async_remote_copy(
            src_ref=block, dst_ref=block,
            send_sem=prsend.at[at], recv_sem=prrecv.at[at], device_id=zdev(step), device_id_type=MESH,
        ).wait_recv()

    def ring(s):
        for sub in range(2):
            for step in (1, -1):
                if 1 <= s <= reach[step]:
                    ring_landed(step, s - 1, sub)
                if s < reach[step]:
                    ring_copy(step, s, sub).start()

    hop(1)
    for k in range(1, qz):
        quad_arrived(k)
    for k in range(qz):
        xf[count * k : count * (k + 1), :] = zq[k].astype(F32)
    xg[0:qrows, :] = xf[0:qrows, :].astype(BF16)

    def start_spread(k, carry):
        spread_copy(k).start()
        return carry

    def wait_spread(k, carry):
        spread_arrived(k)
        return carry

    lax.fori_loop(1, groups, start_spread, 0)
    mine_q = pltpu.make_async_copy(
        xg.at[pl.ds(0, qrows), strip_cols], xall.at[y, x, pl.ds(0, qrows), strip_cols], lsem.at[5]
    )
    mine_q.start()
    own0 = xy_own(0)
    hop(2)

    swap_a.wait()
    lead, follow = pk[...].astype(F32), pks[...].astype(F32)
    stacked = jnp.concatenate([lead, follow], axis=0)
    apair[...] = stacked[:, 0:aw].astype(BF16)
    aall[z] = stacked[:, 0:aw].astype(BF16)
    spread = jnp.concatenate([stacked[:, 0:width], jnp.zeros((16, width), F32)], axis=1)
    odd = jnp.concatenate([jnp.zeros((16, width), F32), stacked[:, 0:width]], axis=1)
    apad[...] = jnp.where(lax.rem(dp, 2) == 0, spread, odd).astype(BF16)
    blank = jnp.zeros((8, units), F32)
    bd[...] = jnp.concatenate(
        [
            jnp.concatenate([lead[:, aw : aw + units], blank], axis=1),
            jnp.concatenate([blank, follow[:, aw : aw + units]], axis=1),
        ],
        axis=0,
    ).astype(BF16)

    def g_copy(k):
        return pltpu.make_async_remote_copy(
            src_ref=gsend, dst_ref=grecv.at[k], send_sem=gssem.at[k], recv_sem=grsem.at[k],
            device_id={"dp": lax.rem(dp + k, groups)}, device_id_type=MESH,
        )

    def start_g(k, carry):
        g_copy(k).start()
        return carry

    def wait_g(k, carry):
        g_copy(k).wait()
        return carry + grecv[k].astype(F32)

    def bring(r):
        for k in range(qz):
            at = (r * qz + k) * count
            xf[at : at + count, 0:part] = zg[quads[r] * qz + k, :, 0:part].astype(F32)
        rows_r = slice(r * qrows, (r + 1) * qrows)
        xg[rows_r, 0:part] = xf[rows_r, 0:part].astype(BF16)

    def panel(block, at):
        return [dot_t(block, wbuf[g, :, at]) for g in range(2)]

    chunk = d_half
    rows = SIDE * tokens

    def multiply(h, db):
        by, bx = place(h, 0, db)

        def step(i, carry):
            at = pl.ds(pl.multiple_of(h * d_half + i * chunk, 128), chunk)
            if h == 0:
                block = xall[by, :, :, at]
            else:
                block = xall[:, bx, :, at]
            for acc, value in zip((accg, accu), panel(block.reshape(rows, chunk), at)):
                value = value.reshape(SIDE, tokens, 2 * units)
                if h == 0:
                    acc[by] = acc[by] + value
                else:
                    acc[:, bx] = acc[:, bx] + value
            return carry

        lax.fori_loop(0, d_half // chunk, step, 0)

    def multiply_q():
        at = pl.ds(part, share)

        def step(i, carry):
            block = xall[i, :, :, at].reshape(rows, share)
            for acc, value in zip((accg, accu), panel(block, at)):
                acc[i] = acc[i] + value.reshape(SIDE, tokens, 2 * units)
            return carry

        lax.fori_loop(0, SIDE, step, 0)

    a_hop(0)
    hop(3)
    mine_q.wait()
    lax.fori_loop(1, groups, wait_spread, 0)
    ring(0)
    xy_near(0)
    a_hop(1)
    hop(4)
    xy_far(0)
    a_hop(2)
    hop(5)
    bring(1)
    own1 = xy_own(1)
    ring(1)
    xy_pass(0, 0)
    a_hop(3)
    hop(6)
    xy_pass(0, 1)
    ring(2)
    xy_near(1)
    a_hop(4)
    hop(7)
    xy_pass(0, 2)
    ring(3)
    a_hop(5)
    hop(8)
    bring(2)
    bring(3)
    own2 = xy_own(2)
    xy_far(1)
    for r in range(nq):
        for k in range(qz):
            at = (r * qz + k) * count
            xt[at : at + count, :] = zg[quads[r] * qz + k, :, part : part + 128].astype(F32)
    tab[...] = xt[...].astype(BF16)
    xy_pass(0, 3)
    xy_pass(1, 0)
    ring(4)
    a_hop(6)
    xy_near(2)
    xy_pass(1, 1)
    a_hop(7)
    for h in range(2):
        xy_last(0, h)
    xy_far(2)
    a_hop(8)
    ring(5)
    own0.wait()
    own1.wait()
    own2.wait()
    for copy in weights:
        copy.wait()
    xy_pass(1, 2)
    xy_pass(1, 3)
    xy_pass(2, 0)
    ring(6)
    gsend[...] = dot_t(apair[...], aall[...].reshape(wide, aw)).astype(BF16)
    lax.fori_loop(1, groups, start_g, 0)
    multiply(0, 0)
    xy_pass(2, 1)
    ring(7)
    multiply(1, 0)
    xy_pass(2, 2)
    for h in range(2):
        xy_last(1, h)
    xy_pass(2, 3)
    multiply(0, -1)
    multiply(0, 1)
    multiply(1, -1)
    multiply(1, 1)
    ring(8)
    multiply_q()
    gmat = lax.fori_loop(1, groups, wait_g, gsend[...].astype(F32))
    xy_last(2, 0)
    multiply(0, 2)
    xy_last(2, 1)
    multiply(1, 2)
    both = accg.shape[3]
    gate = accg[...].reshape(groups * tokens, both)
    hid[...] = (gate * (1.0 / (1.0 + jnp.exp(-gate))) * accu[...].reshape(groups * tokens, both)).astype(BF16)
    strip = pl.ds(pl.multiple_of(2 * width * (dp // 2), 128), 2 * width)
    low = dot_t(bd[...], hid[...])
    tall = dot_t(apad[...], xall[:, :, :, strip].reshape(groups * tokens, 2 * width))
    for k in range(groups):
        lowp[k, :, 0:tokens] = low[:, k * tokens : (k + 1) * tokens]
        lowp[k, :, 64 : 64 + tokens] = tall[:, k * tokens : (k + 1) * tokens]

    def low_copy(k):
        peer = lax.rem(dp + k, groups)
        return pltpu.make_async_remote_copy(
            src_ref=lowp.at[peer], dst_ref=lowr.at[k], send_sem=psend.at[k], recv_sem=precv.at[k],
            device_id={"dp": peer}, device_id_type=MESH,
        )

    def start_low(k, carry):
        low_copy(k).start()
        return carry

    def wait_low(k, carry):
        low_copy(k).wait()
        return carry + lowr[k]

    lax.fori_loop(1, groups, start_low, 0)
    row = lax.broadcasted_iota(jnp.int32, (wide, 128), 0)
    lane = lax.broadcasted_iota(jnp.int32, (wide, 128), 1)
    chooser = jnp.where((row // 8 == lax.rem(lane, experts)) & (lane < 3 * experts), 1.0, 0.0).astype(BF16)
    w8 = dot_t(chooser, tab[...])
    trow = lax.broadcasted_iota(jnp.int32, (tokens, 128), 0)
    tlane = lax.broadcasted_iota(jnp.int32, (tokens, 128), 1)
    finder = jnp.where(tlane - 3 * experts == lax.rem(trow, count), 1.0, 0.0).astype(BF16)
    t0 = lax.broadcasted_iota(jnp.int32, (tokens, tokens), 0)
    t1 = lax.broadcasted_iota(jnp.int32, (tokens, tokens), 1)
    mate = jnp.where(t0 // count == t1 // count, dot_t(finder, tab[...]), 0.0)
    q = jnp.where(t0 == t1, 1.0, 0.0) - mate
    summed = lax.fori_loop(1, groups, wait_low, lowp[dp])

    def shuffle(v, high, low_side):
        pieces = [v[:, qrows * i : qrows * (i + 1)] for i in range(nq)]
        return jnp.where(
            up_side == 1,
            jnp.concatenate([pieces[i] for i in high], axis=1),
            jnp.concatenate([pieces[i] for i in low_side], axis=1),
        )

    steady = shuffle(summed[:, 0:tokens], (0, 1, 3, 2), (0, 2, 3, 1))
    lown[...] = jnp.concatenate([steady[0:8], steady[8:16]], axis=1).astype(BF16)

    def z_copy(k):
        return pltpu.make_async_remote_copy(
            src_ref=lown, dst_ref=lowz.at[z], send_sem=zsend.at[k], recv_sem=zrecv.at[k],
            device_id=zdev(k), device_id_type=MESH,
        )

    def z_arrival(k):
        source = lax.rem(z - k + zs, zs)
        return pltpu.make_async_remote_copy(
            src_ref=lown, dst_ref=lowz.at[source], send_sem=zsend.at[k], recv_sem=zrecv.at[k],
            device_id={"expert": 2 * source + c}, device_id_type=MESH,
        )

    def start_z(k, carry):
        z_copy(k).start()
        return carry

    def wait_z(k, carry):
        z_arrival(k).wait_recv()
        return carry

    def done_z(k, carry):
        z_copy(k).wait_send()
        return carry

    lax.fori_loop(1, zs, start_z, 0)
    lowz[z] = lown[...]
    zt = jnp.dot(summed[:, 64 : 64 + tokens], q, precision=HIGH, preferred_element_type=F32)
    lax.fori_loop(1, zs, wait_z, 0)

    for rho in range(nq):
        there = pl.ds(qz * lax.rem(a + rho, nq), qz)
        found = lowz[there].astype(F32)
        turn = qrows * rho
        for o in range(2):
            lanes = found[:, :, tokens * o : tokens * (o + 1)]
            if turn:
                lanes = jnp.concatenate([lanes[:, :, tokens - turn :], lanes[:, :, : tokens - turn]], axis=2)
            val[there, 8 * o : 8 * o + 8, 0:tokens] = lanes
    values = shuffle(val[...].reshape(wide, 128)[:, 0:tokens], (0, 1, 3, 2), (0, 3, 1, 2)) * w8
    ct[:, 0:tokens] = values
    ct[:, 64 : 64 + tokens] = w8
    here = pl.ds(pl.multiple_of(16 * z, 16), 16)
    mine = ct[here, 0:tokens]
    weight = ct[here, 64 : 64 + tokens]
    inner = jnp.dot(gmat, values, precision=HIGH, preferred_element_type=F32)
    first = weight * (factor * (SCALE * inner - CONTROL * zt))
    second = jnp.dot(mine, q, precision=HIGH, preferred_element_type=F32)
    msgs[:, 0 : 2 * tokens] = jnp.concatenate([first, second], axis=1).astype(BF16)
    msgs[:, 2 * tokens : 2 * tokens + wide] = dot_t(mine, values, precision=HIGH).astype(BF16)

    def m_copy(k):
        return pltpu.make_async_remote_copy(
            src_ref=msgs, dst_ref=met.at[k], send_sem=msend.at[k], recv_sem=mrecv.at[k],
            device_id={"dp": lax.rem(dp + k, groups)}, device_id_type=MESH,
        )

    def start_m(k, carry):
        m_copy(k).start()
        return carry

    def wait_m(k, carry):
        m_copy(k).wait()
        return carry + met[k, :, 2 * tokens : 2 * tokens + wide].astype(F32)

    lax.fori_loop(1, groups, start_m, 0)
    met[0] = msgs[...]
    lax.fori_loop(1, zs, done_z, 0)
    for step in (1, -1):
        for s in range(reach[step]):
            line(step, s).wait_send()
            a_line(step, s).wait_send()
            for sub in range(2):
                ring_copy(step, s, sub).wait_send()
    for k in range(1, qz):
        quad_copy(k).wait_send()

    def done_spread(k, carry):
        spread_copy(k).wait_send()
        return carry

    lax.fori_loop(1, groups, done_spread, 0)
    for copy in started:
        copy.wait_send()
    gram = lax.fori_loop(1, groups, wait_m, msgs[:, 2 * tokens : 2 * tokens + wide].astype(F32))
    for k in range(groups):
        block = met[lax.rem(dp - k + groups, groups), :, 0 : 2 * tokens].astype(F32)
        cot[:, k * tokens : (k + 1) * tokens] = block[:, 0:tokens]
        chat[:, k * tokens : (k + 1) * tokens] = block[:, tokens : 2 * tokens]

    down = SCALE * jnp.dot(cot[...].astype(BF16), hid[...], preferred_element_type=F32)
    along = jnp.dot(
        chat[...].astype(BF16), xall[:, :, :, strip].reshape(groups * tokens, 2 * width),
        preferred_element_type=F32,
    )
    along = jnp.where(lax.rem(dp, 2) == 0, along[:, 0:width], along[:, width : 2 * width])
    slices = aall[...].reshape(wide, aw)
    hi, lo = split(gram)
    through = jnp.dot(hi, slices, preferred_element_type=F32) + jnp.dot(lo, slices, preferred_element_type=F32)
    up = (SCALE * factor) * (SCALE * through[:, 0:width] - CONTROL * along)
    half[:, 0:units] = down[8:16, units : 2 * units]
    half[:, 128 : 128 + width] = up[8:16, :]
    swap = pltpu.make_async_remote_copy(
        src_ref=half, dst_ref=taken, send_sem=csend, recv_sem=crecv,
        device_id={"expert": other}, device_id_type=MESH,
    )
    swap.start()
    swap.wait()
    out_ref[...] = jnp.zeros_like(out_ref)
    out_ref[:, 0:units] = down[0:8, 0:units] + taken[:, 0:units]
    out_ref[:, 128 : 128 + width] = up[0:8, :] + taken[:, 128 : 128 + width]


def part_kernel(both_ref, down_ref, up_ref):
    down_ref[...] = both_ref[:, 0 : down_ref.shape[1]]
    up_ref[...] = both_ref[:, 128 : 128 + up_ref.shape[1]]


def whole(space=pltpu.VMEM):
    return pl.BlockSpec(memory_space=space)


def body(tokens, chosen, router, partner, gate_up, a_down, a_up):
    count, d_model = tokens.shape
    groups = lax.axis_size("dp")
    experts = lax.axis_size("expert")
    zs = experts // 2
    units = gate_up.shape[2]
    width = a_up.shape[2]
    rank = a_up.shape[1]
    gtok = zs * count
    wide = zs * 16
    qz = zs // SIDE
    share = SHARE if d_model == 5120 else d_model // 2
    aw = -(-width // 128) * 128
    mw = 2 * gtok + max(128, wide)
    total = count * groups * experts
    dma = pltpu.SemaphoreType.DMA
    out = pl.pallas_call(
        functools.partial(step_kernel, zs, total, share),
        out_shape=jax.ShapeDtypeStruct((rank, 128 + aw), F32),
        in_specs=[whole()] * 3 + [whole(pltpu.SMEM), whole(pl.ANY)] + [whole()] * 2,
        out_specs=whole(),
        scratch_shapes=[
            pltpu.VMEM((zs, count, d_model - share + 128), BF16),
            pltpu.VMEM((qz, count, d_model), BF16),
            pltpu.VMEM((gtok, d_model), F32),
            pltpu.VMEM((gtok, 128), F32),
            pltpu.VMEM((gtok, d_model), BF16),
            pltpu.VMEM((gtok, 128), BF16),
            pltpu.VMEM((rank, aw + 128), BF16),
            pltpu.VMEM((rank, aw + 128), BF16),
            pltpu.VMEM((16, aw), BF16),
            pltpu.VMEM((16, 2 * width), BF16),
            pltpu.VMEM((zs, 16, aw), BF16),
            pltpu.VMEM((16, 2 * units), BF16),
            pltpu.VMEM((16, wide), BF16),
            pltpu.VMEM((groups, 16, wide), BF16),
            pltpu.VMEM((SIDE, SIDE, gtok, d_model), BF16),
            pltpu.VMEM((2, 2 * units, d_model), BF16),
            pltpu.VMEM((SIDE, SIDE, gtok, 2 * units), F32),
            pltpu.VMEM((SIDE, SIDE, gtok, 2 * units), F32),
            pltpu.VMEM((groups * gtok, 2 * units), BF16),
            pltpu.VMEM((groups, 16, 128), F32),
            pltpu.VMEM((groups, 16, 128), F32),
            pltpu.VMEM((8, 2 * gtok), BF16),
            pltpu.VMEM((zs, 8, 2 * gtok), BF16),
            pltpu.VMEM((zs, 16, 128), F32),
            pltpu.VMEM((wide, 128), F32),
            pltpu.VMEM((16, mw), BF16),
            pltpu.VMEM((groups, 16, mw), BF16),
            pltpu.VMEM((16, groups * gtok), F32),
            pltpu.VMEM((16, groups * gtok), F32),
            pltpu.VMEM((8, 128 + aw), F32),
            pltpu.VMEM((8, 128 + aw), F32),
            dma((120,)), dma((120,)), dma((6,)), dma((2,)), dma((2,)), dma, dma,
            dma((zs,)), dma((zs,)), dma((zs,)), dma((zs,)), dma((qz,)), dma((qz,)),
            dma((groups,)), dma((groups,)), dma((2 * zs,)), dma((2 * zs,)),
            dma((zs,)), dma((zs,)), dma((groups,)), dma((groups,)), dma((groups,)), dma((groups,)),
            dma((zs,)), dma((zs,)), dma((groups,)), dma((groups,)), dma, dma,
        ],
        compiler_params=pltpu.CompilerParams(
            collective_id=0, has_side_effects=True, vmem_limit_bytes=56 << 20
        ),
        name="lorra_step",
    )(tokens, chosen, router, partner, gate_up[0], a_down[0], a_up[0])
    down, up = pl.pallas_call(
        part_kernel,
        out_shape=(
            jax.ShapeDtypeStruct((rank, units), F32),
            jax.ShapeDtypeStruct((rank, width), F32),
        ),
        in_specs=[whole()],
        out_specs=(whole(), whole()),
        name="part",
    )(out)
    return (down[None], up[None])


def solution(mesh):
    placed = (
        P(("dp", "expert"), None),
        P(("dp", "expert"), None),
        P(("dp", "expert"), None),
        P(("dp", "expert")),
        P("expert", None, "dp", None),
        P("expert", None, "dp"),
        P("expert", None, "dp"),
    )
    return jax.shard_map(
        body,
        mesh=mesh,
        in_specs=placed,
        out_specs=(P("expert", None, "dp"), P("expert", None, "dp")),
        check_vma=False,
    )
```

```python
import functools
import math

import jax
import jax.numpy as jnp
from jax import lax
from jax.experimental import pallas as pl
from jax.experimental.pallas import tpu as pltpu
from jax.sharding import PartitionSpec as P

SCALE = 2.0
CONTROL = 0.5
SIDE = 4
SHARE = 1024
HIGH = lax.Precision.HIGHEST
MESH = pl.DeviceIdType.MESH
F32 = jnp.float32
BF16 = jnp.bfloat16


def dot_t(a, b, **kw):
    return lax.dot_general(a, b, (((1,), (1,)), ((), ())), preferred_element_type=F32, **kw)


def split(v):
    hi = v.astype(BF16)
    lo = (v - hi.astype(F32)).astype(BF16)
    return hi, lo


def step_kernel(
    zs, total, share, tok_ref, ids_ref, route_ref, mate_ref, w_ref, adn_ref, aup_ref, out_ref,
    zg, zq, xf, xt, xg, tab, pk, pks, apair, apad, aall, bd, gsend, grecv,
    xall, wbuf, accg, accu, hid, lowp, lowr, lown, lowz, val, ct, msgs, met, cot, chat, hsend, hgot, xgot, flipped,
    ssem, rsem, lsem, wssem, wrsem, asend, arecv, rsend, rrecv, lsend, lrecv, qsend, qrecv,
    pssend, psrecv, prsend, prrecv,
    azsend, azrecv, gssem, grsem, psend, precv, zsend, zrecv, msend, mrecv, csend, crecv, xsend, xrecv,
):
    count, d_model = tok_ref.shape
    part = d_model - share
    d_half = part // 2
    quarter = d_half // 2
    units = w_ref.shape[1]
    width = aup_ref.shape[1]
    aw = apair.shape[1]
    tokens = zs * count
    experts = 2 * zs
    wide = zs * 16
    factor = 2.0 / math.sqrt(total)
    qz = zq.shape[0]
    nq = zs // qz
    qrows = qz * count
    slice_w = share // qz
    dp = lax.axis_index("dp")
    ex = lax.axis_index("expert")
    y, x = dp // SIDE, lax.rem(dp, SIDE)
    z, c = ex // 2, lax.rem(ex, 2)
    a, b = z // qz, lax.rem(z, qz)
    up_side = (2 * b) // qz
    quads = (a, lax.rem(a + 2 * up_side + 3, nq), lax.rem(a + 5 - 2 * up_side, nq), lax.rem(a + 2, nq))
    other = 2 * z + (1 - c)
    groups = SIDE * SIDE

    barrier = pltpu.get_barrier_semaphore()

    def greet_dp(k, carry):
        pl.semaphore_signal(barrier, inc=1, device_id={"dp": lax.rem(dp + k, groups)}, device_id_type=MESH)
        return carry

    def greet_z(k, carry):
        pl.semaphore_signal(
            barrier, inc=1, device_id={"expert": 2 * lax.rem(z + k, zs) + c}, device_id_type=MESH
        )
        return carry

    lax.fori_loop(1, zs, greet_z, 0)
    def greet_across(k, carry):
        pl.semaphore_signal(
            barrier, inc=1, device_id={"dp": lax.rem(dp + k, groups), "expert": other}, device_id_type=MESH
        )
        return carry

    lax.fori_loop(0, groups, greet_across, 0)
    lax.fori_loop(1, groups, greet_dp, 0)

    weights = []
    for g in range(2):
        mine = pltpu.make_async_copy(w_ref.at[g], wbuf.at[g, pl.ds(0, units)], lsem.at[g])
        mine.start()
        weights.append(mine)
    col = lax.broadcasted_iota(jnp.int32, (count, 128), 1)
    row4 = lax.broadcasted_iota(jnp.int32, (count, 128), 0)
    named = lax.rem(col, experts)
    wtab = jnp.zeros((count, 128), F32)
    for k in range(ids_ref.shape[1]):
        place_of = jnp.bitwise_xor(ids_ref[:, k : k + 1], c)
        wtab = wtab + jnp.where(named == place_of, route_ref[:, k : k + 1], 0.0)
    top = wtab.astype(BF16).astype(F32)
    mid = (wtab - top).astype(BF16).astype(F32)
    rest = wtab - top - mid
    pick = jnp.zeros((count, 128), F32)
    for k in range(count):
        pick = jnp.where((row4 == k) & (col - 3 * experts == mate_ref[k]), 1.0, pick)
    packed = jnp.where(
        col < experts, top, jnp.where(col < 2 * experts, mid, jnp.where(col < 3 * experts, rest, pick))
    )
    zq[b] = tok_ref[...]
    zg[z, :, 0:part] = tok_ref[:, 0:part]
    zg[z, :, part : part + 128] = packed.astype(BF16)
    pk[...] = jnp.zeros_like(pk)
    pk[:, 0:width] = aup_ref[...]
    pk[:, aw : aw + units] = adn_ref[...]
    accg[...] = jnp.zeros_like(accg)
    accu[...] = jnp.zeros_like(accu)

    pl.semaphore_wait(barrier, 2 * groups + zs - 2)

    def zdev(step):
        return {"expert": 2 * lax.rem(z + step + zs, zs) + c}

    def quad_copy(k):
        return pltpu.make_async_remote_copy(
            src_ref=zq.at[b], dst_ref=zq.at[b], send_sem=qsend.at[k], recv_sem=qrecv.at[k],
            device_id={"expert": 2 * (a * qz + lax.rem(b + k, qz)) + c}, device_id_type=MESH,
        )

    def quad_arrived(k):
        slot = lax.rem(b - k + qz, qz)
        pltpu.make_async_remote_copy(
            src_ref=zq.at[slot], dst_ref=zq.at[slot], send_sem=qsend.at[k], recv_sem=qrecv.at[k],
            device_id={"expert": 2 * (a * qz + slot) + c}, device_id_type=MESH,
        ).wait_recv()

    def line(step, s):
        block = lax.rem(z - step * s + zs, zs)
        return pltpu.make_async_remote_copy(
            src_ref=zg.at[block], dst_ref=zg.at[block],
            send_sem=(rsend if step > 0 else lsend).at[s], recv_sem=(rrecv if step > 0 else lrecv).at[s],
            device_id=zdev(step), device_id_type=MESH,
        )

    def landed(step, s):
        block = lax.rem(z - step * (s + 1) + zs, zs)
        pltpu.make_async_remote_copy(
            src_ref=zg.at[block], dst_ref=zg.at[block],
            send_sem=(rsend if step > 0 else lsend).at[s], recv_sem=(rrecv if step > 0 else lrecv).at[s],
            device_id=zdev(step), device_id_type=MESH,
        ).wait_recv()

    reach = {1: zs // 2, -1: zs - 1 - zs // 2}

    def hop(s):
        for step in (1, -1):
            if 1 <= s <= reach[step]:
                landed(step, s - 1)
            if s < reach[step]:
                line(step, s).start()

    hop(0)
    for k in range(1, qz):
        quad_copy(k).start()
    swap_a = pltpu.make_async_remote_copy(
        src_ref=pk, dst_ref=pks, send_sem=asend, recv_sem=arecv,
        device_id={"expert": other}, device_id_type=MESH,
    )
    swap_a.start()
    for g in range(2):
        theirs = pltpu.make_async_remote_copy(
            src_ref=w_ref.at[g], dst_ref=wbuf.at[g, pl.ds(units, units)],
            send_sem=wssem.at[g], recv_sem=wrsem.at[g],
            device_id={"expert": other}, device_id_type=MESH,
        )
        theirs.start()
        weights.append(theirs)

    def a_line(step, s):
        block = lax.rem(z - step * s + zs, zs)
        return pltpu.make_async_remote_copy(
            src_ref=aall.at[block], dst_ref=aall.at[block],
            send_sem=azsend.at[(0 if step > 0 else zs // 2) + s], recv_sem=azrecv.at[(0 if step > 0 else zs // 2) + s],
            device_id=zdev(step), device_id_type=MESH,
        )

    def a_landed(step, s):
        block = lax.rem(z - step * (s + 1) + zs, zs)
        pltpu.make_async_remote_copy(
            src_ref=aall.at[block], dst_ref=aall.at[block],
            send_sem=azsend.at[(0 if step > 0 else zs // 2) + s], recv_sem=azrecv.at[(0 if step > 0 else zs // 2) + s],
            device_id=zdev(step), device_id_type=MESH,
        ).wait_recv()

    def a_hop(s):
        for step in (1, -1):
            if 1 <= s <= reach[step]:
                a_landed(step, s - 1)
            if s < reach[step]:
                a_line(step, s).start()

    def far(h, first, step):
        along_x = (h == 0) == first
        yy = y if along_x else lax.rem(y + step + SIDE, SIDE)
        xx = lax.rem(x + step + SIDE, SIDE) if along_x else x
        return {"dp": yy * SIDE + xx}

    def place(h, da, db):
        dx, dy = (da, db) if h == 0 else (db, da)
        return lax.rem(y + dy + SIDE, SIDE), lax.rem(x + dx + SIDE, SIDE)

    def cols(h, piece):
        lo = h * d_half
        if piece is None:
            return pl.ds(lo, d_half)
        return pl.ds(lo + piece * quarter, quarter)

    started = []
    span = (pl.ds(0, qrows), pl.ds(qrows, qrows), pl.ds(2 * qrows, 2 * qrows))
    offsets = (0, -1, 1, 2)

    def number(stage, h, phase, j, kind):
        return stage * 40 + h * 20 + (kind if phase == 0 else 4 + 4 * j + kind)

    def send(stage, h, da, db, piece, first, step, at):
        by, bx = place(h, da, db)
        block = xall.at[by, bx, span[stage], cols(h, piece)]
        source = xg.at[span[stage], cols(h, piece)] if da == 0 and db == 0 else block
        copy = pltpu.make_async_remote_copy(
            src_ref=source, dst_ref=block, send_sem=ssem.at[at], recv_sem=rsem.at[at],
            device_id=far(h, first, step), device_id_type=MESH,
        )
        copy.start()
        started.append(copy)

    def arrived(stage, h, da, db, piece, at):
        by, bx = place(h, da, db)
        block = xall.at[by, bx, span[stage], cols(h, piece)]
        pltpu.make_async_remote_copy(
            src_ref=block, dst_ref=block, send_sem=ssem.at[at], recv_sem=rsem.at[at],
            device_id=far(h, True, 1), device_id_type=MESH,
        ).wait_recv()

    def xy_own(stage):
        for phase in (0, 1):
            for h in range(2):
                for kind, step in ((0, 1), (1, -1)):
                    send(stage, h, 0, 0, None, phase == 0, step, number(stage, h, phase, 0, kind))
        copy = pltpu.make_async_copy(
            xg.at[span[stage], pl.ds(0, part)], xall.at[y, x, span[stage], pl.ds(0, part)], lsem.at[2 + stage]
        )
        copy.start()
        return copy

    def xy_near(stage):
        for h in range(2):
            arrived(stage, h, -1, 0, None, number(stage, h, 0, 0, 0))
            send(stage, h, -1, 0, 0, True, 1, number(stage, h, 0, 0, 2))
            arrived(stage, h, 1, 0, None, number(stage, h, 0, 0, 1))
            send(stage, h, 1, 0, 1, True, -1, number(stage, h, 0, 0, 3))
            for j in (1, 2):
                send(stage, h, offsets[j], 0, None, False, 1, number(stage, h, 1, j, 0))
                send(stage, h, offsets[j], 0, None, False, -1, number(stage, h, 1, j, 1))

    def xy_far(stage):
        for h in range(2):
            arrived(stage, h, 2, 0, 0, number(stage, h, 0, 0, 2))
            arrived(stage, h, 2, 0, 1, number(stage, h, 0, 0, 3))
            send(stage, h, 2, 0, None, False, 1, number(stage, h, 1, 3, 0))
            send(stage, h, 2, 0, None, False, -1, number(stage, h, 1, 3, 1))

    def xy_pass(stage, j):
        for h in range(2):
            arrived(stage, h, offsets[j], -1, None, number(stage, h, 1, j, 0))
            send(stage, h, offsets[j], -1, 0, False, 1, number(stage, h, 1, j, 2))
            arrived(stage, h, offsets[j], 1, None, number(stage, h, 1, j, 1))
            send(stage, h, offsets[j], 1, 1, False, -1, number(stage, h, 1, j, 3))

    def xy_last(stage, h):
        for j in range(4):
            arrived(stage, h, offsets[j], 2, 0, number(stage, h, 1, j, 2))
            arrived(stage, h, offsets[j], 2, 1, number(stage, h, 1, j, 3))

    strip_cols = pl.ds(pl.multiple_of(part + b * slice_w, 128), slice_w)

    def spread_copy(k):
        return pltpu.make_async_remote_copy(
            src_ref=xg.at[pl.ds(0, qrows), strip_cols],
            dst_ref=xall.at[y, x, pl.ds(0, qrows), strip_cols],
            send_sem=pssend.at[k], recv_sem=psrecv.at[k],
            device_id={"dp": lax.rem(dp + k, groups)}, device_id_type=MESH,
        )

    def spread_arrived(k):
        source = lax.rem(dp - k + groups, groups)
        block = xall.at[source // SIDE, lax.rem(source, SIDE), pl.ds(0, qrows), strip_cols]
        pltpu.make_async_remote_copy(
            src_ref=block, dst_ref=block, send_sem=pssend.at[k], recv_sem=psrecv.at[k],
            device_id={"dp": source}, device_id_type=MESH,
        ).wait_recv()

    def piece_at(source, holder, sub):
        gap = lax.rem(source // qz - holder // qz + nq, nq)
        side = (2 * lax.rem(holder, qz)) // qz
        odd_gap = lax.rem(gap, 2)
        theirs = (1 - odd_gap) * (gap // 2) * 3 + odd_gap * (2 - side + (gap // 2) * (2 * side - 1))
        return xall.at[
            pl.ds(2 * sub, 2), :, pl.ds(pl.multiple_of(qrows * theirs, qrows), qrows),
            pl.ds(pl.multiple_of(part + lax.rem(source, qz) * slice_w, 128), slice_w),
        ]

    def ring_slot(step, s, sub):
        return (0 if step > 0 else 2 * (zs // 2)) + 2 * s + sub

    def ring_copy(step, s, sub):
        source = lax.rem(z - step * s + zs, zs)
        peer = lax.rem(z + step + zs, zs)
        at = ring_slot(step, s, sub)
        return pltpu.make_async_remote_copy(
            src_ref=piece_at(source, z, sub), dst_ref=piece_at(source, peer, sub),
            send_sem=prsend.at[at], recv_sem=prrecv.at[at], device_id=zdev(step), device_id_type=MESH,
        )

    def ring_landed(step, s, sub):
        source = lax.rem(z - step * (s + 1) + zs, zs)
        at = ring_slot(step, s, sub)
        block = piece_at(source, z, sub)
        pltpu.make_async_remote_copy(
            src_ref=block, dst_ref=block,
            send_sem=prsend.at[at], recv_sem=prrecv.at[at], device_id=zdev(step), device_id_type=MESH,
        ).wait_recv()

    def ring(s):
        for sub in range(2):
            for step in (1, -1):
                if 1 <= s <= reach[step]:
                    ring_landed(step, s - 1, sub)
                if s < reach[step]:
                    ring_copy(step, s, sub).start()

    hop(1)
    for k in range(1, qz):
        quad_arrived(k)
    for k in range(qz):
        xf[count * k : count * (k + 1), :] = zq[k].astype(F32)
    xg[0:qrows, :] = xf[0:qrows, :].astype(BF16)

    def start_spread(k, carry):
        spread_copy(k).start()
        return carry

    def wait_spread(k, carry):
        spread_arrived(k)
        return carry

    lax.fori_loop(1, groups, start_spread, 0)
    mine_q = pltpu.make_async_copy(
        xg.at[pl.ds(0, qrows), strip_cols], xall.at[y, x, pl.ds(0, qrows), strip_cols], lsem.at[5]
    )
    mine_q.start()
    own0 = xy_own(0)
    hop(2)

    swap_a.wait()
    lead, follow = pk[...].astype(F32), pks[...].astype(F32)
    stacked = jnp.concatenate([lead, follow], axis=0)
    apair[...] = stacked[:, 0:aw].astype(BF16)
    aall[z] = stacked[:, 0:aw].astype(BF16)
    spread = jnp.concatenate([stacked[:, 0:width], jnp.zeros((16, width), F32)], axis=1)
    odd = jnp.concatenate([jnp.zeros((16, width), F32), stacked[:, 0:width]], axis=1)
    apad[...] = jnp.where(lax.rem(dp, 2) == 0, spread, odd).astype(BF16)
    blank = jnp.zeros((8, units), F32)
    bd[...] = jnp.concatenate(
        [
            jnp.concatenate([lead[:, aw : aw + units], blank], axis=1),
            jnp.concatenate([blank, follow[:, aw : aw + units]], axis=1),
        ],
        axis=0,
    ).astype(BF16)

    def g_copy(k):
        return pltpu.make_async_remote_copy(
            src_ref=gsend, dst_ref=grecv.at[k], send_sem=gssem.at[k], recv_sem=grsem.at[k],
            device_id={"dp": lax.rem(dp + k, groups)}, device_id_type=MESH,
        )

    def start_g(k, carry):
        g_copy(k).start()
        return carry

    def wait_g(k, carry):
        g_copy(k).wait()
        return carry + grecv[k].astype(F32)

    def bring(r):
        for k in range(qz):
            at = (r * qz + k) * count
            xf[at : at + count, 0:part] = zg[quads[r] * qz + k, :, 0:part].astype(F32)
        rows_r = slice(r * qrows, (r + 1) * qrows)
        xg[rows_r, 0:part] = xf[rows_r, 0:part].astype(BF16)

    def panel(block, at):
        return [dot_t(block, wbuf[g, :, at]) for g in range(2)]

    chunk = d_half
    rows = SIDE * tokens

    def multiply(h, db):
        by, bx = place(h, 0, db)

        def step(i, carry):
            at = pl.ds(pl.multiple_of(h * d_half + i * chunk, 128), chunk)
            if h == 0:
                block = xall[by, :, :, at]
            else:
                block = xall[:, bx, :, at]
            for acc, value in zip((accg, accu), panel(block.reshape(rows, chunk), at)):
                value = value.reshape(SIDE, tokens, 2 * units)
                if h == 0:
                    acc[by] = acc[by] + value
                else:
                    acc[:, bx] = acc[:, bx] + value
            return carry

        lax.fori_loop(0, d_half // chunk, step, 0)

    def multiply_q():
        at = pl.ds(part, share)

        def step(i, carry):
            block = xall[i, :, :, at].reshape(rows, share)
            for acc, value in zip((accg, accu), panel(block, at)):
                acc[i] = acc[i] + value.reshape(SIDE, tokens, 2 * units)
            return carry

        lax.fori_loop(0, SIDE, step, 0)

    a_hop(0)
    hop(3)
    mine_q.wait()
    lax.fori_loop(1, groups, wait_spread, 0)
    ring(0)
    xy_near(0)
    a_hop(1)
    hop(4)
    xy_far(0)
    a_hop(2)
    hop(5)
    bring(1)
    own1 = xy_own(1)
    ring(1)
    xy_pass(0, 0)
    a_hop(3)
    hop(6)
    xy_pass(0, 1)
    ring(2)
    xy_near(1)
    a_hop(4)
    hop(7)
    xy_pass(0, 2)
    ring(3)
    a_hop(5)
    hop(8)
    bring(2)
    bring(3)
    own2 = xy_own(2)
    xy_far(1)
    for r in range(nq):
        for k in range(qz):
            at = (r * qz + k) * count
            xt[at : at + count, :] = zg[quads[r] * qz + k, :, part : part + 128].astype(F32)
    tab[...] = xt[...].astype(BF16)
    xy_pass(0, 3)
    xy_pass(1, 0)
    ring(4)
    a_hop(6)
    xy_near(2)
    xy_pass(1, 1)
    a_hop(7)
    for h in range(2):
        xy_last(0, h)
    xy_far(2)
    a_hop(8)
    ring(5)
    own0.wait()
    own1.wait()
    own2.wait()
    for copy in weights:
        copy.wait()
    xy_pass(1, 2)
    xy_pass(1, 3)
    xy_pass(2, 0)
    ring(6)
    gsend[...] = dot_t(apair[...], aall[...].reshape(wide, aw)).astype(BF16)
    lax.fori_loop(1, groups, start_g, 0)
    multiply(0, 0)
    xy_pass(2, 1)
    ring(7)
    multiply(1, 0)
    xy_pass(2, 2)
    for h in range(2):
        xy_last(1, h)
    xy_pass(2, 3)
    multiply(0, -1)
    multiply(0, 1)
    multiply(1, -1)
    multiply(1, 1)
    ring(8)
    multiply_q()
    gmat = lax.fori_loop(1, groups, wait_g, gsend[...].astype(F32))
    xy_last(2, 0)
    multiply(0, 2)
    xy_last(2, 1)
    multiply(1, 2)
    strip = pl.ds(pl.multiple_of(2 * width * (dp // 2), 128), 2 * width)
    x_over = pltpu.make_async_remote_copy(
        src_ref=xall.at[:, :, :, strip], dst_ref=xgot, send_sem=xsend, recv_sem=xrecv,
        device_id={"expert": other}, device_id_type=MESH,
    )
    x_over.start()
    both = accg.shape[3]
    gate = accg[...].reshape(groups * tokens, both)
    hid[...] = (gate * (1.0 / (1.0 + jnp.exp(-gate))) * accu[...].reshape(groups * tokens, both)).astype(BF16)
    low = dot_t(bd[...], hid[...])
    tall = dot_t(apad[...], xall[:, :, :, strip].reshape(groups * tokens, 2 * width))
    for k in range(groups):
        lowp[k, :, 0:tokens] = low[:, k * tokens : (k + 1) * tokens]
        lowp[k, :, 64 : 64 + tokens] = tall[:, k * tokens : (k + 1) * tokens]

    def low_copy(k):
        peer = lax.rem(dp + k, groups)
        return pltpu.make_async_remote_copy(
            src_ref=lowp.at[peer], dst_ref=lowr.at[k], send_sem=psend.at[k], recv_sem=precv.at[k],
            device_id={"dp": peer}, device_id_type=MESH,
        )

    def start_low(k, carry):
        low_copy(k).start()
        return carry

    def wait_low(k, carry):
        low_copy(k).wait()
        return carry + lowr[k]

    lax.fori_loop(1, groups, start_low, 0)
    hsend[:, 0:units] = hid[:, units : 2 * units]
    h_over = pltpu.make_async_remote_copy(
        src_ref=hsend, dst_ref=hgot, send_sem=csend, recv_sem=crecv,
        device_id={"expert": other}, device_id_type=MESH,
    )
    h_over.start()
    slabs = aall[...].astype(F32)
    flipped[...] = jnp.concatenate([slabs[:, 8:16], slabs[:, 0:8]], axis=1).astype(BF16)
    row = lax.broadcasted_iota(jnp.int32, (wide, 128), 0)
    lane = lax.broadcasted_iota(jnp.int32, (wide, 128), 1)
    chooser = jnp.where((row // 8 == lax.rem(lane, experts)) & (lane < 3 * experts), 1.0, 0.0).astype(BF16)
    w8 = dot_t(chooser, tab[...])
    trow = lax.broadcasted_iota(jnp.int32, (tokens, 128), 0)
    tlane = lax.broadcasted_iota(jnp.int32, (tokens, 128), 1)
    finder = jnp.where(tlane - 3 * experts == lax.rem(trow, count), 1.0, 0.0).astype(BF16)
    t0 = lax.broadcasted_iota(jnp.int32, (tokens, tokens), 0)
    t1 = lax.broadcasted_iota(jnp.int32, (tokens, tokens), 1)
    mate = jnp.where(t0 // count == t1 // count, dot_t(finder, tab[...]), 0.0)
    q = jnp.where(t0 == t1, 1.0, 0.0) - mate
    summed = lax.fori_loop(1, groups, wait_low, lowp[dp])

    def shuffle(v, high, low_side):
        pieces = [v[:, qrows * i : qrows * (i + 1)] for i in range(nq)]
        return jnp.where(
            up_side == 1,
            jnp.concatenate([pieces[i] for i in high], axis=1),
            jnp.concatenate([pieces[i] for i in low_side], axis=1),
        )

    steady = shuffle(summed[:, 0:tokens], (0, 1, 3, 2), (0, 2, 3, 1))
    lown[...] = jnp.concatenate([steady[0:8], steady[8:16]], axis=1).astype(BF16)

    def z_copy(k):
        return pltpu.make_async_remote_copy(
            src_ref=lown, dst_ref=lowz.at[z], send_sem=zsend.at[k], recv_sem=zrecv.at[k],
            device_id=zdev(k), device_id_type=MESH,
        )

    def z_arrival(k):
        source = lax.rem(z - k + zs, zs)
        return pltpu.make_async_remote_copy(
            src_ref=lown, dst_ref=lowz.at[source], send_sem=zsend.at[k], recv_sem=zrecv.at[k],
            device_id={"expert": 2 * source + c}, device_id_type=MESH,
        )

    def start_z(k, carry):
        z_copy(k).start()
        return carry

    def wait_z(k, carry):
        z_arrival(k).wait_recv()
        return carry

    def done_z(k, carry):
        z_copy(k).wait_send()
        return carry

    lax.fori_loop(1, zs, start_z, 0)
    lowz[z] = lown[...]
    zt = jnp.dot(summed[:, 64 : 64 + tokens], q, precision=HIGH, preferred_element_type=F32)
    lax.fori_loop(1, zs, wait_z, 0)

    for rho in range(nq):
        there = pl.ds(qz * lax.rem(a + rho, nq), qz)
        found = lowz[there].astype(F32)
        turn = qrows * rho
        for o in range(2):
            lanes = found[:, :, tokens * o : tokens * (o + 1)]
            if turn:
                lanes = jnp.concatenate([lanes[:, :, tokens - turn :], lanes[:, :, : tokens - turn]], axis=2)
            val[there, 8 * o : 8 * o + 8, 0:tokens] = lanes
    values = shuffle(val[...].reshape(wide, 128)[:, 0:tokens], (0, 1, 3, 2), (0, 3, 1, 2)) * w8
    ct[:, 0:tokens] = values
    ct[:, 64 : 64 + tokens] = w8
    here = pl.ds(pl.multiple_of(16 * z, 16), 16)
    mine = ct[here, 0:tokens]
    weight = ct[here, 64 : 64 + tokens]
    inner = jnp.dot(gmat, values, precision=HIGH, preferred_element_type=F32)
    first = weight * (factor * (SCALE * inner - CONTROL * zt))
    second = jnp.dot(mine, q, precision=HIGH, preferred_element_type=F32)
    third = dot_t(mine, values, precision=HIGH)
    for o in range(2):
        part_of = slice(8 * o, 8 * o + 8)
        msgs[o, :, 0 : 2 * tokens] = jnp.concatenate([first[part_of], second[part_of]], axis=1).astype(BF16)
        msgs[o, :, 2 * tokens : 2 * tokens + wide] = third[part_of].astype(BF16)

    def m_copy(o, k):
        peer = lax.rem(dp + k, groups)
        return pltpu.make_async_remote_copy(
            src_ref=msgs.at[o], dst_ref=met.at[o, k],
            send_sem=msend.at[o * groups + k], recv_sem=mrecv.at[o * groups + k],
            device_id={"dp": peer, "expert": other} if o else {"dp": peer}, device_id_type=MESH,
        )

    def start_m(k, carry):
        m_copy(0, k).start()
        m_copy(1, k).start()
        return carry

    def wait_m(k, carry):
        out = []
        for o in range(2):
            m_copy(o, k).wait()
            out.append(carry[o] + met[o, k, :, 2 * tokens : 2 * tokens + wide].astype(F32))
        return tuple(out)

    m_copy(1, 0).start()
    lax.fori_loop(1, groups, start_m, 0)
    met[0, 0] = msgs[0]
    lax.fori_loop(1, zs, done_z, 0)
    for step in (1, -1):
        for s in range(reach[step]):
            line(step, s).wait_send()
            a_line(step, s).wait_send()
            for sub in range(2):
                ring_copy(step, s, sub).wait_send()
    for k in range(1, qz):
        quad_copy(k).wait_send()

    def done_spread(k, carry):
        spread_copy(k).wait_send()
        return carry

    lax.fori_loop(1, groups, done_spread, 0)
    for copy in started:
        copy.wait_send()
    x_over.wait()
    h_over.wait()
    m_copy(1, 0).wait()
    grams = lax.fori_loop(
        1, groups, wait_m, tuple(met[o, 0, :, 2 * tokens : 2 * tokens + wide].astype(F32) for o in range(2))
    )
    for o in range(2):
        for k in range(groups):
            block = met[o, lax.rem(dp - k + groups, groups), :, 0 : 2 * tokens].astype(F32)
            cot[o, :, k * tokens : (k + 1) * tokens] = block[:, 0:tokens]
            chat[o, :, k * tokens : (k + 1) * tokens] = block[:, tokens : 2 * tokens]

    def plain(left, right):
        return jnp.dot(left, right, preferred_element_type=F32)

    down = SCALE * (
        plain(cot[0].astype(BF16), hid[...])[:, 0:units] + plain(cot[1].astype(BF16), hgot[...])[:, 0:units]
    )
    along = plain(
        chat[0].astype(BF16), xall[:, :, :, strip].reshape(groups * tokens, 2 * width)
    ) + plain(chat[1].astype(BF16), xgot[...].reshape(groups * tokens, 2 * width))
    along = jnp.where(lax.rem(dp, 2) == 0, along[:, 0:width], along[:, width : 2 * width])
    through = jnp.zeros((8, aw), F32)
    for gram, slices in zip(grams, (aall, flipped)):
        for piece in split(gram):
            through = through + plain(piece, slices[...].reshape(wide, aw))
    up = (SCALE * factor) * (SCALE * through[:, 0:width] - CONTROL * along)
    out_ref[...] = jnp.zeros_like(out_ref)
    out_ref[:, 0:units] = down
    out_ref[:, 128 : 128 + width] = up


def part_kernel(both_ref, down_ref, up_ref):
    down_ref[...] = both_ref[:, 0 : down_ref.shape[1]]
    up_ref[...] = both_ref[:, 128 : 128 + up_ref.shape[1]]


def whole(space=pltpu.VMEM):
    return pl.BlockSpec(memory_space=space)


def body(tokens, chosen, router, partner, gate_up, a_down, a_up):
    count, d_model = tokens.shape
    groups = lax.axis_size("dp")
    experts = lax.axis_size("expert")
    zs = experts // 2
    units = gate_up.shape[2]
    width = a_up.shape[2]
    rank = a_up.shape[1]
    gtok = zs * count
    wide = zs * 16
    qz = zs // SIDE
    share = SHARE if d_model == 5120 else d_model // 2
    aw = -(-width // 128) * 128
    mw = 2 * gtok + max(128, wide)
    total = count * groups * experts
    dma = pltpu.SemaphoreType.DMA
    out = pl.pallas_call(
        functools.partial(step_kernel, zs, total, share),
        out_shape=jax.ShapeDtypeStruct((rank, 128 + aw), F32),
        in_specs=[whole()] * 3 + [whole(pltpu.SMEM), whole(pl.ANY)] + [whole()] * 2,
        out_specs=whole(),
        scratch_shapes=[
            pltpu.VMEM((zs, count, d_model - share + 128), BF16),
            pltpu.VMEM((qz, count, d_model), BF16),
            pltpu.VMEM((gtok, d_model), F32),
            pltpu.VMEM((gtok, 128), F32),
            pltpu.VMEM((gtok, d_model), BF16),
            pltpu.VMEM((gtok, 128), BF16),
            pltpu.VMEM((rank, aw + 128), BF16),
            pltpu.VMEM((rank, aw + 128), BF16),
            pltpu.VMEM((16, aw), BF16),
            pltpu.VMEM((16, 2 * width), BF16),
            pltpu.VMEM((zs, 16, aw), BF16),
            pltpu.VMEM((16, 2 * units), BF16),
            pltpu.VMEM((16, wide), BF16),
            pltpu.VMEM((groups, 16, wide), BF16),
            pltpu.VMEM((SIDE, SIDE, gtok, d_model), BF16),
            pltpu.VMEM((2, 2 * units, d_model), BF16),
            pltpu.VMEM((SIDE, SIDE, gtok, 2 * units), F32),
            pltpu.VMEM((SIDE, SIDE, gtok, 2 * units), F32),
            pltpu.VMEM((groups * gtok, 2 * units), BF16),
            pltpu.VMEM((groups, 16, 128), F32),
            pltpu.VMEM((groups, 16, 128), F32),
            pltpu.VMEM((8, 2 * gtok), BF16),
            pltpu.VMEM((zs, 8, 2 * gtok), BF16),
            pltpu.VMEM((zs, 16, 128), F32),
            pltpu.VMEM((wide, 128), F32),
            pltpu.VMEM((2, 8, mw), BF16),
            pltpu.VMEM((2, groups, 8, mw), BF16),
            pltpu.VMEM((2, 8, groups * gtok), F32),
            pltpu.VMEM((2, 8, groups * gtok), F32),
            pltpu.VMEM((groups * gtok, 128), BF16),
            pltpu.VMEM((groups * gtok, 128), BF16),
            pltpu.VMEM((SIDE, SIDE, gtok, 2 * width), BF16),
            pltpu.VMEM((zs, 16, aw), BF16),
            dma((120,)), dma((120,)), dma((6,)), dma((2,)), dma((2,)), dma, dma,
            dma((zs,)), dma((zs,)), dma((zs,)), dma((zs,)), dma((qz,)), dma((qz,)),
            dma((groups,)), dma((groups,)), dma((2 * zs,)), dma((2 * zs,)),
            dma((zs,)), dma((zs,)), dma((groups,)), dma((groups,)), dma((groups,)), dma((groups,)),
            dma((zs,)), dma((zs,)), dma((2 * groups,)), dma((2 * groups,)), dma, dma, dma, dma,
        ],
        compiler_params=pltpu.CompilerParams(
            collective_id=0, has_side_effects=True, vmem_limit_bytes=56 << 20
        ),
        name="lorra_step",
    )(tokens, chosen, router, partner, gate_up[0], a_down[0], a_up[0])
    down, up = pl.pallas_call(
        part_kernel,
        out_shape=(
            jax.ShapeDtypeStruct((rank, units), F32),
            jax.ShapeDtypeStruct((rank, width), F32),
        ),
        in_specs=[whole()],
        out_specs=(whole(), whole()),
        name="part",
    )(out)
    return (down[None], up[None])


def solution(mesh):
    placed = (
        P(("dp", "expert"), None),
        P(("dp", "expert"), None),
        P(("dp", "expert"), None),
        P(("dp", "expert")),
        P("expert", None, "dp", None),
        P("expert", None, "dp"),
        P("expert", None, "dp"),
    )
    return jax.shard_map(
        body,
        mesh=mesh,
        in_specs=placed,
        out_specs=(P("expert", None, "dp"), P("expert", None, "dp")),
        check_vma=False,
    )
```

```python
import functools
import math

import jax
import jax.numpy as jnp
from jax import lax
from jax.experimental import pallas as pl
from jax.experimental.pallas import tpu as pltpu
from jax.sharding import PartitionSpec as P

SCALE = 2.0
CONTROL = 0.5
SIDE = 4
SHARE = 1024
HIGH = lax.Precision.HIGHEST
MESH = pl.DeviceIdType.MESH
F32 = jnp.float32
BF16 = jnp.bfloat16


def dot_t(a, b, **kw):
    return lax.dot_general(a, b, (((1,), (1,)), ((), ())), preferred_element_type=F32, **kw)


def split(v):
    hi = v.astype(BF16)
    lo = (v - hi.astype(F32)).astype(BF16)
    return hi, lo


def step_kernel(
    zs, total, share, tok_ref, ids_ref, route_ref, mate_ref, w_ref, adn_ref, aup_ref, out_ref,
    zg, zq, xf, xt, xg, tab, pk, pks, apair, apad, aall, bd, gsend, grecv,
    xall, wbuf, accg, accu, hid, lowp, lowr, lown, lowz, val, ct, msgs, met, cot, chat, hsend, hgot, xgot, flipped,
    ssem, rsem, lsem, wssem, wrsem, asend, arecv, rsend, rrecv, lsend, lrecv, qsend, qrecv,
    pssend, psrecv, prsend, prrecv,
    azsend, azrecv, gssem, grsem, psend, precv, zsend, zrecv, msend, mrecv, csend, crecv, xsend, xrecv,
):
    count, d_model = tok_ref.shape
    part = d_model - share
    d_half = part // 2
    quarter = d_half // 2
    units = w_ref.shape[1]
    width = aup_ref.shape[1]
    aw = apair.shape[1]
    tokens = zs * count
    experts = 2 * zs
    wide = zs * 16
    factor = 2.0 / math.sqrt(total)
    qz = zq.shape[0]
    nq = zs // qz
    qrows = qz * count
    slice_w = share // qz
    dp = lax.axis_index("dp")
    ex = lax.axis_index("expert")
    y, x = dp // SIDE, lax.rem(dp, SIDE)
    z, c = ex // 2, lax.rem(ex, 2)
    a, b = z // qz, lax.rem(z, qz)
    up_side = (2 * b) // qz
    quads = (a, lax.rem(a + 2 * up_side + 3, nq), lax.rem(a + 5 - 2 * up_side, nq), lax.rem(a + 2, nq))
    other = 2 * z + (1 - c)
    groups = SIDE * SIDE

    barrier = pltpu.get_barrier_semaphore()

    def greet_dp(k, carry):
        pl.semaphore_signal(barrier, inc=1, device_id={"dp": lax.rem(dp + k, groups)}, device_id_type=MESH)
        return carry

    def greet_z(k, carry):
        pl.semaphore_signal(
            barrier, inc=1, device_id={"expert": 2 * lax.rem(z + k, zs) + c}, device_id_type=MESH
        )
        return carry

    lax.fori_loop(1, zs, greet_z, 0)
    def greet_across(k, carry):
        pl.semaphore_signal(
            barrier, inc=1, device_id={"dp": lax.rem(dp + k, groups), "expert": other}, device_id_type=MESH
        )
        return carry

    lax.fori_loop(0, groups, greet_across, 0)
    lax.fori_loop(1, groups, greet_dp, 0)

    weights = []
    for g in range(2):
        mine = pltpu.make_async_copy(w_ref.at[g], wbuf.at[g, pl.ds(0, units)], lsem.at[g])
        mine.start()
        weights.append(mine)
    col = lax.broadcasted_iota(jnp.int32, (count, 128), 1)
    row4 = lax.broadcasted_iota(jnp.int32, (count, 128), 0)
    named = lax.rem(col, experts)
    wtab = jnp.zeros((count, 128), F32)
    for k in range(ids_ref.shape[1]):
        place_of = jnp.bitwise_xor(ids_ref[:, k : k + 1], c)
        wtab = wtab + jnp.where(named == place_of, route_ref[:, k : k + 1], 0.0)
    top = wtab.astype(BF16).astype(F32)
    mid = (wtab - top).astype(BF16).astype(F32)
    rest = wtab - top - mid
    pick = jnp.zeros((count, 128), F32)
    for k in range(count):
        pick = jnp.where((row4 == k) & (col - 3 * experts == mate_ref[k]), 1.0, pick)
    packed = jnp.where(
        col < experts, top, jnp.where(col < 2 * experts, mid, jnp.where(col < 3 * experts, rest, pick))
    )
    zq[b] = tok_ref[...]
    zg[z, :, 0:part] = tok_ref[:, 0:part]
    zg[z, :, part : part + 128] = packed.astype(BF16)
    pk[...] = jnp.zeros_like(pk)
    pk[:, 0:width] = aup_ref[...]
    pk[:, aw : aw + units] = adn_ref[...]
    accg[...] = jnp.zeros_like(accg)
    accu[...] = jnp.zeros_like(accu)

    pl.semaphore_wait(barrier, 2 * groups + zs - 2)

    def zdev(step):
        return {"expert": 2 * lax.rem(z + step + zs, zs) + c}

    def quad_copy(k):
        return pltpu.make_async_remote_copy(
            src_ref=zq.at[b], dst_ref=zq.at[b], send_sem=qsend.at[k], recv_sem=qrecv.at[k],
            device_id={"expert": 2 * (a * qz + lax.rem(b + k, qz)) + c}, device_id_type=MESH,
        )

    def quad_arrived(k):
        slot = lax.rem(b - k + qz, qz)
        pltpu.make_async_remote_copy(
            src_ref=zq.at[slot], dst_ref=zq.at[slot], send_sem=qsend.at[k], recv_sem=qrecv.at[k],
            device_id={"expert": 2 * (a * qz + slot) + c}, device_id_type=MESH,
        ).wait_recv()

    def line(step, s):
        block = lax.rem(z - step * s + zs, zs)
        return pltpu.make_async_remote_copy(
            src_ref=zg.at[block], dst_ref=zg.at[block],
            send_sem=(rsend if step > 0 else lsend).at[s], recv_sem=(rrecv if step > 0 else lrecv).at[s],
            device_id=zdev(step), device_id_type=MESH,
        )

    def landed(step, s):
        block = lax.rem(z - step * (s + 1) + zs, zs)
        pltpu.make_async_remote_copy(
            src_ref=zg.at[block], dst_ref=zg.at[block],
            send_sem=(rsend if step > 0 else lsend).at[s], recv_sem=(rrecv if step > 0 else lrecv).at[s],
            device_id=zdev(step), device_id_type=MESH,
        ).wait_recv()

    reach = {1: zs // 2, -1: zs - 1 - zs // 2}

    def hop(s):
        for step in (1, -1):
            if 1 <= s <= reach[step]:
                landed(step, s - 1)
            if s < reach[step]:
                line(step, s).start()

    hop(0)
    for k in range(1, qz):
        quad_copy(k).start()
    swap_a = pltpu.make_async_remote_copy(
        src_ref=pk, dst_ref=pks, send_sem=asend, recv_sem=arecv,
        device_id={"expert": other}, device_id_type=MESH,
    )
    swap_a.start()
    for g in range(2):
        theirs = pltpu.make_async_remote_copy(
            src_ref=w_ref.at[g], dst_ref=wbuf.at[g, pl.ds(units, units)],
            send_sem=wssem.at[g], recv_sem=wrsem.at[g],
            device_id={"expert": other}, device_id_type=MESH,
        )
        theirs.start()
        weights.append(theirs)

    def a_line(step, s):
        block = lax.rem(z - step * s + zs, zs)
        return pltpu.make_async_remote_copy(
            src_ref=aall.at[block], dst_ref=aall.at[block],
            send_sem=azsend.at[(0 if step > 0 else zs // 2) + s], recv_sem=azrecv.at[(0 if step > 0 else zs // 2) + s],
            device_id=zdev(step), device_id_type=MESH,
        )

    def a_landed(step, s):
        block = lax.rem(z - step * (s + 1) + zs, zs)
        pltpu.make_async_remote_copy(
            src_ref=aall.at[block], dst_ref=aall.at[block],
            send_sem=azsend.at[(0 if step > 0 else zs // 2) + s], recv_sem=azrecv.at[(0 if step > 0 else zs // 2) + s],
            device_id=zdev(step), device_id_type=MESH,
        ).wait_recv()

    def a_hop(s):
        for step in (1, -1):
            if 1 <= s <= reach[step]:
                a_landed(step, s - 1)
            if s < reach[step]:
                a_line(step, s).start()

    def far(h, first, step):
        along_x = (h == 0) == first
        yy = y if along_x else lax.rem(y + step + SIDE, SIDE)
        xx = lax.rem(x + step + SIDE, SIDE) if along_x else x
        return {"dp": yy * SIDE + xx}

    def place(h, da, db):
        dx, dy = (da, db) if h == 0 else (db, da)
        return lax.rem(y + dy + SIDE, SIDE), lax.rem(x + dx + SIDE, SIDE)

    def cols(h, piece):
        lo = h * d_half
        if piece is None:
            return pl.ds(lo, d_half)
        return pl.ds(lo + piece * quarter, quarter)

    started = []
    span = (pl.ds(0, qrows), pl.ds(qrows, qrows), pl.ds(2 * qrows, 2 * qrows))
    offsets = (0, -1, 1, 2)

    def number(stage, h, phase, j, kind):
        return stage * 40 + h * 20 + (kind if phase == 0 else 4 + 4 * j + kind)

    def send(stage, h, da, db, piece, first, step, at):
        by, bx = place(h, da, db)
        block = xall.at[by, bx, span[stage], cols(h, piece)]
        source = xg.at[span[stage], cols(h, piece)] if da == 0 and db == 0 else block
        copy = pltpu.make_async_remote_copy(
            src_ref=source, dst_ref=block, send_sem=ssem.at[at], recv_sem=rsem.at[at],
            device_id=far(h, first, step), device_id_type=MESH,
        )
        copy.start()
        started.append(copy)

    def arrived(stage, h, da, db, piece, at):
        by, bx = place(h, da, db)
        block = xall.at[by, bx, span[stage], cols(h, piece)]
        pltpu.make_async_remote_copy(
            src_ref=block, dst_ref=block, send_sem=ssem.at[at], recv_sem=rsem.at[at],
            device_id=far(h, True, 1), device_id_type=MESH,
        ).wait_recv()

    def xy_own(stage):
        for phase in (0, 1):
            for h in range(2):
                for kind, step in ((0, 1), (1, -1)):
                    send(stage, h, 0, 0, None, phase == 0, step, number(stage, h, phase, 0, kind))
        copy = pltpu.make_async_copy(
            xg.at[span[stage], pl.ds(0, part)], xall.at[y, x, span[stage], pl.ds(0, part)], lsem.at[2 + stage]
        )
        copy.start()
        return copy

    def xy_near(stage):
        for h in range(2):
            arrived(stage, h, -1, 0, None, number(stage, h, 0, 0, 0))
            send(stage, h, -1, 0, 0, True, 1, number(stage, h, 0, 0, 2))
            arrived(stage, h, 1, 0, None, number(stage, h, 0, 0, 1))
            send(stage, h, 1, 0, 1, True, -1, number(stage, h, 0, 0, 3))
            for j in (1, 2):
                send(stage, h, offsets[j], 0, None, False, 1, number(stage, h, 1, j, 0))
                send(stage, h, offsets[j], 0, None, False, -1, number(stage, h, 1, j, 1))

    def xy_far(stage):
        for h in range(2):
            arrived(stage, h, 2, 0, 0, number(stage, h, 0, 0, 2))
            arrived(stage, h, 2, 0, 1, number(stage, h, 0, 0, 3))
            send(stage, h, 2, 0, None, False, 1, number(stage, h, 1, 3, 0))
            send(stage, h, 2, 0, None, False, -1, number(stage, h, 1, 3, 1))

    def xy_pass(stage, j):
        for h in range(2):
            arrived(stage, h, offsets[j], -1, None, number(stage, h, 1, j, 0))
            send(stage, h, offsets[j], -1, 0, False, 1, number(stage, h, 1, j, 2))
            arrived(stage, h, offsets[j], 1, None, number(stage, h, 1, j, 1))
            send(stage, h, offsets[j], 1, 1, False, -1, number(stage, h, 1, j, 3))

    def xy_last(stage, h):
        for j in range(4):
            arrived(stage, h, offsets[j], 2, 0, number(stage, h, 1, j, 2))
            arrived(stage, h, offsets[j], 2, 1, number(stage, h, 1, j, 3))

    strip_cols = pl.ds(pl.multiple_of(part + b * slice_w, 128), slice_w)

    def spread_copy(k):
        return pltpu.make_async_remote_copy(
            src_ref=xg.at[pl.ds(0, qrows), strip_cols],
            dst_ref=xall.at[y, x, pl.ds(0, qrows), strip_cols],
            send_sem=pssend.at[k], recv_sem=psrecv.at[k],
            device_id={"dp": lax.rem(dp + k, groups)}, device_id_type=MESH,
        )

    def spread_arrived(k):
        source = lax.rem(dp - k + groups, groups)
        block = xall.at[source // SIDE, lax.rem(source, SIDE), pl.ds(0, qrows), strip_cols]
        pltpu.make_async_remote_copy(
            src_ref=block, dst_ref=block, send_sem=pssend.at[k], recv_sem=psrecv.at[k],
            device_id={"dp": source}, device_id_type=MESH,
        ).wait_recv()

    def piece_at(source, holder, sub):
        gap = lax.rem(source // qz - holder // qz + nq, nq)
        side = (2 * lax.rem(holder, qz)) // qz
        odd_gap = lax.rem(gap, 2)
        theirs = (1 - odd_gap) * (gap // 2) * 3 + odd_gap * (2 - side + (gap // 2) * (2 * side - 1))
        return xall.at[
            pl.ds(2 * sub, 2), :, pl.ds(pl.multiple_of(qrows * theirs, qrows), qrows),
            pl.ds(pl.multiple_of(part + lax.rem(source, qz) * slice_w, 128), slice_w),
        ]

    def ring_slot(step, s, sub):
        return (0 if step > 0 else 2 * (zs // 2)) + 2 * s + sub

    def ring_copy(step, s, sub):
        source = lax.rem(z - step * s + zs, zs)
        peer = lax.rem(z + step + zs, zs)
        at = ring_slot(step, s, sub)
        return pltpu.make_async_remote_copy(
            src_ref=piece_at(source, z, sub), dst_ref=piece_at(source, peer, sub),
            send_sem=prsend.at[at], recv_sem=prrecv.at[at], device_id=zdev(step), device_id_type=MESH,
        )

    def ring_landed(step, s, sub):
        source = lax.rem(z - step * (s + 1) + zs, zs)
        at = ring_slot(step, s, sub)
        block = piece_at(source, z, sub)
        pltpu.make_async_remote_copy(
            src_ref=block, dst_ref=block,
            send_sem=prsend.at[at], recv_sem=prrecv.at[at], device_id=zdev(step), device_id_type=MESH,
        ).wait_recv()

    def ring(s):
        for sub in range(2):
            for step in (1, -1):
                if 1 <= s <= reach[step]:
                    ring_landed(step, s - 1, sub)
                if s < reach[step]:
                    ring_copy(step, s, sub).start()

    hop(1)
    for k in range(1, qz):
        quad_arrived(k)
    for k in range(qz):
        xf[count * k : count * (k + 1), :] = zq[k].astype(F32)
    xg[0:qrows, :] = xf[0:qrows, :].astype(BF16)

    def start_spread(k, carry):
        spread_copy(k).start()
        return carry

    def wait_spread(k, carry):
        spread_arrived(k)
        return carry

    lax.fori_loop(1, groups, start_spread, 0)
    mine_q = pltpu.make_async_copy(
        xg.at[pl.ds(0, qrows), strip_cols], xall.at[y, x, pl.ds(0, qrows), strip_cols], lsem.at[5]
    )
    mine_q.start()
    own0 = xy_own(0)
    hop(2)

    swap_a.wait()
    lead, follow = pk[...].astype(F32), pks[...].astype(F32)
    stacked = jnp.concatenate([lead, follow], axis=0)
    apair[...] = stacked[:, 0:aw].astype(BF16)
    aall[z] = stacked[:, 0:aw].astype(BF16)
    spread = jnp.concatenate([stacked[:, 0:width], jnp.zeros((16, width), F32)], axis=1)
    odd = jnp.concatenate([jnp.zeros((16, width), F32), stacked[:, 0:width]], axis=1)
    apad[...] = jnp.where(lax.rem(dp, 2) == 0, spread, odd).astype(BF16)
    blank = jnp.zeros((8, units), F32)
    bd[...] = jnp.concatenate(
        [
            jnp.concatenate([lead[:, aw : aw + units], blank], axis=1),
            jnp.concatenate([blank, follow[:, aw : aw + units]], axis=1),
        ],
        axis=0,
    ).astype(BF16)

    def g_copy(k):
        return pltpu.make_async_remote_copy(
            src_ref=gsend, dst_ref=grecv.at[k], send_sem=gssem.at[k], recv_sem=grsem.at[k],
            device_id={"dp": lax.rem(dp + k, groups)}, device_id_type=MESH,
        )

    def start_g(k, carry):
        g_copy(k).start()
        return carry

    def wait_g(k, carry):
        g_copy(k).wait()
        return carry + grecv[k].astype(F32)

    def bring(r):
        for k in range(qz):
            at = (r * qz + k) * count
            xf[at : at + count, 0:part] = zg[quads[r] * qz + k, :, 0:part].astype(F32)
        rows_r = slice(r * qrows, (r + 1) * qrows)
        xg[rows_r, 0:part] = xf[rows_r, 0:part].astype(BF16)

    def panel(block, at):
        return [dot_t(block, wbuf[g, :, at]) for g in range(2)]

    chunk = d_half
    rows = SIDE * tokens

    def multiply(h, db):
        by, bx = place(h, 0, db)

        def step(i, carry):
            at = pl.ds(pl.multiple_of(h * d_half + i * chunk, 128), chunk)
            if h == 0:
                block = xall[by, :, :, at]
            else:
                block = xall[:, bx, :, at]
            for acc, value in zip((accg, accu), panel(block.reshape(rows, chunk), at)):
                value = value.reshape(SIDE, tokens, 2 * units)
                if h == 0:
                    acc[by] = acc[by] + value
                else:
                    acc[:, bx] = acc[:, bx] + value
            return carry

        lax.fori_loop(0, d_half // chunk, step, 0)

    def multiply_q():
        at = pl.ds(part, share)

        def step(i, carry):
            block = xall[i, :, :, at].reshape(rows, share)
            for acc, value in zip((accg, accu), panel(block, at)):
                acc[i] = acc[i] + value.reshape(SIDE, tokens, 2 * units)
            return carry

        lax.fori_loop(0, SIDE, step, 0)

    a_hop(0)
    hop(3)
    mine_q.wait()
    lax.fori_loop(1, groups, wait_spread, 0)
    ring(0)
    xy_near(0)
    a_hop(1)
    hop(4)
    xy_far(0)
    a_hop(2)
    hop(5)
    bring(1)
    own1 = xy_own(1)
    ring(1)
    xy_pass(0, 0)
    a_hop(3)
    hop(6)
    xy_pass(0, 1)
    ring(2)
    xy_near(1)
    a_hop(4)
    hop(7)
    xy_pass(0, 2)
    ring(3)
    a_hop(5)
    hop(8)
    bring(2)
    bring(3)
    own2 = xy_own(2)
    xy_far(1)
    for r in range(nq):
        for k in range(qz):
            at = (r * qz + k) * count
            xt[at : at + count, :] = zg[quads[r] * qz + k, :, part : part + 128].astype(F32)
    tab[...] = xt[...].astype(BF16)
    xy_pass(0, 3)
    xy_pass(1, 0)
    ring(4)
    a_hop(6)
    xy_near(2)
    xy_pass(1, 1)
    a_hop(7)
    for h in range(2):
        xy_last(0, h)
    xy_far(2)
    a_hop(8)
    ring(5)
    own0.wait()
    own1.wait()
    own2.wait()
    for copy in weights:
        copy.wait()
    xy_pass(1, 2)
    xy_pass(1, 3)
    xy_pass(2, 0)
    ring(6)
    gsend[...] = dot_t(apair[...], aall[...].reshape(wide, aw)).astype(BF16)
    lax.fori_loop(1, groups, start_g, 0)
    xy_pass(2, 1)
    ring(7)
    xy_pass(2, 2)
    multiply(0, 0)
    multiply(1, 0)
    for h in range(2):
        xy_last(1, h)
    xy_pass(2, 3)
    multiply(0, -1)
    multiply(0, 1)
    multiply(1, -1)
    multiply(1, 1)
    ring(8)
    multiply_q()
    gmat = lax.fori_loop(1, groups, wait_g, gsend[...].astype(F32))
    xy_last(2, 0)
    multiply(0, 2)
    xy_last(2, 1)
    multiply(1, 2)
    strip = pl.ds(pl.multiple_of(2 * width * (dp // 2), 128), 2 * width)
    x_over = pltpu.make_async_remote_copy(
        src_ref=xall.at[:, :, :, strip], dst_ref=xgot, send_sem=xsend, recv_sem=xrecv,
        device_id={"expert": other}, device_id_type=MESH,
    )
    x_over.start()
    both = accg.shape[3]
    gate = accg[...].reshape(groups * tokens, both)
    hid[...] = (gate * (1.0 / (1.0 + jnp.exp(-gate))) * accu[...].reshape(groups * tokens, both)).astype(BF16)
    low = dot_t(bd[...], hid[...])
    tall = dot_t(apad[...], xall[:, :, :, strip].reshape(groups * tokens, 2 * width))
    for k in range(groups):
        lowp[k, :, 0:tokens] = low[:, k * tokens : (k + 1) * tokens]
        lowp[k, :, 64 : 64 + tokens] = tall[:, k * tokens : (k + 1) * tokens]

    def low_copy(k):
        peer = lax.rem(dp + k, groups)
        return pltpu.make_async_remote_copy(
            src_ref=lowp.at[peer], dst_ref=lowr.at[k], send_sem=psend.at[k], recv_sem=precv.at[k],
            device_id={"dp": peer}, device_id_type=MESH,
        )

    def start_low(k, carry):
        low_copy(k).start()
        return carry

    def wait_low(k, carry):
        low_copy(k).wait()
        return carry + lowr[k]

    lax.fori_loop(1, groups, start_low, 0)
    hsend[:, 0:units] = hid[:, units : 2 * units]
    h_over = pltpu.make_async_remote_copy(
        src_ref=hsend, dst_ref=hgot, send_sem=csend, recv_sem=crecv,
        device_id={"expert": other}, device_id_type=MESH,
    )
    h_over.start()
    slabs = aall[...].astype(F32)
    flipped[...] = jnp.concatenate([slabs[:, 8:16], slabs[:, 0:8]], axis=1).astype(BF16)
    row = lax.broadcasted_iota(jnp.int32, (wide, 128), 0)
    lane = lax.broadcasted_iota(jnp.int32, (wide, 128), 1)
    chooser = jnp.where((row // 8 == lax.rem(lane, experts)) & (lane < 3 * experts), 1.0, 0.0).astype(BF16)
    w8 = dot_t(chooser, tab[...])
    trow = lax.broadcasted_iota(jnp.int32, (tokens, 128), 0)
    tlane = lax.broadcasted_iota(jnp.int32, (tokens, 128), 1)
    finder = jnp.where(tlane - 3 * experts == lax.rem(trow, count), 1.0, 0.0).astype(BF16)
    t0 = lax.broadcasted_iota(jnp.int32, (tokens, tokens), 0)
    t1 = lax.broadcasted_iota(jnp.int32, (tokens, tokens), 1)
    mate = jnp.where(t0 // count == t1 // count, dot_t(finder, tab[...]), 0.0)
    q = jnp.where(t0 == t1, 1.0, 0.0) - mate
    summed = lax.fori_loop(1, groups, wait_low, lowp[dp])

    def shuffle(v, high, low_side):
        pieces = [v[:, qrows * i : qrows * (i + 1)] for i in range(nq)]
        return jnp.where(
            up_side == 1,
            jnp.concatenate([pieces[i] for i in high], axis=1),
            jnp.concatenate([pieces[i] for i in low_side], axis=1),
        )

    steady = shuffle(summed[:, 0:tokens], (0, 1, 3, 2), (0, 2, 3, 1))
    lown[...] = jnp.concatenate([steady[0:8], steady[8:16]], axis=1).astype(BF16)

    def z_copy(k):
        return pltpu.make_async_remote_copy(
            src_ref=lown, dst_ref=lowz.at[z], send_sem=zsend.at[k], recv_sem=zrecv.at[k],
            device_id=zdev(k), device_id_type=MESH,
        )

    def z_arrival(k):
        source = lax.rem(z - k + zs, zs)
        return pltpu.make_async_remote_copy(
            src_ref=lown, dst_ref=lowz.at[source], send_sem=zsend.at[k], recv_sem=zrecv.at[k],
            device_id={"expert": 2 * source + c}, device_id_type=MESH,
        )

    def start_z(k, carry):
        z_copy(k).start()
        return carry

    def wait_z(k, carry):
        z_arrival(k).wait_recv()
        return carry

    def done_z(k, carry):
        z_copy(k).wait_send()
        return carry

    lax.fori_loop(1, zs, start_z, 0)
    lowz[z] = lown[...]
    zt = jnp.dot(summed[:, 64 : 64 + tokens], q, precision=HIGH, preferred_element_type=F32)
    lax.fori_loop(1, zs, wait_z, 0)

    for rho in range(nq):
        there = pl.ds(qz * lax.rem(a + rho, nq), qz)
        found = lowz[there].astype(F32)
        turn = qrows * rho
        for o in range(2):
            lanes = found[:, :, tokens * o : tokens * (o + 1)]
            if turn:
                lanes = jnp.concatenate([lanes[:, :, tokens - turn :], lanes[:, :, : tokens - turn]], axis=2)
            val[there, 8 * o : 8 * o + 8, 0:tokens] = lanes
    values = shuffle(val[...].reshape(wide, 128)[:, 0:tokens], (0, 1, 3, 2), (0, 3, 1, 2)) * w8
    ct[:, 0:tokens] = values
    ct[:, 64 : 64 + tokens] = w8
    here = pl.ds(pl.multiple_of(16 * z, 16), 16)
    mine = ct[here, 0:tokens]
    weight = ct[here, 64 : 64 + tokens]
    inner = jnp.dot(gmat, values, precision=HIGH, preferred_element_type=F32)
    first = weight * (factor * (SCALE * inner - CONTROL * zt))
    second = jnp.dot(mine, q, precision=HIGH, preferred_element_type=F32)
    third = dot_t(mine, values, precision=HIGH)
    for o in range(2):
        part_of = slice(8 * o, 8 * o + 8)
        msgs[o, :, 0 : 2 * tokens] = jnp.concatenate([first[part_of], second[part_of]], axis=1).astype(BF16)
        msgs[o, :, 2 * tokens : 2 * tokens + wide] = third[part_of].astype(BF16)

    def m_copy(o, k):
        peer = lax.rem(dp + k, groups)
        return pltpu.make_async_remote_copy(
            src_ref=msgs.at[o], dst_ref=met.at[o, k],
            send_sem=msend.at[o * groups + k], recv_sem=mrecv.at[o * groups + k],
            device_id={"dp": peer, "expert": other} if o else {"dp": peer}, device_id_type=MESH,
        )

    def start_m(k, carry):
        m_copy(0, k).start()
        m_copy(1, k).start()
        return carry

    def wait_m(k, carry):
        out = []
        for o in range(2):
            m_copy(o, k).wait()
            out.append(carry[o] + met[o, k, :, 2 * tokens : 2 * tokens + wide].astype(F32))
        return tuple(out)

    m_copy(1, 0).start()
    lax.fori_loop(1, groups, start_m, 0)
    met[0, 0] = msgs[0]
    lax.fori_loop(1, zs, done_z, 0)
    for step in (1, -1):
        for s in range(reach[step]):
            line(step, s).wait_send()
            a_line(step, s).wait_send()
            for sub in range(2):
                ring_copy(step, s, sub).wait_send()
    for k in range(1, qz):
        quad_copy(k).wait_send()

    def done_spread(k, carry):
        spread_copy(k).wait_send()
        return carry

    lax.fori_loop(1, groups, done_spread, 0)
    for copy in started:
        copy.wait_send()
    x_over.wait()
    h_over.wait()
    m_copy(1, 0).wait()
    grams = lax.fori_loop(
        1, groups, wait_m, tuple(met[o, 0, :, 2 * tokens : 2 * tokens + wide].astype(F32) for o in range(2))
    )
    for o in range(2):
        for k in range(groups):
            block = met[o, lax.rem(dp - k + groups, groups), :, 0 : 2 * tokens].astype(F32)
            cot[o, :, k * tokens : (k + 1) * tokens] = block[:, 0:tokens]
            chat[o, :, k * tokens : (k + 1) * tokens] = block[:, tokens : 2 * tokens]

    def plain(left, right):
        return jnp.dot(left, right, preferred_element_type=F32)

    down = SCALE * (
        plain(cot[0].astype(BF16), hid[...])[:, 0:units] + plain(cot[1].astype(BF16), hgot[...])[:, 0:units]
    )
    along = plain(
        chat[0].astype(BF16), xall[:, :, :, strip].reshape(groups * tokens, 2 * width)
    ) + plain(chat[1].astype(BF16), xgot[...].reshape(groups * tokens, 2 * width))
    along = jnp.where(lax.rem(dp, 2) == 0, along[:, 0:width], along[:, width : 2 * width])
    through = jnp.zeros((8, aw), F32)
    for gram, slices in zip(grams, (aall, flipped)):
        for piece in split(gram):
            through = through + plain(piece, slices[...].reshape(wide, aw))
    up = (SCALE * factor) * (SCALE * through[:, 0:width] - CONTROL * along)
    out_ref[...] = jnp.zeros_like(out_ref)
    out_ref[:, 0:units] = down
    out_ref[:, 128 : 128 + width] = up


def part_kernel(both_ref, down_ref, up_ref):
    down_ref[...] = both_ref[:, 0 : down_ref.shape[1]]
    up_ref[...] = both_ref[:, 128 : 128 + up_ref.shape[1]]


def whole(space=pltpu.VMEM):
    return pl.BlockSpec(memory_space=space)


def body(tokens, chosen, router, partner, gate_up, a_down, a_up):
    count, d_model = tokens.shape
    groups = lax.axis_size("dp")
    experts = lax.axis_size("expert")
    zs = experts // 2
    units = gate_up.shape[2]
    width = a_up.shape[2]
    rank = a_up.shape[1]
    gtok = zs * count
    wide = zs * 16
    qz = zs // SIDE
    share = SHARE if d_model == 5120 else d_model // 2
    aw = -(-width // 128) * 128
    mw = 2 * gtok + max(128, wide)
    total = count * groups * experts
    dma = pltpu.SemaphoreType.DMA
    out = pl.pallas_call(
        functools.partial(step_kernel, zs, total, share),
        out_shape=jax.ShapeDtypeStruct((rank, 128 + aw), F32),
        in_specs=[whole()] * 3 + [whole(pltpu.SMEM), whole(pl.ANY)] + [whole()] * 2,
        out_specs=whole(),
        scratch_shapes=[
            pltpu.VMEM((zs, count, d_model - share + 128), BF16),
            pltpu.VMEM((qz, count, d_model), BF16),
            pltpu.VMEM((gtok, d_model), F32),
            pltpu.VMEM((gtok, 128), F32),
            pltpu.VMEM((gtok, d_model), BF16),
            pltpu.VMEM((gtok, 128), BF16),
            pltpu.VMEM((rank, aw + 128), BF16),
            pltpu.VMEM((rank, aw + 128), BF16),
            pltpu.VMEM((16, aw), BF16),
            pltpu.VMEM((16, 2 * width), BF16),
            pltpu.VMEM((zs, 16, aw), BF16),
            pltpu.VMEM((16, 2 * units), BF16),
            pltpu.VMEM((16, wide), BF16),
            pltpu.VMEM((groups, 16, wide), BF16),
            pltpu.VMEM((SIDE, SIDE, gtok, d_model), BF16),
            pltpu.VMEM((2, 2 * units, d_model), BF16),
            pltpu.VMEM((SIDE, SIDE, gtok, 2 * units), F32),
            pltpu.VMEM((SIDE, SIDE, gtok, 2 * units), F32),
            pltpu.VMEM((groups * gtok, 2 * units), BF16),
            pltpu.VMEM((groups, 16, 128), F32),
            pltpu.VMEM((groups, 16, 128), F32),
            pltpu.VMEM((8, 2 * gtok), BF16),
            pltpu.VMEM((zs, 8, 2 * gtok), BF16),
            pltpu.VMEM((zs, 16, 128), F32),
            pltpu.VMEM((wide, 128), F32),
            pltpu.VMEM((2, 8, mw), BF16),
            pltpu.VMEM((2, groups, 8, mw), BF16),
            pltpu.VMEM((2, 8, groups * gtok), F32),
            pltpu.VMEM((2, 8, groups * gtok), F32),
            pltpu.VMEM((groups * gtok, 128), BF16),
            pltpu.VMEM((groups * gtok, 128), BF16),
            pltpu.VMEM((SIDE, SIDE, gtok, 2 * width), BF16),
            pltpu.VMEM((zs, 16, aw), BF16),
            dma((120,)), dma((120,)), dma((6,)), dma((2,)), dma((2,)), dma, dma,
            dma((zs,)), dma((zs,)), dma((zs,)), dma((zs,)), dma((qz,)), dma((qz,)),
            dma((groups,)), dma((groups,)), dma((2 * zs,)), dma((2 * zs,)),
            dma((zs,)), dma((zs,)), dma((groups,)), dma((groups,)), dma((groups,)), dma((groups,)),
            dma((zs,)), dma((zs,)), dma((2 * groups,)), dma((2 * groups,)), dma, dma, dma, dma,
        ],
        compiler_params=pltpu.CompilerParams(
            collective_id=0, has_side_effects=True, vmem_limit_bytes=56 << 20
        ),
        name="lorra_step",
    )(tokens, chosen, router, partner, gate_up[0], a_down[0], a_up[0])
    down, up = pl.pallas_call(
        part_kernel,
        out_shape=(
            jax.ShapeDtypeStruct((rank, units), F32),
            jax.ShapeDtypeStruct((rank, width), F32),
        ),
        in_specs=[whole()],
        out_specs=(whole(), whole()),
        name="part",
    )(out)
    return (down[None], up[None])


def solution(mesh):
    placed = (
        P(("dp", "expert"), None),
        P(("dp", "expert"), None),
        P(("dp", "expert"), None),
        P(("dp", "expert")),
        P("expert", None, "dp", None),
        P("expert", None, "dp"),
        P("expert", None, "dp"),
    )
    return jax.shard_map(
        body,
        mesh=mesh,
        in_specs=placed,
        out_specs=(P("expert", None, "dp"), P("expert", None, "dp")),
        check_vma=False,
    )
```
